32 devices in a mesh: wide: 8 (over z, y), narrow: 4 (over x, core).
Axes of the slice: x: 2, y: 2, z: 4, core: 2. Of those that a mesh axis runs over, the one named last changes fastest.
Arguments:
- frames: float32 [32768, 440], P(('wide', 'narrow')), may hold values from -8 to 8
- targets: float32 [32768, 2048], P(('wide', 'narrow')), may hold values from -7 to 7
- projection: float32 [32, 440, 512], P(('wide', 'narrow')), may hold values from -0.25 to 0.25
- phases: float32 [32, 512], P(('wide', 'narrow')), may hold values from 0 to 6.283185
- block_order: int32 [32], replicated, may hold values from 0 to 31, each once
Outputs:
- residual: float32 [32768, 2048], P(('wide', 'narrow'))
- weights: float32 [2, 512, 2048], replicated
The draws below stay inside these ranges and needn't reach their ends.
Inputs may be any that keep to these rules, and one draw needn't show every extreme that they name: `block_order`: a permutation; steps use its first 2 entries.
All inputs are finite; a program needn't handle non-finite values.
Results may differ from the reference program's by a relative error of at most 0.0003.
Values sent between devices are 32-bit elements; how exact they have to be, the bound alone decides.
No kernel may reach another device: no remote copies, remote signals or barrier semaphores. Data moves between devices by JAX's collectives and lax.ppermute only.
A program may use at most 128 MiB of HBM per device.

```python
import jax
import jax.numpy as jnp
from jax import lax

DIM = 440
FEATS = 512
TARGETS = 2048
STEPS = 2
BLOCKS = 32
ROWS = 32768


def shared_labels(key):
    return jax.random.randint(jax.random.fold_in(key, 11), (ROWS,), 0, TARGETS)


def draw_frames(key, part):
    labels = shared_labels(key)
    centers = jax.random.normal(jax.random.fold_in(key, 12), (TARGETS, DIM), jnp.float32)
    noise = 0.5 * jax.random.normal(jax.random.fold_in(key, 13), (ROWS, DIM), jnp.float32)
    return jnp.clip(centers[labels] + noise, -8.0, 8.0)


def draw_targets(key, part):
    labels = shared_labels(key)
    onehot = (labels[:, None] == jnp.arange(TARGETS)[None, :]).astype(jnp.float32)
    noise = jnp.clip(0.5 * jax.random.normal(jax.random.fold_in(key, 14), (ROWS, TARGETS), jnp.float32), -2.5, 2.5)
    return 4.0 * (onehot - 1.0 / TARGETS) + noise


def block_scale(stream_key, dims, split, low, top_value):
    gain, own = 1.0, jax.random.fold_in(stream_key, 6)
    for dim, parts in split:
        heights = jnp.exp(jax.random.uniform(jax.random.fold_in(own, dim), (parts,), jnp.float32, low / len(split), top_value / len(split)))
        gain = gain * jnp.repeat(heights, dims[dim] // parts).reshape([-1 if axis == dim else 1 for axis in range(len(dims))])
    return gain


def normal_values(key, dims, scale, limit, pieces=(), kind=jnp.bfloat16):
    level = block_scale(key, dims, pieces, -0.22, 0.18) if pieces else 1.0
    result = jax.random.normal(key, dims, jnp.float32) * scale * level
    return jnp.minimum(jnp.maximum(result, -limit), limit).astype(kind)


def setup_inputs(seed: int = 0) -> dict:
    splits = jax.random.split(jax.random.key(seed), 6)
    return {
        "frames": draw_frames(jax.random.fold_in(splits[5], 71), 0),
        "targets": draw_targets(jax.random.fold_in(splits[5], 71), 0),
        "projection": normal_values(splits[2], (BLOCKS, DIM, FEATS), DIM ** -0.5, 0.25, ((0, 32),), jnp.float32),
        "phases": jnp.clip(6.283185 * jax.random.uniform(splits[3], (BLOCKS, FEATS), jnp.float32) ** block_scale(splits[3], (BLOCKS, FEATS), ((0, 32),), -0.2, 0.2), 0.0, 6.283185),
        "block_order": jax.random.permutation(splits[4], BLOCKS).astype(jnp.int32),
    }


def features_of(frames, block_proj, block_phase):
    inner = jnp.dot(frames.astype(jnp.float32), block_proj.astype(jnp.float32), precision=lax.Precision.HIGHEST, preferred_element_type=jnp.float32)
    return jnp.sqrt(2.0 / block_proj.shape[1]) * jnp.cos(inner + block_phase[None, :])

def solve_block(gram_sum, cross_sum):
    width = gram_sum.shape[0]
    damping = 0.1 * jnp.trace(gram_sum) / width
    factor = jnp.linalg.cholesky(gram_sum + damping * jnp.eye(width, dtype=gram_sum.dtype))
    return jax.scipy.linalg.cho_solve((factor, True), cross_sum)

def reference(frames, targets, projection, phases, block_order):
    residual = targets
    solved = []
    for step_index in range(STEPS):
        chosen = block_order[step_index]
        feats = features_of(frames, projection[chosen], phases[chosen])
        gram_sum = jnp.dot(feats.T.astype(jnp.float32), feats.astype(jnp.float32), precision=lax.Precision.HIGHEST, preferred_element_type=jnp.float32)
        cross_sum = jnp.dot(feats.T.astype(jnp.float32), residual.astype(jnp.float32), precision=lax.Precision.HIGHEST, preferred_element_type=jnp.float32)
        weights = solve_block(gram_sum, cross_sum)
        residual = residual - jnp.dot(feats.astype(jnp.float32), weights.astype(jnp.float32), precision=lax.Precision.HIGHEST, preferred_element_type=jnp.float32)
        solved.append(weights)
    return (residual, jnp.stack(solved))
```

```python
import functools
import math

import jax
import jax.numpy as jnp
from jax import lax
from jax.experimental import pallas as pl
from jax.experimental.pallas import tpu as pltpu
from jax.sharding import PartitionSpec as P

ALL = ("wide", "narrow")
F32 = jnp.float32
BF16 = jnp.bfloat16
HIGHEST = lax.Precision.HIGHEST
VMEM_LIMIT = 56 * 1024 * 1024


def params(**more):
    return pltpu.CompilerParams(vmem_limit_bytes=VMEM_LIMIT, **more)


def cost(flops, nbytes):
    return pl.CostEstimate(flops=int(flops), bytes_accessed=int(nbytes), transcendentals=0)


def split(value):
    high = value.astype(BF16)
    return high, (value - high.astype(F32)).astype(BF16)


def dot_bf16(left, right):
    return jnp.dot(left, right, preferred_element_type=F32)


def dot3(left, right):
    (lh, ll), (rh, rl) = left, right
    return dot_bf16(lh, rh) + (dot_bf16(lh, rl) + dot_bf16(ll, rh))


def dot_full(left, right):
    return jnp.dot(left, right, precision=HIGHEST, preferred_element_type=F32)


TWO_PI = 2.0 * math.pi
PART_A = 6.28125
PART_B = 2.0 ** -24 * round((TWO_PI - PART_A) * 2.0 ** 24 / 2 ** 5) * 2 ** 5
PART_C = TWO_PI - PART_A - PART_B
COS_POLY = [(-1.0) ** k / math.factorial(2 * k) for k in range(10)]


def cosine(value):
    turns = jnp.floor(value * (1.0 / TWO_PI) + 0.5)
    rest = value - turns * PART_A
    rest = rest - turns * PART_B
    rest = rest - turns * PART_C
    half = rest * 0.5
    square = half * half
    poly = SIN_POLY[-1]
    for coefficient in SIN_POLY[-2::-1]:
        poly = poly * square + coefficient
    sine = half * poly
    return 1.0 - 2.0 * sine * sine


SIN_POLY = [(-1.0) ** k / math.factorial(2 * k + 1) for k in range(7)]


def pack_kernel(s_ref, own_ref, oth_ref, pown_ref, poth_ref, out_ref):
    depth = own_ref.shape[1]
    take_own, take_oth = s_ref[1], s_ref[2]
    value = jnp.where(take_own == 1, own_ref[0], jnp.where(take_oth == 1, oth_ref[0], 0.0))
    phase = jnp.where(take_own == 1, pown_ref[0], jnp.where(take_oth == 1, poth_ref[0], 0.0))
    out_ref[0, :depth, :] = value
    tail = out_ref.shape[1] - depth
    rows = lax.broadcasted_iota(jnp.int32, (tail, out_ref.shape[2]), 0)
    out_ref[0, depth:, :] = jnp.where(rows == 0, jnp.broadcast_to(phase, rows.shape), 0.0)


def pack(scalars, own, oth, phase_own, phase_oth, padded):
    _, depth, feats = own.shape
    width = feats // 4
    block = pl.BlockSpec((1, depth, width), lambda q, s: (0, 0, q ^ s[0]))
    phase = pl.BlockSpec((1, 1, width), lambda q, s: (0, 0, q ^ s[0]))
    return pl.pallas_call(
        pack_kernel,
        out_shape=jax.ShapeDtypeStruct((4, padded, width), F32),
        grid_spec=pltpu.PrefetchScalarGridSpec(
            num_scalar_prefetch=1,
            grid=(4,),
            in_specs=[block, block, phase, phase],
            out_specs=pl.BlockSpec((1, padded, width), lambda q, s: (q, 0, 0)),
        ),
        compiler_params=params(),
        name="pack",
    )(scalars, own, oth, phase_own[:, None, :], phase_oth[:, None, :])


def features_kernel(s_ref, x_ref, p_ref, fh_ref, fl_ref, th_ref, tl_ref):
    depth = x_ref.shape[1]
    order = s_ref[0]
    blocks = [p_ref[i ^ order] for i in range(4)]
    whole = jnp.concatenate(blocks, axis=1)
    inner = dot_full(x_ref[...], whole[:depth]) + whole[depth : depth + 1]
    feats = math.sqrt(2.0 / whole.shape[1]) * cosine(inner)
    high, low = split(feats)
    fh_ref[...], fl_ref[...] = high, low
    high, low = split(feats.T)
    th_ref[...], tl_ref[...] = high, low


def features(order, frames, blocks):
    rows, depth = frames.shape
    feats = blocks.shape[0] * blocks.shape[2]
    tile = 512
    flat = pl.BlockSpec((tile, feats), lambda i, s: (i, 0))
    turned = pl.BlockSpec((feats, tile), lambda i, s: (0, i))
    return pl.pallas_call(
        features_kernel,
        out_shape=[jax.ShapeDtypeStruct((rows, feats), BF16)] * 2 + [jax.ShapeDtypeStruct((feats, rows), BF16)] * 2,
        grid_spec=pltpu.PrefetchScalarGridSpec(
            num_scalar_prefetch=1,
            grid=(rows // tile,),
            in_specs=[
                pl.BlockSpec((tile, depth), lambda i, s: (i, 0)),
                pl.BlockSpec(blocks.shape, lambda i, s: (0, 0, 0)),
            ],
            out_specs=[flat, flat, turned, turned],
        ),
        compiler_params=params(),
        cost_estimate=cost(12 * rows * depth * feats, 4 * rows * depth + 8 * rows * feats),
        name="features",
    )(order, frames, blocks)


def gram_kernel(s_ref, mh, ml, mth, mtl, oh, ol, oth, otl, out_ref):
    order, half_row, m_is_second = s_ref[0], s_ref[1], s_ref[2]
    feats, rows = mth.shape
    half = feats // 2
    pieces, _, height, _ = out_ref.shape

    def put(tile, value):
        for g in range(pieces):
            out_ref[g ^ order, tile] = value[g * height : (g + 1) * height]

    top = (mth[:half], mtl[:half])
    low = (mth[half:], mtl[half:])
    left = (mh[:, :half], ml[:, :half])
    right = (mh[:, half:], ml[:, half:])
    put(0, dot3(top, left))
    put(1, dot3(low, left))
    put(2, dot3(low, right))

    def cross(th, tl, h, l):
        start = pl.multiple_of(half_row * half, half)
        side = (th[pl.ds(start, half)], tl[pl.ds(start, half)])
        put(3, dot3(side, (h[:, :half], l[:, :half])))
        put(4, dot3(side, (h[:, half:], l[:, half:])))

    @pl.when(m_is_second == 1)
    def _():
        cross(mth, mtl, oh, ol)

    @pl.when(m_is_second == 0)
    def _():
        cross(oth, otl, mh, ml)


def gram(scalars, mine, other):
    rows, feats = mine[0].shape
    return pl.pallas_call(
        gram_kernel,
        out_shape=jax.ShapeDtypeStruct((16, 5, feats // 32, feats // 2), F32),
        in_specs=[pl.BlockSpec(memory_space=pltpu.SMEM)] + [pl.BlockSpec(memory_space=pltpu.VMEM)] * 8,
        out_specs=pl.BlockSpec(memory_space=pltpu.VMEM),
        compiler_params=params(),
        cost_estimate=cost(6 * rows * feats * feats * 1.25, 16 * rows * feats),
        name="gram",
    )(scalars, *mine, *other)


def cross_kernel(s_ref, t_ref, ath, atl, bth, btl, out_ref):
    place, swap = s_ref[1], s_ref[0] & 1
    feats = ath.shape[0]
    width = out_ref.shape[2]
    right = split(t_ref[...])
    first = pl.multiple_of(place * feats, feats)
    second = pl.multiple_of((1 - place) * feats, feats)
    for left, start in (((ath[...], atl[...]), first), ((bth[...], btl[...]), second)):
        value = dot3(left, right)
        for k in range(2):
            out_ref[k ^ swap, pl.ds(start, feats), :] = value[:, k * width : (k + 1) * width]


def cross(scalars, targets, mine, other):
    rows, columns = targets.shape
    feats = mine[2].shape[0]
    width = columns // 16
    whole = pl.BlockSpec((feats, rows), lambda k, s: (0, 0))
    return pl.pallas_call(
        cross_kernel,
        out_shape=jax.ShapeDtypeStruct((8, 2 * feats, width), F32),
        grid_spec=pltpu.PrefetchScalarGridSpec(
            num_scalar_prefetch=1,
            grid=(4,),
            in_specs=[pl.BlockSpec((rows, 2 * width), lambda k, s: (0, (s[0] >> 1) ^ k))] + [whole] * 4,
            out_specs=pl.BlockSpec((2, 2 * feats, width), lambda k, s: (k, 0, 0)),
        ),
        compiler_params=params(),
        cost_estimate=cost(6 * rows * feats * columns, 4 * rows * columns),
        name="cross",
    )(scalars, targets, mine[2], mine[3], other[2], other[3])


def assemble_kernel(s_ref, g_ref, a_ref, side_ref):
    order = s_ref[0]
    pieces, _, height, half = g_ref.shape
    for g in range(pieces):
        piece = g_ref[g ^ order]
        here = slice(g * height, (g + 1) * height)
        there = slice(half + g * height, half + (g + 1) * height)
        a_ref[here, :half] = piece[0]
        a_ref[there, :half] = piece[1]
        a_ref[there, half:] = piece[2]
        side_ref[here, :half] = piece[3]
        side_ref[here, half:] = piece[4]
    a_ref[:half, half:] = a_ref[half:, :half].T
    whole = a_ref[...]
    eye = lax.broadcasted_iota(jnp.int32, whole.shape, 0) == lax.broadcasted_iota(jnp.int32, whole.shape, 1)
    diagonal = jnp.where(eye, whole, 0.0)
    damping = 0.1 * jnp.sum(diagonal) / whole.shape[0]
    a_ref[...] = whole + jnp.where(eye, damping, 0.0)


def assemble(order, pieces):
    half = pieces.shape[3]
    return pl.pallas_call(
        assemble_kernel,
        out_shape=[jax.ShapeDtypeStruct((2 * half, 2 * half), F32), jax.ShapeDtypeStruct((half, 2 * half), F32)],
        in_specs=[pl.BlockSpec(memory_space=pltpu.SMEM), pl.BlockSpec(memory_space=pltpu.VMEM)],
        out_specs=[pl.BlockSpec(memory_space=pltpu.VMEM)] * 2,
        compiler_params=params(),
        name="assemble",
    )(order, pieces)


def square_kernel(l_ref, out_ref):
    value = l_ref[...]
    out_ref[...] = dot_full(value.T, value)


def square(inverse_factor):
    return pl.pallas_call(
        square_kernel,
        out_shape=jax.ShapeDtypeStruct(inverse_factor.shape, F32),
        compiler_params=params(),
        name="square",
    )(inverse_factor)


def couple_kernel(s_ref, own_ref, oth_ref, gown_ref, goth_ref, out_ref):
    core = s_ref[0]
    half = gown_ref.shape[0]
    second = jnp.where(core == 1, own_ref[...], oth_ref[...])
    top = jnp.where(core == 0, gown_ref[...], goth_ref[...])
    low = jnp.where(core == 0, goth_ref[...], gown_ref[...])
    out_ref[...] = dot_full(second[:, :half], top) + dot_full(second[:, half:], low)


def couple(core, own, oth, side_own, side_oth):
    return pl.pallas_call(
        couple_kernel,
        out_shape=jax.ShapeDtypeStruct(own.shape, F32),
        in_specs=[pl.BlockSpec(memory_space=pltpu.SMEM)] + [pl.BlockSpec(memory_space=pltpu.VMEM)] * 4,
        compiler_params=params(),
        name="couple",
    )(core, own, oth, side_own, side_oth)


def solve_kernel(s_ref, own_ref, oth_ref, b_ref, c_ref, out_ref):
    core, place = s_ref[0], s_ref[1]
    feats = own_ref.shape[0]
    width = c_ref.shape[2]
    first = jnp.where(core == 0, own_ref[...], oth_ref[...])
    second = jnp.where(core == 0, oth_ref[...], own_ref[...])

    def rows_of(step):
        start = pl.multiple_of((step ^ place) * feats, feats)
        return jnp.concatenate([c_ref[k, pl.ds(start, feats), :] for k in range(2)], axis=1)

    one = dot_full(first, rows_of(0))
    two = dot_full(second, rows_of(1)) - dot_full(b_ref[...], one)
    for k in range(2):
        out_ref[k, :feats, :] = one[:, k * width : (k + 1) * width]
        out_ref[k, feats:, :] = two[:, k * width : (k + 1) * width]


def solve(scalars, own, oth, coupling, crossed):
    count, height, width = crossed.shape
    feats = own.shape[0]
    whole = pl.BlockSpec((feats, feats), lambda k, s: (0, 0))
    pair = pl.BlockSpec((2, height, width), lambda k, s: (k, 0, 0))
    return pl.pallas_call(
        solve_kernel,
        out_shape=jax.ShapeDtypeStruct(crossed.shape, F32),
        grid_spec=pltpu.PrefetchScalarGridSpec(
            num_scalar_prefetch=1, grid=(count // 2,), in_specs=[whole] * 3 + [pair], out_specs=pair
        ),
        compiler_params=params(),
        cost_estimate=cost(36 * feats * feats * count * width, 8 * count * height * width),
        name="solve",
    )(scalars, own, oth, coupling, crossed)


def residual_kernel(s_ref, t_ref, ah, al, bh, bl, wa_ref, wb_ref, *rest):
    r_ref, w_ref = rest[-2:]
    k = pl.program_id(0)
    swap, core = s_ref[0] & 1, s_ref[1]
    feats = ah.shape[1]
    width = wa_ref.shape[2]

    def go(source):
        chunks = [source[i ^ swap] for i in range(2)]
        first = jnp.concatenate([v[:feats] for v in chunks], axis=1)
        second = jnp.concatenate([v[feats:] for v in chunks], axis=1)
        w_ref[0], w_ref[1] = first, second
        mine = jnp.where(core == 0, first, second)
        other = jnp.where(core == 0, second, first)
        fitted = dot3((ah[...], al[...]), split(mine)) + dot3((bh[...], bl[...]), split(other))
        r_ref[...] = t_ref[...] - fitted

    @pl.when(k < 2)
    def _():
        go(wa_ref)

    @pl.when(k >= 2)
    def _():
        go(wb_ref)


def residual_part(scalars, targets, mine, other, wa, wb, before):
    rows, columns = targets.shape
    feats = mine[0].shape[1]
    count, height, width = wa.shape
    whole = pl.BlockSpec((rows, feats), lambda k, s: (0, 0))
    block = pl.BlockSpec((rows, 2 * width), lambda k, s: (0, (s[0] >> 1) ^ k))
    anywhere = pl.BlockSpec(memory_space=pl.ANY)
    in_specs = [block] + [whole] * 4 + [
        pl.BlockSpec((2, height, width), lambda k, s: (jnp.minimum(k, 1), 0, 0)),
        pl.BlockSpec((2, height, width), lambda k, s: (jnp.maximum(k - 2, 0), 0, 0)),
    ]
    aliases = {}
    if before:
        in_specs += [anywhere] * 2
        aliases = {8: 0, 9: 1}
    return pl.pallas_call(
        residual_kernel,
        out_shape=[
            jax.ShapeDtypeStruct((rows, columns), F32),
            jax.ShapeDtypeStruct((2, feats, columns), F32),
        ],
        grid_spec=pltpu.PrefetchScalarGridSpec(
            num_scalar_prefetch=1,
            grid=(4,),
            in_specs=in_specs,
            out_specs=[block, pl.BlockSpec((2, feats, 2 * width), lambda k, s: (0, 0, (s[0] >> 1) ^ k))],
        ),
        input_output_aliases=aliases,
        compiler_params=params(),
        cost_estimate=cost(6 * rows * feats * columns, 6 * rows * columns),
        name="residual",
    )(scalars, targets, mine[0], mine[1], other[0], other[1], wa, wb, *before)


def inverse_factor_of(matrix):
    factor = jnp.linalg.cholesky(matrix)
    eye = jnp.eye(matrix.shape[0], dtype=matrix.dtype)
    return lax.linalg.triangular_solve(factor, eye, left_side=True, lower=True)


def ints(*values):
    return jnp.stack([jnp.asarray(v, jnp.int32) for v in values])


def per_device(count, frames, targets, projection, phases, block_order):
    n_bits = count.bit_length() - 1
    device = lax.axis_index(ALL)
    bit = [(device >> k) & 1 for k in range(n_bits)]
    core = bit[0]
    one = jnp.where(core == 0, bit[1], bit[2])
    two = jnp.where(core == 0, bit[2], bit[1])
    near, far = bit[3], bit[4]
    more = [1 << k for k in range(5, n_bits)]

    def exchange(value, even, odd=None):
        odd = even if odd is None else odd
        pairs = [(i, i ^ (odd if i & 1 else even)) for i in range(count)]
        return lax.ppermute(value, ALL, pairs)

    def flood(value, masks):
        for mask in masks:
            value = value + exchange(value, mask)
        return value

    wanted = block_order[core]
    projection_oth, phases_oth = exchange(projection, 1), exchange(phases, 1)
    padded = (projection.shape[1] // 8 + 1) * 8
    blocks = pack(
        ints(one * 2 + two, wanted == device, wanted == (device ^ 1)),
        projection, projection_oth, phases, phases_oth, padded,
    )
    part = blocks[:2] + exchange(blocks[2:], 2, 4)
    part = part[:1] + exchange(part[1:], 4, 2)
    part = flood(part, [8, 16] + more)
    part = jnp.concatenate([part, exchange(part, 4, 2)])
    blocks = jnp.concatenate([part, exchange(part, 2, 4)])
    blocks_oth = exchange(blocks, 1)
    mine = features(ints(one * 2 + two), frames, blocks)
    other = features(ints(two * 2 + one), frames, blocks_oth)

    order_own = one * 8 + two * 4 + near * 2 + far
    order_oth = two * 8 + one * 4 + near * 2 + far
    sent = gram(ints(order_oth, 1 - core, 1 - core), other, mine)
    sent = exchange(sent, 1)
    kept = gram(ints(order_own, core, core), mine, other)
    pieces = kept + sent
    pieces = pieces[:8] + exchange(pieces[8:], 2, 4)
    pieces = pieces[:4] + exchange(pieces[4:], 4, 2)
    pieces = pieces[:2] + exchange(pieces[2:], 8)
    pieces = pieces[:1] + exchange(pieces[1:], 16)
    pieces = flood(pieces, more)
    for masks in ((16,), (8,), (4, 2), (2, 4)):
        pieces = jnp.concatenate([pieces, exchange(pieces, *masks)])
    matrix, side = assemble(ints(order_own), pieces)
    side_oth = exchange(side, 1)

    base_own = core * 8 + one * 4 + two * 2 + near
    base_oth = (1 - core) * 8 + two * 4 + one * 2 + near
    place = far ^ core
    sent = cross(ints(base_oth, place), targets, mine, other)
    sent = exchange(sent, 1)
    kept = cross(ints(base_own, place), targets, mine, other)
    crossed = (kept[:4] + sent[:4]) + exchange(kept[4:] + sent[4:], 2, 4)
    crossed = crossed[:2] + exchange(crossed[2:], 4, 2)
    crossed = crossed[:1] + exchange(crossed[1:], 8)
    feats = crossed.shape[1] // 2
    crossed = crossed[:, :feats] + exchange(crossed[:, feats:], 16)
    crossed = flood(crossed, more)
    crossed = jnp.concatenate([crossed, exchange(crossed, 16)], axis=1)
    crossed = jnp.concatenate([crossed, exchange(crossed, 8)])
    crossed = jnp.concatenate([crossed, exchange(crossed, 4, 2)])
    crossed_b = exchange(crossed, 2, 4)

    inverse = square(inverse_factor_of(matrix))
    inverse_oth = exchange(inverse, 1)
    coupling = couple(ints(core), inverse, inverse_oth, side, side_oth)
    to_solve = ints(core, far)
    wa = solve(to_solve, inverse, inverse_oth, coupling, crossed)
    wa_oth = exchange(wa, 1)
    wb = solve(to_solve, inverse, inverse_oth, coupling, crossed_b)
    wb_oth = exchange(wb, 1)
    outs = residual_part(ints(base_own, core), targets, mine, other, wa, wb, ())
    outs = residual_part(ints(base_oth, core), targets, mine, other, wa_oth, wb_oth, tuple(outs))
    return tuple(outs)


def solution(mesh):
    count = math.prod(mesh.shape.values())
    return jax.shard_map(
        functools.partial(per_device, count),
        mesh=mesh,
        in_specs=(
            P(ALL, None),
            P(ALL, None),
            P(ALL, None, None),
            P(ALL, None),
            P(),
        ),
        out_specs=(P(ALL, None), P()),
        check_vma=False,
    )
```

```python
import functools
import math

import jax
import jax.numpy as jnp
from jax import lax
from jax.experimental import pallas as pl
from jax.experimental.pallas import tpu as pltpu
from jax.sharding import PartitionSpec as P

ALL = ("wide", "narrow")
F32 = jnp.float32
BF16 = jnp.bfloat16
HIGHEST = lax.Precision.HIGHEST


BASE_OWN, BASE_OTH, CORE, FAR, PLACE, ORDER_OWN, ORDER_OTH, QUARTER_OWN, QUARTER_OTH, DEVICE = range(10)


def params(mib=24):
    return pltpu.CompilerParams(vmem_limit_bytes=mib * 1024 * 1024)


def cost(flops, nbytes):
    return pl.CostEstimate(flops=int(flops), bytes_accessed=int(nbytes), transcendentals=0)


def split(value):
    high = value.astype(BF16)
    return high, (value - high.astype(F32)).astype(BF16)


def dot_bf16(left, right):
    return jnp.dot(left, right, preferred_element_type=F32)


def dot3(left, right):
    (lh, ll), (rh, rl) = left, right
    return dot_bf16(lh, rh) + (dot_bf16(lh, rl) + dot_bf16(ll, rh))


def dot_full(left, right):
    return jnp.dot(left, right, precision=HIGHEST, preferred_element_type=F32)


TWO_PI = 2.0 * math.pi
PART_A = 6.28125
PART_B = 2.0 ** -24 * round((TWO_PI - PART_A) * 2.0 ** 24 / 2 ** 5) * 2 ** 5
PART_C = TWO_PI - PART_A - PART_B
SIN_POLY = [(-1.0) ** k / math.factorial(2 * k + 1) for k in range(7)]


def cosine(value):
    turns = jnp.floor(value * (1.0 / TWO_PI) + 0.5)
    rest = value - turns * PART_A
    rest = rest - turns * PART_B
    rest = rest - turns * PART_C
    half = rest * 0.5
    square = half * half
    poly = SIN_POLY[-1]
    for coefficient in SIN_POLY[-2::-1]:
        poly = poly * square + coefficient
    sine = half * poly
    return 1.0 - 2.0 * sine * sine


def pack_kernel(s_ref, order_ref, own_ref, oth_ref, pown_ref, poth_ref, out_ref):
    depth = own_ref.shape[1]
    wanted = order_ref[s_ref[CORE]]
    take_own = wanted == s_ref[DEVICE]
    take_oth = wanted == (s_ref[DEVICE] ^ 1)
    value = jnp.where(take_own, own_ref[0], jnp.where(take_oth, oth_ref[0], 0.0))
    phase = jnp.where(take_own, pown_ref[0], jnp.where(take_oth, poth_ref[0], 0.0))
    out_ref[0, :depth, :] = value
    tail = out_ref.shape[1] - depth
    rows = lax.broadcasted_iota(jnp.int32, (tail, out_ref.shape[2]), 0)
    out_ref[0, depth:, :] = jnp.where(rows == 0, jnp.broadcast_to(phase, rows.shape), 0.0)


def pack(scalars, block_order, own, oth, phase_own, phase_oth, padded):
    _, depth, feats = own.shape
    width = feats // 4
    block = pl.BlockSpec((1, depth, width), lambda q, s, o: (0, 0, q ^ s[QUARTER_OWN]))
    phase = pl.BlockSpec((1, 1, width), lambda q, s, o: (0, 0, q ^ s[QUARTER_OWN]))
    return pl.pallas_call(
        pack_kernel,
        out_shape=jax.ShapeDtypeStruct((4, padded, width), F32),
        grid_spec=pltpu.PrefetchScalarGridSpec(
            num_scalar_prefetch=2,
            grid=(4,),
            in_specs=[block, block, phase, phase],
            out_specs=pl.BlockSpec((1, padded, width), lambda q, s, o: (q, 0, 0)),
        ),
        compiler_params=params(),
        name="pack",
    )(scalars, block_order, own, oth, phase_own[:, None, :], phase_oth[:, None, :])


def features_kernel(quarter, s_ref, x_ref, p_ref, fh_ref, fl_ref, th_ref, tl_ref):
    depth = x_ref.shape[0]
    order = s_ref[quarter]
    turned = jnp.concatenate([p_ref[i ^ order] for i in range(4)], axis=1).T
    inner = dot_full(turned[:, :depth], x_ref[...]) + turned[:, depth : depth + 1]
    feats = math.sqrt(2.0 / turned.shape[0]) * cosine(inner)
    th_ref[...], tl_ref[...] = split(feats)
    fh_ref[...], fl_ref[...] = split(feats.T)


def features(quarter, scalars, frames_turned, blocks):
    depth, rows = frames_turned.shape
    feats = blocks.shape[0] * blocks.shape[2]
    tile = 256
    flat = pl.BlockSpec((tile, feats), lambda i, s: (i, 0))
    turned = pl.BlockSpec((feats, tile), lambda i, s: (0, i))
    return pl.pallas_call(
        functools.partial(features_kernel, quarter),
        out_shape=[jax.ShapeDtypeStruct((rows, feats), BF16)] * 2 + [jax.ShapeDtypeStruct((feats, rows), BF16)] * 2,
        grid_spec=pltpu.PrefetchScalarGridSpec(
            num_scalar_prefetch=1,
            grid=(rows // tile,),
            in_specs=[
                pl.BlockSpec((depth, tile), lambda i, s: (0, i)),
                pl.BlockSpec(blocks.shape, lambda i, s: (0, 0, 0)),
            ],
            out_specs=[flat, flat, turned, turned],
        ),
        compiler_params=params(),
        cost_estimate=cost(12 * rows * depth * feats, 4 * rows * depth + 8 * rows * feats),
        name="features",
    )(scalars, frames_turned, blocks)


def gram_kernel(kept, s_ref, mh, ml, mth, mtl, oh, ol, oth, otl, out_ref):
    order = s_ref[ORDER_OWN if kept else ORDER_OTH]
    half_row = s_ref[CORE] if kept else 1 - s_ref[CORE]
    m_is_second = half_row
    feats, _ = mth.shape
    half = feats // 2
    pieces, _, height, _ = out_ref.shape

    def put(tile, value):
        for g in range(pieces):
            out_ref[g ^ order, tile] = value[g * height : (g + 1) * height]

    top = (mth[:half], mtl[:half])
    low = (mth[half:], mtl[half:])
    left = (mh[:, :half], ml[:, :half])
    right = (mh[:, half:], ml[:, half:])
    put(0, dot3(top, left))
    put(1, dot3(low, left))
    put(2, dot3(low, right))

    def cross(th, tl, h, l):
        start = pl.multiple_of(half_row * half, half)
        side = (th[pl.ds(start, half)], tl[pl.ds(start, half)])
        put(3, dot3(side, (h[:, :half], l[:, :half])))
        put(4, dot3(side, (h[:, half:], l[:, half:])))

    @pl.when(m_is_second == 1)
    def _():
        cross(mth, mtl, oh, ol)

    @pl.when(m_is_second == 0)
    def _():
        cross(oth, otl, mh, ml)


def gram(kept, scalars, mine, other):
    rows, feats = mine[0].shape
    return pl.pallas_call(
        functools.partial(gram_kernel, kept),
        out_shape=jax.ShapeDtypeStruct((16, 5, feats // 32, feats // 2), F32),
        in_specs=[pl.BlockSpec(memory_space=pltpu.SMEM)] + [pl.BlockSpec(memory_space=pltpu.VMEM)] * 8,
        out_specs=pl.BlockSpec(memory_space=pltpu.VMEM),
        compiler_params=params(),
        cost_estimate=cost(6 * rows * feats * feats * 1.25, 16 * rows * feats),
        name="gram",
    )(scalars, *mine, *other)


def cross_kernel(base, s_ref, t_ref, ath, atl, bth, btl, *rest):
    out_ref = rest[-1]
    place, swap = s_ref[PLACE], s_ref[base] & 1
    feats = ath.shape[0]
    half = feats // 2
    width = out_ref.shape[2]
    right = split(t_ref[...])

    def rows_of(th, tl, start):
        def body(i, carry):
            at = pl.multiple_of(i * half, half)
            value = dot3((th[pl.ds(at, half), :], tl[pl.ds(at, half), :]), right)
            to = pl.ds(pl.multiple_of(start + at, half), half)
            for k in range(2):
                part = value[:, k * width : (k + 1) * width]
                if len(rest) == 2:
                    part = part + rest[0][k ^ swap, to, :]
                out_ref[k ^ swap, to, :] = part
            return carry

        lax.fori_loop(0, 2, body, 0)

    rows_of(ath, atl, place * feats)
    rows_of(bth, btl, (1 - place) * feats)


def cross(base, group, scalars, targets, mine, other, before=()):
    rows, columns = targets.shape
    feats = mine[2].shape[0]
    width = columns // 16
    whole = pl.BlockSpec((feats, rows), lambda k, s: (0, 0))
    pair = pl.BlockSpec((2, 2 * feats, width), lambda k, s: (k, 0, 0))
    return pl.pallas_call(
        functools.partial(cross_kernel, base),
        out_shape=jax.ShapeDtypeStruct((4, 2 * feats, width), F32),
        grid_spec=pltpu.PrefetchScalarGridSpec(
            num_scalar_prefetch=1,
            grid=(2,),
            in_specs=[pl.BlockSpec((rows, 2 * width), lambda k, s: (0, (s[base] >> 1) ^ (2 * group + k)))]
            + [whole] * 4
            + [pair] * len(before),
            out_specs=pair,
        ),
        compiler_params=params(),
        cost_estimate=cost(3 * rows * feats * columns, 2 * rows * columns),
        name="cross",
    )(scalars, targets, mine[2], mine[3], other[2], other[3], *before)


def unit_inverse(block):
    size, lanes = block.shape
    groups = size // 8
    lane = lax.broadcasted_iota(jnp.int32, (8, lanes), 1)
    sub = lax.broadcasted_iota(jnp.int32, (8, lanes), 0)

    def wide(column):
        return jnp.broadcast_to(column, (8, lanes))

    def turn(i, carry):
        rows, pivots = list(carry[0]), list(carry[1])
        before = list(rows)
        top_pivots = pivots[0]
        for j in range(0, 8, 2):
            pair = (lane == j) | (lane == j + 1)
            top = rows[0]
            col_a, col_b = wide(top[:, j : j + 1]), wide(top[:, j + 1 : j + 2])
            a, b, c = wide(col_a[j : j + 1]), wide(col_a[j + 1 : j + 2]), wide(col_b[j + 1 : j + 2])
            row_a, row_b = wide(top[j : j + 1]), wide(top[j + 1 : j + 2])
            inv_a = 1.0 / a
            inv_c = a * (1.0 / (a * c - b * b))
            link = b * inv_a
            use_a = jnp.where(lane == j, 1.0, jnp.where(lane == j + 1, 0.0, row_a))
            use_b = jnp.where(lane == j, -link, jnp.where(lane == j + 1, 1.0, row_b - link * row_a))
            m_a = jnp.where(sub > j, col_a * inv_a, 0.0)
            m_b = jnp.where(sub > j + 1, (col_b - m_a * b) * inv_c, 0.0)
            unit = jnp.where(pair & (lane == sub), 1.0, 0.0)
            rows[0] = jnp.where(pair, unit, top) - m_a * use_a - m_b * use_b
            top_pivots = jnp.where(sub == j, a, jnp.where(sub == j + 1, c - link * b, top_pivots))
            for g in range(1, groups):
                m_a = wide(rows[g][:, j : j + 1]) * inv_a
                m_b = (wide(rows[g][:, j + 1 : j + 2]) - m_a * b) * inv_c
                rows[g] = jnp.where(pair, 0.0, rows[g]) - m_a * use_a - m_b * use_b
        for g in range(1, groups):
            rows[g] = jnp.where(g < groups - i, rows[g], before[g])
        rows = [pltpu.roll(r, lanes - 8, 1) for r in rows]
        return tuple(rows[1:] + rows[:1]), tuple(pivots[1:] + [top_pivots])

    start = tuple(block[8 * g : 8 * g + 8] for g in range(groups))
    rows, pivots = lax.fori_loop(0, groups, turn, (start, start))
    scaled = [
        jnp.where(lane <= sub + 8 * g, rows[g] * lax.rsqrt(pivots[g]), 0.0) for g in range(groups)
    ]
    return jnp.concatenate(scaled, axis=0)


def eliminate(m_ref, start, size):
    total = m_ref.shape[0]
    here = slice(start, start + size)
    inverse = unit_inverse(m_ref[here, here])
    if start:
        m_ref[here, :start] = dot_full(inverse, m_ref[here, :start])
    if start + size < total:
        below = slice(start + size, total)
        panel = lax.dot_general(
            m_ref[below, here], inverse, (((1,), (1,)), ((), ())), precision=HIGHEST, preferred_element_type=F32
        )
        m_ref[here, below] = dot_full(inverse, m_ref[here, below])
        m_ref[below, here] = jnp.zeros((total - start - size, size), F32)
        m_ref[here, here] = inverse
        m_ref[below, :] = m_ref[below, :] - dot_full(panel, m_ref[here, :])
    else:
        m_ref[here, here] = inverse


def assemble_kernel(s_ref, g_ref, a_ref, side_ref):
    order = s_ref[ORDER_OWN]
    pieces, _, height, half = g_ref.shape
    for g in range(pieces):
        piece = g_ref[g ^ order]
        here = slice(g * height, (g + 1) * height)
        there = slice(half + g * height, half + (g + 1) * height)
        a_ref[here, :half] = piece[0]
        a_ref[there, :half] = piece[1]
        a_ref[there, half:] = piece[2]
        side_ref[here, :half] = piece[3]
        side_ref[here, half:] = piece[4]
    a_ref[:half, half:] = a_ref[half:, :half].T
    whole = a_ref[...]
    eye = lax.broadcasted_iota(jnp.int32, whole.shape, 0) == lax.broadcasted_iota(jnp.int32, whole.shape, 1)
    diagonal = jnp.where(eye, whole, 0.0)
    damping = 0.1 * jnp.sum(diagonal) / whole.shape[0]
    a_ref[...] = whole + jnp.where(eye, damping, 0.0)
    eliminate(a_ref, 0, whole.shape[0] // 4)


def assemble(order, pieces):
    half = pieces.shape[3]
    return pl.pallas_call(
        assemble_kernel,
        out_shape=[jax.ShapeDtypeStruct((2 * half, 2 * half), F32), jax.ShapeDtypeStruct((half, 2 * half), F32)],
        in_specs=[pl.BlockSpec(memory_space=pltpu.SMEM), pl.BlockSpec(memory_space=pltpu.VMEM)],
        out_specs=[pl.BlockSpec(memory_space=pltpu.VMEM)] * 2,
        compiler_params=params(),
        cost_estimate=cost(1e10, 4e6),
        name="assemble",
    )(order, pieces)


def factor_kernel(step, m_ref, out_ref):
    out_ref[...] = m_ref[...]
    eliminate(out_ref, step * (m_ref.shape[0] // 4), m_ref.shape[0] // 4)
    if step == 3:
        whole = out_ref[...]
        low = lax.broadcasted_iota(jnp.int32, whole.shape, 0) >= lax.broadcasted_iota(jnp.int32, whole.shape, 1)
        whole = jnp.where(low, whole, 0.0)
        out_ref[...] = dot_full(whole.T, whole)


def factor(step, matrix):
    return pl.pallas_call(
        functools.partial(factor_kernel, step),
        out_shape=jax.ShapeDtypeStruct(matrix.shape, F32),
        in_specs=[pl.BlockSpec(memory_space=pltpu.VMEM)],
        out_specs=pl.BlockSpec(memory_space=pltpu.VMEM),
        compiler_params=params(),
        cost_estimate=cost(1e10, 4e6),
        name="factor",
    )(matrix)


def couple_kernel(s_ref, own_ref, oth_ref, gown_ref, goth_ref, out_ref):
    core = s_ref[CORE]
    half = gown_ref.shape[0]
    second = jnp.where(core == 1, own_ref[...], oth_ref[...])
    top = jnp.where(core == 0, gown_ref[...], goth_ref[...])
    low = jnp.where(core == 0, goth_ref[...], gown_ref[...])
    out_ref[...] = dot_full(second[:, :half], top) + dot_full(second[:, half:], low)


def couple(core, own, oth, side_own, side_oth):
    return pl.pallas_call(
        couple_kernel,
        out_shape=jax.ShapeDtypeStruct(own.shape, F32),
        in_specs=[pl.BlockSpec(memory_space=pltpu.SMEM)] + [pl.BlockSpec(memory_space=pltpu.VMEM)] * 4,
        compiler_params=params(),
        name="couple",
    )(core, own, oth, side_own, side_oth)


def solve_kernel(s_ref, own_ref, oth_ref, b_ref, c_ref, out_ref, one_ref):
    core, far = s_ref[CORE], s_ref[FAR]
    feats = own_ref.shape[0]
    half = feats // 2
    width = c_ref.shape[2]

    def columns_of(step):
        start = pl.multiple_of((step ^ far) * feats, feats)
        return jnp.concatenate([c_ref[k, pl.ds(start, feats), :] for k in range(2)], axis=1)

    right = columns_of(0)

    def first(i, carry):
        here = pl.ds(pl.multiple_of(i * half, half), half)
        one = dot_full(jnp.where(core == 0, own_ref[here, :], oth_ref[here, :]), right)
        one_ref[here, :] = one
        for k in range(2):
            out_ref[k, here, :] = one[:, k * width : (k + 1) * width]
        return carry

    lax.fori_loop(0, 2, first, 0)
    right_two = jnp.concatenate([columns_of(1), one_ref[...]], axis=0)

    def second(i, carry):
        here = pl.ds(pl.multiple_of(i * half, half), half)
        there = pl.ds(pl.multiple_of(feats + i * half, half), half)
        left = jnp.where(core == 0, oth_ref[here, :], own_ref[here, :])
        two = dot_full(jnp.concatenate([left, -b_ref[here, :]], axis=1), right_two)
        for k in range(2):
            out_ref[k, there, :] = two[:, k * width : (k + 1) * width]
        return carry

    lax.fori_loop(0, 2, second, 0)


def solve(scalars, own, oth, coupling, crossed):
    count, height, width = crossed.shape
    feats = own.shape[0]
    whole = pl.BlockSpec((feats, feats), lambda k, s: (0, 0))
    pair = pl.BlockSpec((2, height, width), lambda k, s: (k, 0, 0))
    return pl.pallas_call(
        solve_kernel,
        out_shape=jax.ShapeDtypeStruct(crossed.shape, F32),
        grid_spec=pltpu.PrefetchScalarGridSpec(
            num_scalar_prefetch=1,
            grid=(count // 2,),
            in_specs=[whole] * 3 + [pair],
            out_specs=pair,
            scratch_shapes=[pltpu.VMEM((feats, 2 * width), F32)],
        ),
        compiler_params=params(),
        cost_estimate=cost(36 * feats * feats * count * width, 8 * count * height * width),
        name="solve",
    )(scalars, own, oth, coupling, crossed)


def residual_kernel(base, s_ref, t_ref, ah, al, bh, bl, w_in, *rest):
    r_ref, w_ref = rest[-2:]
    swap, core = s_ref[base] & 1, s_ref[CORE]
    rows, feats = ah.shape
    half = rows // 2

    def take(step):
        start = pl.multiple_of(step * feats, feats)
        return jnp.concatenate([w_in[i ^ swap, pl.ds(start, feats), :] for i in range(2)], axis=1)

    mine, other = take(core), take(1 - core)
    w_ref[core], w_ref[1 - core] = mine, other
    (mh, ml), (oh, ol) = split(mine), split(other)

    def body(i, carry):
        here = pl.ds(pl.multiple_of(i * half, half), half)
        fitted = dot3((ah[here, :], al[here, :]), (mh, ml)) + dot3((bh[here, :], bl[here, :]), (oh, ol))
        r_ref[here, :] = t_ref[here, :] - fitted
        return carry

    lax.fori_loop(0, 2, body, 0)


def residual_part(base, group, scalars, targets, mine, other, weights, before):
    rows, columns = targets.shape
    feats = mine[0].shape[1]
    _, height, width = weights.shape
    whole = pl.BlockSpec((rows, feats), lambda k, s: (0, 0))
    block = pl.BlockSpec((rows, 2 * width), lambda k, s: (0, (s[base] >> 1) ^ (2 * group + k)))
    anywhere = pl.BlockSpec(memory_space=pl.ANY)
    return pl.pallas_call(
        functools.partial(residual_kernel, base),
        out_shape=[
            jax.ShapeDtypeStruct((rows, columns), F32),
            jax.ShapeDtypeStruct((2, feats, columns), F32),
        ],
        grid_spec=pltpu.PrefetchScalarGridSpec(
            num_scalar_prefetch=1,
            grid=(2,),
            in_specs=[block]
            + [whole] * 4
            + [pl.BlockSpec((2, height, width), lambda k, s: (k, 0, 0))]
            + [anywhere] * len(before),
            out_specs=[
                block,
                pl.BlockSpec((2, feats, 2 * width), lambda k, s: (0, 0, (s[base] >> 1) ^ (2 * group + k))),
            ],
        ),
        input_output_aliases={7: 0, 8: 1} if before else {},
        compiler_params=params(),
        cost_estimate=cost(3 * rows * feats * columns, 3 * rows * columns),
        name="residual",
    )(scalars, targets, mine[0], mine[1], other[0], other[1], weights, *before)


def ints(*values):
    return jnp.stack([jnp.asarray(v, jnp.int32) for v in values])


def per_device(count, frames, targets, projection, phases, block_order):
    n_bits = count.bit_length() - 1
    device = lax.axis_index(ALL)
    bit = [(device >> k) & 1 for k in range(n_bits)]
    core = bit[0]
    one = jnp.where(core == 0, bit[1], bit[2])
    two = jnp.where(core == 0, bit[2], bit[1])
    near, far = bit[3], bit[4]
    more = [1 << k for k in range(5, n_bits)]

    def exchange(value, even, odd=None):
        odd = even if odd is None else odd
        pairs = [(i, i ^ (odd if i & 1 else even)) for i in range(count)]
        return lax.ppermute(value, ALL, pairs)

    def flood(value, masks):
        for mask in masks:
            value = value + exchange(value, mask)
        return value

    scalars = ints(
        core * 8 + one * 4 + two * 2 + near,
        (1 - core) * 8 + two * 4 + one * 2 + near,
        core,
        far,
        far ^ core,
        one * 8 + two * 4 + near * 2 + far,
        two * 8 + one * 4 + near * 2 + far,
        one * 2 + two,
        two * 2 + one,
        device,
    )

    projection_oth, phases_oth = exchange(projection, 1), exchange(phases, 1)
    padded = (projection.shape[1] // 8 + 1) * 8
    blocks = pack(scalars, block_order, projection, projection_oth, phases, phases_oth, padded)
    part = blocks[:2] + exchange(blocks[2:], 2, 4)
    part = part[:1] + exchange(part[1:], 4, 2)
    part = flood(part, [8, 16] + more)
    part = jnp.concatenate([part, exchange(part, 4, 2)])
    blocks = jnp.concatenate([part, exchange(part, 2, 4)])
    blocks_oth = exchange(blocks, 1)
    mine = features(QUARTER_OWN, scalars, frames.T, blocks)
    other = features(QUARTER_OTH, scalars, frames.T, blocks_oth)

    def after(done, sides):
        gated = lax.optimization_barrier([done, *sides[0], *sides[1]])
        return gated[1:5], gated[5:]

    sides = mine, other
    gram_sent = gram(False, scalars, other, mine)
    gram_came = exchange(gram_sent, 1)
    sides = after(gram_sent, sides)
    sent = cross(BASE_OTH, 1, scalars, targets, *sides)
    came_b = exchange(sent, 1)
    sides = after(sent, sides)
    pieces = gram(True, scalars, *sides) + gram_came
    sides = after(pieces, sides)
    sent = cross(BASE_OTH, 0, scalars, targets, *sides)
    came_a = exchange(sent, 1)
    sides = after(sent, sides)
    moving = cross(BASE_OWN, 1, scalars, targets, *sides, (came_b,))
    sides = after(moving, sides)
    staying = cross(BASE_OWN, 0, scalars, targets, *sides, (came_a,))

    moved = exchange(pieces[8:], 2, 4)
    pieces = pieces[:8] + moved
    pieces = pieces[:4] + exchange(pieces[4:], 4, 2)
    pieces, staying = lax.optimization_barrier([pieces, staying])
    pieces = pieces[:2] + exchange(pieces[2:], 8)
    pieces = pieces[:1] + exchange(pieces[1:], 16)
    pieces = flood(pieces, more)
    for masks in ((16,), (8,), (4, 2), (2, 4)):
        pieces = jnp.concatenate([pieces, exchange(pieces, *masks)])

    moved = exchange(moving, 2, 4)
    crossed = staying + moved
    crossed = crossed[:2] + exchange(crossed[2:], 4, 2)
    crossed = crossed[:1] + exchange(crossed[1:], 8)
    feats = crossed.shape[1] // 2
    crossed = crossed[:, :feats] + exchange(crossed[:, feats:], 16)
    crossed = flood(crossed, more)
    crossed = jnp.concatenate([crossed, exchange(crossed, 16)], axis=1)
    crossed = jnp.concatenate([crossed, exchange(crossed, 8)])
    crossed = jnp.concatenate([crossed, exchange(crossed, 4, 2)])

    matrix, side = assemble(scalars, pieces)
    side_oth = exchange(side, 1)
    for step in (1, 2, 3):
        matrix = factor(step, matrix)
    inverse = matrix
    inverse_oth = exchange(inverse, 1)
    coupling = couple(scalars, inverse, inverse_oth, side, side_oth)
    weights = solve(scalars, inverse, inverse_oth, coupling, crossed)
    weights_b = exchange(weights, 2, 4)
    outs = ()
    for group, part in ((0, weights), (1, weights_b)):
        part_oth = exchange(part, 1)
        for base, value in ((BASE_OWN, part), (BASE_OTH, part_oth)):
            outs = residual_part(base, group, scalars, targets, mine, other, value, tuple(outs))
    return tuple(outs)


def solution(mesh):
    count = math.prod(mesh.shape.values())

    def body(*arrays):
        return per_device(count, *arrays)

    return jax.shard_map(
        body,
        mesh=mesh,
        in_specs=(
            P(ALL, None),
            P(ALL, None),
            P(ALL, None, None),
            P(ALL, None),
            P(),
        ),
        out_specs=(P(ALL, None), P()),
        check_vma=False,
    )
```

```python
import functools
import math

import jax
import jax.numpy as jnp
from jax import lax
from jax.experimental import pallas as pl
from jax.experimental.pallas import tpu as pltpu
from jax.sharding import PartitionSpec as P

ALL = ("wide", "narrow")
F32 = jnp.float32
BF16 = jnp.bfloat16
HIGHEST = lax.Precision.HIGHEST


BASE_OWN, BASE_OTH, CORE, TURN, ORDER_OWN, ORDER_OTH, QUARTER_OWN, QUARTER_OTH, DEVICE = range(9)


def params(mib=24):
    return pltpu.CompilerParams(vmem_limit_bytes=mib * 1024 * 1024)


def cost(flops, nbytes):
    return pl.CostEstimate(flops=int(flops), bytes_accessed=int(nbytes), transcendentals=0)


def split(value):
    high = value.astype(BF16)
    return high, (value - high.astype(F32)).astype(BF16)


def dot_bf16(left, right):
    return jnp.dot(left, right, preferred_element_type=F32)


def dot3(left, right):
    (lh, ll), (rh, rl) = left, right
    return dot_bf16(lh, rh) + (dot_bf16(lh, rl) + dot_bf16(ll, rh))


def dot_full(left, right):
    return jnp.dot(left, right, precision=HIGHEST, preferred_element_type=F32)


TWO_PI = 2.0 * math.pi
PART_A = 6.28125
PART_B = 2.0 ** -24 * round((TWO_PI - PART_A) * 2.0 ** 24 / 2 ** 5) * 2 ** 5
PART_C = TWO_PI - PART_A - PART_B
SIN_POLY = [(-1.0) ** k / math.factorial(2 * k + 1) for k in range(7)]


def cosine(value):
    turns = jnp.floor(value * (1.0 / TWO_PI) + 0.5)
    rest = value - turns * PART_A
    rest = rest - turns * PART_B
    rest = rest - turns * PART_C
    half = rest * 0.5
    square = half * half
    poly = SIN_POLY[-1]
    for coefficient in SIN_POLY[-2::-1]:
        poly = poly * square + coefficient
    sine = half * poly
    return 1.0 - 2.0 * sine * sine


def pack_kernel(s_ref, order_ref, own_ref, oth_ref, pown_ref, poth_ref, out_ref):
    depth = own_ref.shape[1]
    wanted = order_ref[s_ref[CORE]]
    take_own = wanted == s_ref[DEVICE]
    take_oth = wanted == (s_ref[DEVICE] ^ 1)
    value = jnp.where(take_own, own_ref[0], jnp.where(take_oth, oth_ref[0], 0.0))
    phase = jnp.where(take_own, pown_ref[0], jnp.where(take_oth, poth_ref[0], 0.0))
    out_ref[0, :depth, :] = value
    tail = out_ref.shape[1] - depth
    rows = lax.broadcasted_iota(jnp.int32, (tail, out_ref.shape[2]), 0)
    out_ref[0, depth:, :] = jnp.where(rows == 0, jnp.broadcast_to(phase, rows.shape), 0.0)


def pack(scalars, block_order, own, oth, phase_own, phase_oth, padded):
    _, depth, feats = own.shape
    width = feats // 4
    block = pl.BlockSpec((1, depth, width), lambda q, s, o: (0, 0, q ^ s[QUARTER_OWN]))
    phase = pl.BlockSpec((1, 1, width), lambda q, s, o: (0, 0, q ^ s[QUARTER_OWN]))
    return pl.pallas_call(
        pack_kernel,
        out_shape=jax.ShapeDtypeStruct((4, padded, width), F32),
        grid_spec=pltpu.PrefetchScalarGridSpec(
            num_scalar_prefetch=2,
            grid=(4,),
            in_specs=[block, block, phase, phase],
            out_specs=pl.BlockSpec((1, padded, width), lambda q, s, o: (q, 0, 0)),
        ),
        compiler_params=params(),
        name="pack",
    )(scalars, block_order, own, oth, phase_own[:, None, :], phase_oth[:, None, :])


def features_kernel(quarter, s_ref, x_ref, p_ref, fh_ref, fl_ref, th_ref, tl_ref):
    depth = x_ref.shape[0]
    order = s_ref[quarter]
    turned = jnp.concatenate([p_ref[i ^ order] for i in range(4)], axis=1).T
    inner = dot_full(turned[:, :depth], x_ref[...]) + turned[:, depth : depth + 1]
    feats = math.sqrt(2.0 / turned.shape[0]) * cosine(inner)
    th_ref[...], tl_ref[...] = split(feats)
    fh_ref[...], fl_ref[...] = split(feats.T)


def features(quarter, scalars, frames_turned, blocks):
    depth, rows = frames_turned.shape
    feats = blocks.shape[0] * blocks.shape[2]
    tile = 256
    flat = pl.BlockSpec((tile, feats), lambda i, s: (i, 0))
    turned = pl.BlockSpec((feats, tile), lambda i, s: (0, i))
    return pl.pallas_call(
        functools.partial(features_kernel, quarter),
        out_shape=[jax.ShapeDtypeStruct((rows, feats), BF16)] * 2 + [jax.ShapeDtypeStruct((feats, rows), BF16)] * 2,
        grid_spec=pltpu.PrefetchScalarGridSpec(
            num_scalar_prefetch=1,
            grid=(rows // tile,),
            in_specs=[
                pl.BlockSpec((depth, tile), lambda i, s: (0, i)),
                pl.BlockSpec(blocks.shape, lambda i, s: (0, 0, 0)),
            ],
            out_specs=[flat, flat, turned, turned],
        ),
        compiler_params=params(),
        cost_estimate=cost(12 * rows * depth * feats, 4 * rows * depth + 8 * rows * feats),
        name="features",
    )(scalars, frames_turned, blocks)


def gram_kernel(kept, s_ref, mh, ml, mth, mtl, oh, ol, oth, otl, out_ref):
    order = s_ref[ORDER_OWN if kept else ORDER_OTH]
    half_row = s_ref[CORE] if kept else 1 - s_ref[CORE]
    m_is_second = half_row
    feats, _ = mth.shape
    half = feats // 2
    pieces, _, height, _ = out_ref.shape

    def put(tile, value):
        for g in range(pieces):
            out_ref[g ^ order, tile] = value[g * height : (g + 1) * height]

    top = (mth[:half], mtl[:half])
    low = (mth[half:], mtl[half:])
    left = (mh[:, :half], ml[:, :half])
    right = (mh[:, half:], ml[:, half:])
    put(0, dot3(top, left))
    put(1, dot3(low, left))
    put(2, dot3(low, right))

    def cross(th, tl, h, l):
        start = pl.multiple_of(half_row * half, half)
        side = (th[pl.ds(start, half)], tl[pl.ds(start, half)])
        put(3, dot3(side, (h[:, :half], l[:, :half])))
        put(4, dot3(side, (h[:, half:], l[:, half:])))

    @pl.when(m_is_second == 1)
    def _():
        cross(mth, mtl, oh, ol)

    @pl.when(m_is_second == 0)
    def _():
        cross(oth, otl, mh, ml)


def gram(kept, scalars, mine, other):
    rows, feats = mine[0].shape
    return pl.pallas_call(
        functools.partial(gram_kernel, kept),
        out_shape=jax.ShapeDtypeStruct((16, 5, feats // 32, feats // 2), F32),
        in_specs=[pl.BlockSpec(memory_space=pltpu.SMEM)] + [pl.BlockSpec(memory_space=pltpu.VMEM)] * 8,
        out_specs=pl.BlockSpec(memory_space=pltpu.VMEM),
        compiler_params=params(),
        cost_estimate=cost(6 * rows * feats * feats * 1.25, 16 * rows * feats),
        name="gram",
    )(scalars, *mine, *other)


def cross_kernel(base, s_ref, t_ref, ath, atl, bth, btl, *rest):
    out_ref = rest[-1]
    core, turn, swap = s_ref[CORE], s_ref[TURN], s_ref[base] & 1
    half = ath.shape[0] // 2
    width = out_ref.shape[2]
    right = split(t_ref[...])

    def rows_of(th, tl, step):
        def body(i, carry):
            at = pl.ds(pl.multiple_of(i * half, half), half)
            value = dot3((th[at, :], tl[at, :]), right)
            to = pl.ds(pl.multiple_of(((2 * step + i) ^ turn) * half, half), half)
            for k in range(2):
                part = value[:, k * width : (k + 1) * width]
                if len(rest) == 2:
                    part = part + rest[0][k ^ swap, to, :]
                out_ref[k ^ swap, to, :] = part
            return carry

        lax.fori_loop(0, 2, body, 0)

    rows_of(ath, atl, core)
    rows_of(bth, btl, 1 - core)


def cross(base, group, scalars, targets, mine, other, before=()):
    rows, columns = targets.shape
    feats = mine[2].shape[0]
    width = columns // 16
    whole = pl.BlockSpec((feats, rows), lambda k, s: (0, 0))
    pair = pl.BlockSpec((2, 2 * feats, width), lambda k, s: (k, 0, 0))
    return pl.pallas_call(
        functools.partial(cross_kernel, base),
        out_shape=jax.ShapeDtypeStruct((4, 2 * feats, width), F32),
        grid_spec=pltpu.PrefetchScalarGridSpec(
            num_scalar_prefetch=1,
            grid=(2,),
            in_specs=[pl.BlockSpec((rows, 2 * width), lambda k, s: (0, 4 * group + ((s[base] >> 1) ^ k)))]
            + [whole] * 4
            + [pair] * len(before),
            out_specs=pair,
        ),
        compiler_params=params(),
        cost_estimate=cost(3 * rows * feats * columns, 2 * rows * columns),
        name="cross",
    )(scalars, targets, mine[2], mine[3], other[2], other[3], *before)


def unit_inverse(block):
    size, lanes = block.shape
    groups = size // 8
    lane = lax.broadcasted_iota(jnp.int32, (8, lanes), 1)
    sub = lax.broadcasted_iota(jnp.int32, (8, lanes), 0)

    def wide(row):
        return jnp.broadcast_to(row, (8, lanes))

    def make(active):
        def turn(i, carry):
            rows, pivots = list(carry[0]), list(carry[1])
            spots = [jnp.full((8, lanes), 8 * i + k, jnp.int32) for k in range(8)]
            here = (lane >= 8 * i) & (lane < 8 * i + 8)
            top = rows[0]
            cols = [jnp.take_along_axis(top, spot, axis=1) for spot in spots]
            x = jnp.where(here, jnp.where(lane - 8 * i == sub, 1.0, 0.0), top)
            diagonal, inverse = top, []
            for j in range(0, 8, 2):
                a, b, c = wide(cols[j][j : j + 1]), wide(cols[j][j + 1 : j + 2]), wide(cols[j + 1][j + 1 : j + 2])
                inv_a = 1.0 / a
                inv_c = a * (1.0 / (a * c - b * b))
                link = b * inv_a
                inverse += [inv_a, inv_c]
                diagonal = jnp.where(sub == j, a, jnp.where(sub == j + 1, c - link * b, diagonal))
                m_a = jnp.where(sub > j, cols[j] * inv_a, 0.0)
                m_b = jnp.where(sub > j + 1, (cols[j + 1] - m_a * b) * inv_c, 0.0)

                def swept(value):
                    one = wide(value[j : j + 1])
                    two = wide(value[j + 1 : j + 2]) - link * one
                    return value - m_a * one - m_b * two

                for k in range(j + 1, 8):
                    cols[k] = swept(cols[k])
                x = swept(x)
            rest, z = x, [None] * 8
            for j in range(7, -1, -1):
                z[j] = wide(rest[j : j + 1]) * inverse[j]
                if j:
                    rest = rest - jnp.where(sub < j, cols[j], 0.0) * z[j]
            for g in range(1, active):
                parts = [jnp.take_along_axis(rows[g], spots[k], axis=1) * z[k] for k in range(8)]
                total = ((parts[0] + parts[1]) + (parts[2] + parts[3])) + ((parts[4] + parts[5]) + (parts[6] + parts[7]))
                rows[g] = jnp.where(g < groups - i, jnp.where(here, 0.0, rows[g]) - total, rows[g])
            return tuple(rows[1:] + [x]), tuple(pivots[1:] + [diagonal])

        return turn

    start = tuple(block[8 * g : 8 * g + 8] for g in range(groups))
    state = (start, start)
    state = lax.fori_loop(0, groups // 2, make(groups), state)
    rows, pivots = lax.fori_loop(groups // 2, groups, make(groups // 2), state)
    scaled = [
        jnp.where(lane <= sub + 8 * g, rows[g] * lax.rsqrt(pivots[g]), 0.0) for g in range(groups)
    ]
    return jnp.concatenate(scaled, axis=0)


def eliminate(m_ref, start, size):
    total = m_ref.shape[0]
    here = slice(start, start + size)
    inverse = unit_inverse(m_ref[here, here])
    if start:
        m_ref[here, :start] = dot_full(inverse, m_ref[here, :start])
    if start + size < total:
        below = slice(start + size, total)
        panel = lax.dot_general(
            m_ref[below, here], inverse, (((1,), (1,)), ((), ())), precision=HIGHEST, preferred_element_type=F32
        )
        m_ref[here, below] = dot_full(inverse, m_ref[here, below])
        m_ref[below, here] = jnp.zeros((total - start - size, size), F32)
        m_ref[here, here] = inverse
        m_ref[below, :] = m_ref[below, :] - dot_full(panel, m_ref[here, :])
    else:
        m_ref[here, here] = inverse


def assemble_kernel(s_ref, g_ref, a_ref, side_ref):
    order = s_ref[ORDER_OWN]
    pieces, _, height, half = g_ref.shape
    for g in range(pieces):
        piece = g_ref[g ^ order]
        here = slice(g * height, (g + 1) * height)
        there = slice(half + g * height, half + (g + 1) * height)
        a_ref[here, :half] = piece[0]
        a_ref[there, :half] = piece[1]
        a_ref[there, half:] = piece[2]
        side_ref[here, :half] = piece[3]
        side_ref[here, half:] = piece[4]
    a_ref[:half, half:] = a_ref[half:, :half].T
    whole = a_ref[...]
    eye = lax.broadcasted_iota(jnp.int32, whole.shape, 0) == lax.broadcasted_iota(jnp.int32, whole.shape, 1)
    diagonal = jnp.where(eye, whole, 0.0)
    damping = 0.1 * jnp.sum(diagonal) / whole.shape[0]
    a_ref[...] = whole + jnp.where(eye, damping, 0.0)
    eliminate(a_ref, 0, whole.shape[0] // 4)


def assemble(order, pieces):
    half = pieces.shape[3]
    return pl.pallas_call(
        assemble_kernel,
        out_shape=[jax.ShapeDtypeStruct((2 * half, 2 * half), F32), jax.ShapeDtypeStruct((half, 2 * half), F32)],
        in_specs=[pl.BlockSpec(memory_space=pltpu.SMEM), pl.BlockSpec(memory_space=pltpu.VMEM)],
        out_specs=[pl.BlockSpec(memory_space=pltpu.VMEM)] * 2,
        compiler_params=params(),
        cost_estimate=cost(1e10, 4e6),
        name="assemble",
    )(order, pieces)


def factor_kernel(step, m_ref, out_ref):
    out_ref[...] = m_ref[...]
    eliminate(out_ref, step * (m_ref.shape[0] // 4), m_ref.shape[0] // 4)
    if step == 3:
        whole = out_ref[...]
        low = lax.broadcasted_iota(jnp.int32, whole.shape, 0) >= lax.broadcasted_iota(jnp.int32, whole.shape, 1)
        whole = jnp.where(low, whole, 0.0)
        out_ref[...] = dot_full(whole.T, whole)


def factor(step, matrix):
    return pl.pallas_call(
        functools.partial(factor_kernel, step),
        out_shape=jax.ShapeDtypeStruct(matrix.shape, F32),
        in_specs=[pl.BlockSpec(memory_space=pltpu.VMEM)],
        out_specs=pl.BlockSpec(memory_space=pltpu.VMEM),
        compiler_params=params(),
        cost_estimate=cost(1e10, 4e6),
        name="factor",
    )(matrix)


def couple_kernel(s_ref, own_ref, oth_ref, gown_ref, goth_ref, out_ref):
    core = s_ref[CORE]
    half = gown_ref.shape[0]
    second = jnp.where(core == 1, own_ref[...], oth_ref[...])
    top = jnp.where(core == 0, gown_ref[...], goth_ref[...])
    low = jnp.where(core == 0, goth_ref[...], gown_ref[...])
    out_ref[...] = dot_full(second[:, :half], top) + dot_full(second[:, half:], low)


def couple(core, own, oth, side_own, side_oth):
    return pl.pallas_call(
        couple_kernel,
        out_shape=jax.ShapeDtypeStruct(own.shape, F32),
        in_specs=[pl.BlockSpec(memory_space=pltpu.SMEM)] + [pl.BlockSpec(memory_space=pltpu.VMEM)] * 4,
        compiler_params=params(),
        name="couple",
    )(core, own, oth, side_own, side_oth)


def solve_kernel(s_ref, own_ref, oth_ref, b_ref, c_ref, out_ref, one_ref):
    core, turn = s_ref[CORE], s_ref[TURN]
    feats = own_ref.shape[0]
    half = feats // 2
    width = c_ref.shape[2]

    def columns_of(step):
        starts = [pl.multiple_of(((2 * step + i) ^ turn) * half, half) for i in range(2)]
        return jnp.concatenate(
            [jnp.concatenate([c_ref[k, pl.ds(at, half), :] for k in range(2)], axis=1) for at in starts], axis=0
        )

    right = columns_of(0)

    def first(i, carry):
        here = pl.ds(pl.multiple_of(i * half, half), half)
        one = dot_full(jnp.where(core == 0, own_ref[here, :], oth_ref[here, :]), right)
        one_ref[here, :] = one
        for k in range(2):
            out_ref[k, here, :] = one[:, k * width : (k + 1) * width]
        return carry

    lax.fori_loop(0, 2, first, 0)
    right_two = jnp.concatenate([columns_of(1), one_ref[...]], axis=0)

    def second(i, carry):
        here = pl.ds(pl.multiple_of(i * half, half), half)
        there = pl.ds(pl.multiple_of(feats + i * half, half), half)
        left = jnp.where(core == 0, oth_ref[here, :], own_ref[here, :])
        two = dot_full(jnp.concatenate([left, -b_ref[here, :]], axis=1), right_two)
        for k in range(2):
            out_ref[k, there, :] = two[:, k * width : (k + 1) * width]
        return carry

    lax.fori_loop(0, 2, second, 0)


def solve(scalars, own, oth, coupling, crossed):
    count, height, width = crossed.shape
    feats = own.shape[0]
    whole = pl.BlockSpec((feats, feats), lambda k, s: (0, 0))
    pair = pl.BlockSpec((2, height, width), lambda k, s: (k, 0, 0))
    return pl.pallas_call(
        solve_kernel,
        out_shape=jax.ShapeDtypeStruct(crossed.shape, F32),
        grid_spec=pltpu.PrefetchScalarGridSpec(
            num_scalar_prefetch=1,
            grid=(count // 2,),
            in_specs=[whole] * 3 + [pair],
            out_specs=pair,
            scratch_shapes=[pltpu.VMEM((feats, 2 * width), F32)],
        ),
        compiler_params=params(),
        cost_estimate=cost(36 * feats * feats * count * width, 8 * count * height * width),
        name="solve",
    )(scalars, own, oth, coupling, crossed)


def residual_kernel(s_ref, t_ref, ah, al, bh, bl, wa_ref, wb_ref, *rest):
    r_ref, w_ref = rest[-2:]
    own = pl.program_id(0) == 0
    swap, core = jnp.where(own, s_ref[BASE_OWN], s_ref[BASE_OTH]) & 1, s_ref[CORE]
    rows, feats = ah.shape
    half = rows // 2

    def take(step):
        here = pl.ds(pl.multiple_of(step * feats, feats), feats)
        return jnp.concatenate(
            [jnp.where(own, wa_ref[i ^ swap, here, :], wb_ref[i ^ swap, here, :]) for i in range(2)], axis=1
        )

    mine, other = take(core), take(1 - core)
    w_ref[core], w_ref[1 - core] = mine, other
    (mh, ml), (oh, ol) = split(mine), split(other)

    def body(i, carry):
        here = pl.ds(pl.multiple_of(i * half, half), half)
        fitted = dot3((ah[here, :], al[here, :]), (mh, ml)) + dot3((bh[here, :], bl[here, :]), (oh, ol))
        r_ref[here, :] = t_ref[here, :] - fitted
        return carry

    lax.fori_loop(0, 2, body, 0)


def residual_part(group, pair, scalars, targets, mine, other, weights, weights_oth, before):
    rows, columns = targets.shape
    feats = mine[0].shape[1]
    _, height, width = weights.shape
    whole = pl.BlockSpec((rows, feats), lambda k, s: (0, 0))

    def place(k, s):
        return 4 * group + ((jnp.where(k == 0, s[BASE_OWN], s[BASE_OTH]) >> 1) ^ pair)

    block = pl.BlockSpec((rows, 2 * width), lambda k, s: (0, place(k, s)))
    both = pl.BlockSpec((2, height, width), lambda k, s: (0, 0, 0))
    anywhere = pl.BlockSpec(memory_space=pl.ANY)
    return pl.pallas_call(
        residual_kernel,
        out_shape=[
            jax.ShapeDtypeStruct((rows, columns), F32),
            jax.ShapeDtypeStruct((2, feats, columns), F32),
        ],
        grid_spec=pltpu.PrefetchScalarGridSpec(
            num_scalar_prefetch=1,
            grid=(2,),
            in_specs=[block] + [whole] * 4 + [both] * 2 + [anywhere] * len(before),
            out_specs=[block, pl.BlockSpec((2, feats, 2 * width), lambda k, s: (0, 0, place(k, s)))],
        ),
        input_output_aliases={8: 0, 9: 1} if before else {},
        compiler_params=params(),
        cost_estimate=cost(3 * rows * feats * columns, 3 * rows * columns),
        name="residual",
    )(scalars, targets, mine[0], mine[1], other[0], other[1], weights, weights_oth, *before)


def ints(*values):
    return jnp.stack([jnp.asarray(v, jnp.int32) for v in values])


def per_device(count, frames, targets, projection, phases, block_order):
    n_bits = count.bit_length() - 1
    device = lax.axis_index(ALL)
    bit = [(device >> k) & 1 for k in range(n_bits)]
    core = bit[0]
    one = jnp.where(core == 0, bit[1], bit[2])
    two = jnp.where(core == 0, bit[2], bit[1])
    near, far = bit[3], bit[4]
    more = [1 << k for k in range(5, n_bits)]

    def exchange(value, even, odd=None):
        odd = even if odd is None else odd
        pairs = [(i, i ^ (odd if i & 1 else even)) for i in range(count)]
        return lax.ppermute(value, ALL, pairs)

    def flood(value, masks):
        for mask in masks:
            value = value + exchange(value, mask)
        return value

    scalars = ints(
        core * 4 + one * 2 + two,
        (1 - core) * 4 + two * 2 + one,
        core,
        near * 2 + far,
        one * 8 + two * 4 + near * 2 + far,
        two * 8 + one * 4 + near * 2 + far,
        one * 2 + two,
        two * 2 + one,
        device,
    )

    projection_oth, phases_oth = exchange(projection, 1), exchange(phases, 1)
    padded = (projection.shape[1] // 8 + 1) * 8
    blocks = pack(scalars, block_order, projection, projection_oth, phases, phases_oth, padded)
    part = blocks[:2] + exchange(blocks[2:], 2, 4)
    part = part[:1] + exchange(part[1:], 4, 2)
    part = flood(part, [8, 16] + more)
    part = jnp.concatenate([part, exchange(part, 4, 2)])
    blocks = jnp.concatenate([part, exchange(part, 2, 4)])
    blocks_oth = exchange(blocks, 1)
    mine = features(QUARTER_OWN, scalars, frames.T, blocks)
    other = features(QUARTER_OTH, scalars, frames.T, blocks_oth)

    def after(done, sides):
        gated = lax.optimization_barrier([done, *sides[0], *sides[1]])
        return gated[1:5], gated[5:]

    sides = mine, other
    gram_sent = gram(False, scalars, other, mine)
    gram_came = exchange(gram_sent, 1)
    sides = after(gram_sent, sides)
    sent = cross(BASE_OTH, 0, scalars, targets, *sides)
    came = exchange(sent, 1)
    sides = after(sent, sides)
    pieces = gram(True, scalars, *sides) + gram_came
    sides = after(pieces, sides)
    moved = exchange(pieces[8:], 2, 4)
    pieces = pieces[:8] + moved
    kept = [cross(BASE_OWN, 0, scalars, targets, *sides, (came,))]
    sides = after(kept[0], sides)
    sent = cross(BASE_OTH, 1, scalars, targets, *sides)
    came = exchange(sent, 1)
    sides = after(sent, sides)
    kept.append(cross(BASE_OWN, 1, scalars, targets, *sides, (came,)))

    moved = exchange(pieces[4:], 4, 2)
    pieces = pieces[:4] + moved
    pieces, kept[1] = lax.optimization_barrier([pieces, kept[1]])
    moved = exchange(pieces[2:], 8)
    pieces = pieces[:2] + moved
    pieces = pieces[:1] + exchange(pieces[1:], 16)
    pieces = flood(pieces, more)
    for masks in ((16,), (8,), (4, 2), (2, 4)):
        pieces = jnp.concatenate([pieces, exchange(pieces, *masks)])

    crossed = []
    for value in kept:
        moved = exchange(value[2:], 2, 4)
        value = value[:2] + moved
        value = value[:1] + exchange(value[1:], 4, 2)
        for mask in (8, 16):
            middle = value.shape[1] // 2
            value = value[:, :middle] + exchange(value[:, middle:], mask)
        value = flood(value, more)
        for mask in (16, 8):
            value = jnp.concatenate([value, exchange(value, mask)], axis=1)
        crossed.append(jnp.concatenate([value, exchange(value, 4, 2)]))

    matrix, side = assemble(scalars, pieces)
    side_oth = exchange(side, 1)
    for step in (1, 2, 3):
        matrix = factor(step, matrix)
    inverse = matrix
    inverse_oth = exchange(inverse, 1)
    coupling = couple(scalars, inverse, inverse_oth, side, side_oth)
    parts = []
    for value in crossed:
        near_part = solve(scalars, inverse, inverse_oth, coupling, value)
        parts.append((near_part, exchange(near_part, 2, 4)))
    outs = ()
    for pair in range(2):
        for group in range(2):
            value = parts[group][pair]
            value_oth = exchange(value, 1)
            outs = residual_part(group, pair, scalars, targets, mine, other, value, value_oth, tuple(outs))
    return tuple(outs)


def solution(mesh):
    count = math.prod(mesh.shape.values())

    def body(*arrays):
        return per_device(count, *arrays)

    return jax.shard_map(
        body,
        mesh=mesh,
        in_specs=(
            P(ALL, None),
            P(ALL, None),
            P(ALL, None, None),
            P(ALL, None),
            P(),
        ),
        out_specs=(P(ALL, None), P()),
        check_vma=False,
    )
```

```python
import functools
import math

import jax
import jax.numpy as jnp
from jax import lax
from jax.experimental import pallas as pl
from jax.experimental.pallas import tpu as pltpu
from jax.sharding import PartitionSpec as P

ALL = ("wide", "narrow")
F32 = jnp.float32
BF16 = jnp.bfloat16
HIGHEST = lax.Precision.HIGHEST


BASE_OWN, BASE_OTH, CORE, TURN, ORDER_OWN, ORDER_OTH, QUARTER_OWN, QUARTER_OTH, DEVICE = range(9)


def params(mib=24):
    return pltpu.CompilerParams(vmem_limit_bytes=mib * 1024 * 1024)


def cost(flops, nbytes):
    return pl.CostEstimate(flops=int(flops), bytes_accessed=int(nbytes), transcendentals=0)


def split(value):
    high = value.astype(BF16)
    return high, (value - high.astype(F32)).astype(BF16)


def dot_bf16(left, right):
    return jnp.dot(left, right, preferred_element_type=F32)


def dot3(left, right):
    (lh, ll), (rh, rl) = left, right
    return dot_bf16(lh, rh) + (dot_bf16(lh, rl) + dot_bf16(ll, rh))


def dot_full(left, right):
    return jnp.dot(left, right, precision=HIGHEST, preferred_element_type=F32)


TWO_PI = 2.0 * math.pi
PART_A = 6.28125
PART_B = 2.0 ** -24 * round((TWO_PI - PART_A) * 2.0 ** 24 / 2 ** 5) * 2 ** 5
PART_C = TWO_PI - PART_A - PART_B
SIN_POLY = [(-1.0) ** k / math.factorial(2 * k + 1) for k in range(7)]


def cosine(value):
    turns = jnp.floor(value * (1.0 / TWO_PI) + 0.5)
    rest = value - turns * PART_A
    rest = rest - turns * PART_B
    rest = rest - turns * PART_C
    half = rest * 0.5
    square = half * half
    poly = SIN_POLY[-1]
    for coefficient in SIN_POLY[-2::-1]:
        poly = poly * square + coefficient
    sine = half * poly
    return 1.0 - 2.0 * sine * sine


def pack_kernel(s_ref, order_ref, own_ref, oth_ref, pown_ref, poth_ref, out_ref):
    depth = own_ref.shape[1]
    wanted = order_ref[s_ref[CORE]]
    take_own = wanted == s_ref[DEVICE]
    take_oth = wanted == (s_ref[DEVICE] ^ 1)
    value = jnp.where(take_own, own_ref[0], jnp.where(take_oth, oth_ref[0], 0.0))
    phase = jnp.where(take_own, pown_ref[0], jnp.where(take_oth, poth_ref[0], 0.0))
    out_ref[0, :depth, :] = value
    tail = out_ref.shape[1] - depth
    rows = lax.broadcasted_iota(jnp.int32, (tail, out_ref.shape[2]), 0)
    out_ref[0, depth:, :] = jnp.where(rows == 0, jnp.broadcast_to(phase, rows.shape), 0.0)


def pack(scalars, block_order, own, oth, phase_own, phase_oth, padded):
    _, depth, feats = own.shape
    width = feats // 4
    block = pl.BlockSpec((1, depth, width), lambda q, s, o: (0, 0, q ^ s[QUARTER_OWN]))
    phase = pl.BlockSpec((1, 1, width), lambda q, s, o: (0, 0, q ^ s[QUARTER_OWN]))
    return pl.pallas_call(
        pack_kernel,
        out_shape=jax.ShapeDtypeStruct((4, padded, width), F32),
        grid_spec=pltpu.PrefetchScalarGridSpec(
            num_scalar_prefetch=2,
            grid=(4,),
            in_specs=[block, block, phase, phase],
            out_specs=pl.BlockSpec((1, padded, width), lambda q, s, o: (q, 0, 0)),
        ),
        compiler_params=params(),
        name="pack",
    )(scalars, block_order, own, oth, phase_own[:, None, :], phase_oth[:, None, :])


def features_kernel(quarter, s_ref, x_ref, p_ref, fh_ref, fl_ref, th_ref, tl_ref):
    depth = x_ref.shape[0]
    order = s_ref[quarter]
    turned = jnp.concatenate([p_ref[i ^ order] for i in range(4)], axis=1).T
    inner = dot_full(turned[:, :depth], x_ref[...]) + turned[:, depth : depth + 1]
    feats = math.sqrt(2.0 / turned.shape[0]) * cosine(inner)
    th_ref[...], tl_ref[...] = split(feats)
    fh_ref[...], fl_ref[...] = split(feats.T)


def features(quarter, scalars, frames_turned, blocks):
    depth, rows = frames_turned.shape
    feats = blocks.shape[0] * blocks.shape[2]
    tile = 256
    flat = pl.BlockSpec((tile, feats), lambda i, s: (i, 0))
    turned = pl.BlockSpec((feats, tile), lambda i, s: (0, i))
    return pl.pallas_call(
        functools.partial(features_kernel, quarter),
        out_shape=[jax.ShapeDtypeStruct((rows, feats), BF16)] * 2 + [jax.ShapeDtypeStruct((feats, rows), BF16)] * 2,
        grid_spec=pltpu.PrefetchScalarGridSpec(
            num_scalar_prefetch=1,
            grid=(rows // tile,),
            in_specs=[
                pl.BlockSpec((depth, tile), lambda i, s: (0, i)),
                pl.BlockSpec(blocks.shape, lambda i, s: (0, 0, 0)),
            ],
            out_specs=[flat, flat, turned, turned],
        ),
        compiler_params=params(),
        cost_estimate=cost(12 * rows * depth * feats, 4 * rows * depth + 8 * rows * feats),
        name="features",
    )(scalars, frames_turned, blocks)


def gram_kernel(kept, s_ref, mh, ml, mth, mtl, oh, ol, oth, otl, out_ref):
    order = s_ref[ORDER_OWN if kept else ORDER_OTH]
    half_row = s_ref[CORE] if kept else 1 - s_ref[CORE]
    m_is_second = half_row
    feats, _ = mth.shape
    half = feats // 2
    pieces, _, height, _ = out_ref.shape

    def put(tile, value):
        for g in range(pieces):
            out_ref[g ^ order, tile] = value[g * height : (g + 1) * height]

    top = (mth[:half], mtl[:half])
    low = (mth[half:], mtl[half:])
    left = (mh[:, :half], ml[:, :half])
    right = (mh[:, half:], ml[:, half:])
    put(0, dot3(top, left))
    put(1, dot3(low, left))
    put(2, dot3(low, right))

    def cross(th, tl, h, l):
        start = pl.multiple_of(half_row * half, half)
        side = (th[pl.ds(start, half)], tl[pl.ds(start, half)])
        put(3, dot3(side, (h[:, :half], l[:, :half])))
        put(4, dot3(side, (h[:, half:], l[:, half:])))

    @pl.when(m_is_second == 1)
    def _():
        cross(mth, mtl, oh, ol)

    @pl.when(m_is_second == 0)
    def _():
        cross(oth, otl, mh, ml)


def gram(kept, scalars, mine, other):
    rows, feats = mine[0].shape
    return pl.pallas_call(
        functools.partial(gram_kernel, kept),
        out_shape=jax.ShapeDtypeStruct((16, 5, feats // 32, feats // 2), F32),
        in_specs=[pl.BlockSpec(memory_space=pltpu.SMEM)] + [pl.BlockSpec(memory_space=pltpu.VMEM)] * 8,
        out_specs=pl.BlockSpec(memory_space=pltpu.VMEM),
        compiler_params=params(),
        cost_estimate=cost(6 * rows * feats * feats * 1.25, 16 * rows * feats),
        name="gram",
    )(scalars, *mine, *other)


def cross_kernel(base, s_ref, t_ref, ath, atl, bth, btl, *rest):
    out_ref = rest[-1]
    core, turn, swap = s_ref[CORE], s_ref[TURN], s_ref[base] & 1
    half = ath.shape[0] // 2
    width = out_ref.shape[2]
    first = 2 * pl.program_id(0)
    right = split(t_ref[...])

    def rows_of(th, tl, step):
        def body(i, carry):
            at = pl.ds(pl.multiple_of(i * half, half), half)
            value = dot3((th[at, :], tl[at, :]), right)
            to = pl.ds(pl.multiple_of(((2 * step + i) ^ turn) * half, half), half)
            for k in range(2):
                part = value[:, k * width : (k + 1) * width]
                if len(rest) == 2:
                    part = part + rest[0][first + (k ^ swap), to, :]
                out_ref[first + (k ^ swap), to, :] = part
            return carry

        lax.fori_loop(0, 2, body, 0)

    rows_of(ath, atl, core)
    rows_of(bth, btl, 1 - core)


def cross(base, group, scalars, targets, mine, other, before=()):
    rows, columns = targets.shape
    feats = mine[2].shape[0]
    width = columns // 16
    whole = pl.BlockSpec(memory_space=pltpu.VMEM)
    return pl.pallas_call(
        functools.partial(cross_kernel, base),
        out_shape=jax.ShapeDtypeStruct((4, 2 * feats, width), F32),
        grid_spec=pltpu.PrefetchScalarGridSpec(
            num_scalar_prefetch=1,
            grid=(2,),
            in_specs=[pl.BlockSpec((rows, 2 * width), lambda k, s: (0, 4 * group + ((s[base] >> 1) ^ k)))]
            + [whole] * (4 + len(before)),
            out_specs=whole,
        ),
        compiler_params=params(),
        cost_estimate=cost(3 * rows * feats * columns, 2 * rows * columns),
        name="cross",
    )(scalars, targets, mine[2], mine[3], other[2], other[3], *before)


def unit_inverse(block):
    size, lanes = block.shape
    groups = size // 8
    lane = lax.broadcasted_iota(jnp.int32, (8, lanes), 1)
    sub = lax.broadcasted_iota(jnp.int32, (8, lanes), 0)

    def wide(row):
        return jnp.broadcast_to(row, (8, lanes))

    def make(active):
        def turn(i, carry):
            rows, pivots = list(carry[0]), list(carry[1])
            spots = [jnp.full((8, lanes), 8 * i + k, jnp.int32) for k in range(8)]
            here = (lane >= 8 * i) & (lane < 8 * i + 8)
            top = rows[0]
            cols = [jnp.take_along_axis(top, spot, axis=1) for spot in spots]
            x = jnp.where(here, jnp.where(lane - 8 * i == sub, 1.0, 0.0), top)
            diagonal, inverse = top, []
            for j in range(0, 8, 2):
                a, b, c = wide(cols[j][j : j + 1]), wide(cols[j][j + 1 : j + 2]), wide(cols[j + 1][j + 1 : j + 2])
                inv_a = 1.0 / a
                inv_c = a * (1.0 / (a * c - b * b))
                link = b * inv_a
                inverse += [inv_a, inv_c]
                diagonal = jnp.where(sub == j, a, jnp.where(sub == j + 1, c - link * b, diagonal))
                m_a = jnp.where(sub > j, cols[j] * inv_a, 0.0)
                m_b = jnp.where(sub > j + 1, (cols[j + 1] - m_a * b) * inv_c, 0.0)

                def swept(value):
                    one = wide(value[j : j + 1])
                    two = wide(value[j + 1 : j + 2]) - link * one
                    return value - m_a * one - m_b * two

                for k in range(j + 1, 8):
                    cols[k] = swept(cols[k])
                x = swept(x)
            rest, z = x, [None] * 8
            for j in range(7, -1, -1):
                z[j] = wide(rest[j : j + 1]) * inverse[j]
                if j:
                    rest = rest - jnp.where(sub < j, cols[j], 0.0) * z[j]
            for g in range(1, active):
                parts = [jnp.take_along_axis(rows[g], spots[k], axis=1) * z[k] for k in range(8)]
                total = ((parts[0] + parts[1]) + (parts[2] + parts[3])) + ((parts[4] + parts[5]) + (parts[6] + parts[7]))
                rows[g] = jnp.where(g < groups - i, jnp.where(here, 0.0, rows[g]) - total, rows[g])
            return tuple(rows[1:] + [x]), tuple(pivots[1:] + [diagonal])

        return turn

    start = tuple(block[8 * g : 8 * g + 8] for g in range(groups))
    state = (start, start)
    state = lax.fori_loop(0, groups // 2, make(groups), state)
    rows, pivots = lax.fori_loop(groups // 2, groups, make(groups // 2), state)
    scaled = [
        jnp.where(lane <= sub + 8 * g, rows[g] * lax.rsqrt(pivots[g]), 0.0) for g in range(groups)
    ]
    return jnp.concatenate(scaled, axis=0)


def eliminate(m_ref, start, size):
    total = m_ref.shape[0]
    here = slice(start, start + size)
    inverse = unit_inverse(m_ref[here, here])
    if start:
        m_ref[here, :start] = dot_full(inverse, m_ref[here, :start])
    if start + size < total:
        below = slice(start + size, total)
        panel = lax.dot_general(
            m_ref[below, here], inverse, (((1,), (1,)), ((), ())), precision=HIGHEST, preferred_element_type=F32
        )
        m_ref[here, below] = dot_full(inverse, m_ref[here, below])
        m_ref[below, here] = jnp.zeros((total - start - size, size), F32)
        m_ref[here, here] = inverse
        m_ref[below, :] = m_ref[below, :] - dot_full(panel, m_ref[here, :])
    else:
        m_ref[here, here] = inverse


def assemble_kernel(s_ref, g_ref, a_ref, side_ref):
    order = s_ref[ORDER_OWN]
    pieces, _, height, half = g_ref.shape
    for g in range(pieces):
        piece = g_ref[g ^ order]
        here = slice(g * height, (g + 1) * height)
        there = slice(half + g * height, half + (g + 1) * height)
        a_ref[here, :half] = piece[0]
        a_ref[there, :half] = piece[1]
        a_ref[there, half:] = piece[2]
        side_ref[here, :half] = piece[3]
        side_ref[here, half:] = piece[4]
    a_ref[:half, half:] = a_ref[half:, :half].T
    whole = a_ref[...]
    eye = lax.broadcasted_iota(jnp.int32, whole.shape, 0) == lax.broadcasted_iota(jnp.int32, whole.shape, 1)
    diagonal = jnp.where(eye, whole, 0.0)
    damping = 0.1 * jnp.sum(diagonal) / whole.shape[0]
    a_ref[...] = whole + jnp.where(eye, damping, 0.0)
    eliminate(a_ref, 0, whole.shape[0] // 4)


def assemble(order, pieces):
    half = pieces.shape[3]
    return pl.pallas_call(
        assemble_kernel,
        out_shape=[jax.ShapeDtypeStruct((2 * half, 2 * half), F32), jax.ShapeDtypeStruct((half, 2 * half), F32)],
        in_specs=[pl.BlockSpec(memory_space=pltpu.SMEM), pl.BlockSpec(memory_space=pltpu.VMEM)],
        out_specs=[pl.BlockSpec(memory_space=pltpu.VMEM)] * 2,
        compiler_params=params(),
        cost_estimate=cost(1e10, 4e6),
        name="assemble",
    )(order, pieces)


def factor_kernel(step, m_ref, out_ref):
    out_ref[...] = m_ref[...]
    eliminate(out_ref, step * (m_ref.shape[0] // 4), m_ref.shape[0] // 4)
    if step == 3:
        whole = out_ref[...]
        low = lax.broadcasted_iota(jnp.int32, whole.shape, 0) >= lax.broadcasted_iota(jnp.int32, whole.shape, 1)
        whole = jnp.where(low, whole, 0.0)
        out_ref[...] = dot_full(whole.T, whole)


def factor(step, matrix):
    return pl.pallas_call(
        functools.partial(factor_kernel, step),
        out_shape=jax.ShapeDtypeStruct(matrix.shape, F32),
        in_specs=[pl.BlockSpec(memory_space=pltpu.VMEM)],
        out_specs=pl.BlockSpec(memory_space=pltpu.VMEM),
        compiler_params=params(),
        cost_estimate=cost(1e10, 4e6),
        name="factor",
    )(matrix)


def couple_kernel(s_ref, own_ref, oth_ref, gown_ref, goth_ref, out_ref):
    core = s_ref[CORE]
    half = gown_ref.shape[0]
    second = jnp.where(core == 1, own_ref[...], oth_ref[...])
    top = jnp.where(core == 0, gown_ref[...], goth_ref[...])
    low = jnp.where(core == 0, goth_ref[...], gown_ref[...])
    out_ref[...] = dot_full(second[:, :half], top) + dot_full(second[:, half:], low)


def couple(core, own, oth, side_own, side_oth):
    return pl.pallas_call(
        couple_kernel,
        out_shape=jax.ShapeDtypeStruct(own.shape, F32),
        in_specs=[pl.BlockSpec(memory_space=pltpu.SMEM)] + [pl.BlockSpec(memory_space=pltpu.VMEM)] * 4,
        compiler_params=params(),
        name="couple",
    )(core, own, oth, side_own, side_oth)


def solve_kernel(s_ref, own_ref, oth_ref, b_ref, c_ref, out_ref, one_ref):
    core, turn = s_ref[CORE], s_ref[TURN]
    feats = own_ref.shape[0]
    half = feats // 2
    width = c_ref.shape[2]

    def columns_of(step):
        starts = [pl.multiple_of(((2 * step + i) ^ turn) * half, half) for i in range(2)]
        return jnp.concatenate(
            [jnp.concatenate([c_ref[k, pl.ds(at, half), :] for k in range(2)], axis=1) for at in starts], axis=0
        )

    right = columns_of(0)

    def first(i, carry):
        here = pl.ds(pl.multiple_of(i * half, half), half)
        one = dot_full(jnp.where(core == 0, own_ref[here, :], oth_ref[here, :]), right)
        one_ref[here, :] = one
        for k in range(2):
            out_ref[k, here, :] = one[:, k * width : (k + 1) * width]
        return carry

    lax.fori_loop(0, 2, first, 0)
    right_two = jnp.concatenate([columns_of(1), one_ref[...]], axis=0)

    def second(i, carry):
        here = pl.ds(pl.multiple_of(i * half, half), half)
        there = pl.ds(pl.multiple_of(feats + i * half, half), half)
        left = jnp.where(core == 0, oth_ref[here, :], own_ref[here, :])
        two = dot_full(jnp.concatenate([left, -b_ref[here, :]], axis=1), right_two)
        for k in range(2):
            out_ref[k, there, :] = two[:, k * width : (k + 1) * width]
        return carry

    lax.fori_loop(0, 2, second, 0)


def solve(scalars, own, oth, coupling, crossed):
    count, height, width = crossed.shape
    feats = own.shape[0]
    whole = pl.BlockSpec((feats, feats), lambda k, s: (0, 0))
    pair = pl.BlockSpec((2, height, width), lambda k, s: (k, 0, 0))
    return pl.pallas_call(
        solve_kernel,
        out_shape=jax.ShapeDtypeStruct(crossed.shape, F32),
        grid_spec=pltpu.PrefetchScalarGridSpec(
            num_scalar_prefetch=1,
            grid=(count // 2,),
            in_specs=[whole] * 3 + [pair],
            out_specs=pair,
            scratch_shapes=[pltpu.VMEM((feats, 2 * width), F32)],
        ),
        compiler_params=params(),
        cost_estimate=cost(36 * feats * feats * count * width, 8 * count * height * width),
        name="solve",
    )(scalars, own, oth, coupling, crossed)


def residual_kernel(s_ref, t_ref, ah, al, bh, bl, wa_ref, wb_ref, *rest):
    r_ref, w_ref = rest[-2:]
    own = pl.program_id(0) == 0
    half = t_ref.shape[0]
    swap, core = jnp.where(own, s_ref[BASE_OWN], s_ref[BASE_OTH]) & 1, s_ref[CORE]
    feats = ah.shape[1]

    def take(step):
        here = pl.ds(pl.multiple_of(step * feats, feats), feats)
        return jnp.concatenate(
            [jnp.where(own, wa_ref[i ^ swap, here, :], wb_ref[i ^ swap, here, :]) for i in range(2)], axis=1
        )

    mine, other = take(core), take(1 - core)
    w_ref[core], w_ref[1 - core] = mine, other
    here = pl.ds(pl.multiple_of(pl.program_id(1) * half, half), half)
    fitted = dot3((ah[here, :], al[here, :]), split(mine)) + dot3((bh[here, :], bl[here, :]), split(other))
    r_ref[...] = t_ref[...] - fitted


def residual_part(group, pair, scalars, targets, mine, other, weights, weights_oth, before):
    rows, columns = targets.shape
    feats = mine[0].shape[1]
    _, _, width = weights.shape
    whole = pl.BlockSpec(memory_space=pltpu.VMEM)

    def place(k, s):
        return 4 * group + ((jnp.where(k == 0, s[BASE_OWN], s[BASE_OTH]) >> 1) ^ pair)

    block = pl.BlockSpec((rows // 2, 2 * width), lambda k, i, s: (i, place(k, s)))
    anywhere = pl.BlockSpec(memory_space=pl.ANY)
    return pl.pallas_call(
        residual_kernel,
        out_shape=[
            jax.ShapeDtypeStruct((rows, columns), F32),
            jax.ShapeDtypeStruct((2, feats, columns), F32),
        ],
        grid_spec=pltpu.PrefetchScalarGridSpec(
            num_scalar_prefetch=1,
            grid=(2, 2),
            in_specs=[block] + [whole] * 6 + [anywhere] * len(before),
            out_specs=[block, pl.BlockSpec((2, feats, 2 * width), lambda k, i, s: (0, 0, place(k, s)))],
        ),
        input_output_aliases={8: 0, 9: 1} if before else {},
        compiler_params=params(),
        cost_estimate=cost(3 * rows * feats * columns, 3 * rows * columns),
        name="residual",
    )(scalars, targets, mine[0], mine[1], other[0], other[1], weights, weights_oth, *before)


def ints(*values):
    return jnp.stack([jnp.asarray(v, jnp.int32) for v in values])


def per_device(count, frames, targets, projection, phases, block_order):
    n_bits = count.bit_length() - 1
    device = lax.axis_index(ALL)
    bit = [(device >> k) & 1 for k in range(n_bits)]
    core = bit[0]
    one = jnp.where(core == 0, bit[1], bit[2])
    two = jnp.where(core == 0, bit[2], bit[1])
    near, far = bit[3], bit[4]
    more = [1 << k for k in range(5, n_bits)]

    def exchange(value, even, odd=None):
        odd = even if odd is None else odd
        pairs = [(i, i ^ (odd if i & 1 else even)) for i in range(count)]
        return lax.ppermute(value, ALL, pairs)

    def flood(value, masks):
        for mask in masks:
            value = value + exchange(value, mask)
        return value

    scalars = ints(
        core * 4 + one * 2 + two,
        (1 - core) * 4 + two * 2 + one,
        core,
        near * 2 + far,
        one * 8 + two * 4 + near * 2 + far,
        two * 8 + one * 4 + near * 2 + far,
        one * 2 + two,
        two * 2 + one,
        device,
    )

    projection_oth, phases_oth = exchange(projection, 1), exchange(phases, 1)
    padded = (projection.shape[1] // 8 + 1) * 8
    blocks = pack(scalars, block_order, projection, projection_oth, phases, phases_oth, padded)
    part = blocks[:2] + exchange(blocks[2:], 2, 4)
    part = part[:1] + exchange(part[1:], 4, 2)
    part = flood(part, [8, 16] + more)
    part = jnp.concatenate([part, exchange(part, 4, 2)])
    blocks = jnp.concatenate([part, exchange(part, 2, 4)])
    blocks_oth = exchange(blocks, 1)
    mine = features(QUARTER_OWN, scalars, frames.T, blocks)
    other = features(QUARTER_OTH, scalars, frames.T, blocks_oth)

    def after(done, sides):
        gated = lax.optimization_barrier([done, *sides[0], *sides[1]])
        return gated[1:5], gated[5:]

    sides = mine, other
    gram_sent = gram(False, scalars, other, mine)
    gram_came = exchange(gram_sent, 1)
    sides = after(gram_sent, sides)
    sent = cross(BASE_OTH, 0, scalars, targets, *sides)
    came = exchange(sent, 1)
    sides = after(sent, sides)
    pieces = gram(True, scalars, *sides) + gram_came
    sides = after(pieces, sides)
    moved = exchange(pieces[8:], 2, 4)
    pieces = pieces[:8] + moved
    kept = [cross(BASE_OWN, 0, scalars, targets, *sides, (came,))]
    sides = after(kept[0], sides)
    sent = cross(BASE_OTH, 1, scalars, targets, *sides)
    came = exchange(sent, 1)
    sides = after(sent, sides)
    kept.append(cross(BASE_OWN, 1, scalars, targets, *sides, (came,)))

    pieces = pieces[:4] + exchange(pieces[4:], 4, 2)
    pieces, kept[1] = lax.optimization_barrier([pieces, kept[1]])
    pieces = pieces[:2] + exchange(pieces[2:], 8)
    pieces = pieces[:1] + exchange(pieces[1:], 16)
    pieces = flood(pieces, more)
    for masks in ((16,), (8,), (4, 2), (2, 4)):
        pieces = jnp.concatenate([pieces, exchange(pieces, *masks)])

    crossed = []
    for value in kept:
        value = value[:2] + exchange(value[2:], 2, 4)
        value = value[:1] + exchange(value[1:], 4, 2)
        for mask in (8, 16):
            middle = value.shape[1] // 2
            value = value[:, :middle] + exchange(value[:, middle:], mask)
        value = flood(value, more)
        for mask in (16, 8):
            value = jnp.concatenate([value, exchange(value, mask)], axis=1)
        crossed.append(jnp.concatenate([value, exchange(value, 4, 2)]))

    matrix, side = assemble(scalars, pieces)
    side_oth = exchange(side, 1)
    for step in (1, 2, 3):
        matrix = factor(step, matrix)
    inverse = matrix
    inverse_oth = exchange(inverse, 1)
    coupling = couple(scalars, inverse, inverse_oth, side, side_oth)
    parts = []
    for value in crossed:
        near_part = solve(scalars, inverse, inverse_oth, coupling, value)
        parts.append((near_part, exchange(near_part, 2, 4)))
    outs = ()
    for pair in range(2):
        for group in range(2):
            value = parts[group][pair]
            value_oth = exchange(value, 1)
            outs = residual_part(group, pair, scalars, targets, mine, other, value, value_oth, tuple(outs))
    return tuple(outs)


def solution(mesh):
    count = math.prod(mesh.shape.values())

    def body(*arrays):
        return per_device(count, *arrays)

    return jax.shard_map(
        body,
        mesh=mesh,
        in_specs=(
            P(ALL, None),
            P(ALL, None),
            P(ALL, None, None),
            P(ALL, None),
            P(),
        ),
        out_specs=(P(ALL, None), P()),
        check_vma=False,
    )
```

```python
import functools
import math

import jax
import jax.numpy as jnp
from jax import lax
from jax.experimental import pallas as pl
from jax.experimental.pallas import tpu as pltpu
from jax.sharding import PartitionSpec as P

ALL = ("wide", "narrow")
F32 = jnp.float32
BF16 = jnp.bfloat16
HIGHEST = lax.Precision.HIGHEST


BASE_OWN, BASE_OTH, CORE, TURN, ORDER_OWN, ORDER_OTH, QUARTER_OWN, QUARTER_OTH, DEVICE = range(9)


def params(mib=24):
    return pltpu.CompilerParams(vmem_limit_bytes=mib * 1024 * 1024)


def cost(flops, nbytes):
    return pl.CostEstimate(flops=int(flops), bytes_accessed=int(nbytes), transcendentals=0)


def split(value):
    high = value.astype(BF16)
    return high, (value - high.astype(F32)).astype(BF16)


def dot_bf16(left, right):
    return jnp.dot(left, right, preferred_element_type=F32)


def dot3(left, right):
    (lh, ll), (rh, rl) = left, right
    return dot_bf16(lh, rh) + (dot_bf16(lh, rl) + dot_bf16(ll, rh))


def dot_full(left, right):
    return jnp.dot(left, right, precision=HIGHEST, preferred_element_type=F32)


TWO_PI = 2.0 * math.pi
PART_A = 6.28125
PART_B = 2.0 ** -24 * round((TWO_PI - PART_A) * 2.0 ** 24 / 2 ** 5) * 2 ** 5
PART_C = TWO_PI - PART_A - PART_B
SIN_POLY = [(-1.0) ** k / math.factorial(2 * k + 1) for k in range(7)]


def cosine(value):
    turns = jnp.floor(value * (1.0 / TWO_PI) + 0.5)
    rest = value - turns * PART_A
    rest = rest - turns * PART_B
    rest = rest - turns * PART_C
    half = rest * 0.5
    square = half * half
    poly = SIN_POLY[-1]
    for coefficient in SIN_POLY[-2::-1]:
        poly = poly * square + coefficient
    sine = half * poly
    return 1.0 - 2.0 * sine * sine


def pack_kernel(s_ref, order_ref, own_ref, oth_ref, pown_ref, poth_ref, out_ref):
    depth = own_ref.shape[1]
    wanted = order_ref[s_ref[CORE]]
    take_own = wanted == s_ref[DEVICE]
    take_oth = wanted == (s_ref[DEVICE] ^ 1)
    value = jnp.where(take_own, own_ref[0], jnp.where(take_oth, oth_ref[0], 0.0))
    phase = jnp.where(take_own, pown_ref[0], jnp.where(take_oth, poth_ref[0], 0.0))
    out_ref[0, :depth, :] = value
    tail = out_ref.shape[1] - depth
    rows = lax.broadcasted_iota(jnp.int32, (tail, out_ref.shape[2]), 0)
    out_ref[0, depth:, :] = jnp.where(rows == 0, jnp.broadcast_to(phase, rows.shape), 0.0)


def pack(scalars, block_order, own, oth, phase_own, phase_oth, padded):
    _, depth, feats = own.shape
    width = feats // 4
    block = pl.BlockSpec((1, depth, width), lambda q, s, o: (0, 0, q ^ s[QUARTER_OWN]))
    phase = pl.BlockSpec((1, 1, width), lambda q, s, o: (0, 0, q ^ s[QUARTER_OWN]))
    return pl.pallas_call(
        pack_kernel,
        out_shape=jax.ShapeDtypeStruct((4, padded, width), F32),
        grid_spec=pltpu.PrefetchScalarGridSpec(
            num_scalar_prefetch=2,
            grid=(4,),
            in_specs=[block, block, phase, phase],
            out_specs=pl.BlockSpec((1, padded, width), lambda q, s, o: (q, 0, 0)),
        ),
        compiler_params=params(),
        name="pack",
    )(scalars, block_order, own, oth, phase_own[:, None, :], phase_oth[:, None, :])


def features_kernel(quarter, s_ref, x_ref, p_ref, *rest):
    fh_ref, fl_ref, th_ref, tl_ref = rest[-4:]
    depth = x_ref.shape[0]
    order = s_ref[quarter]
    turned = jnp.concatenate([p_ref[i ^ order] for i in range(4)], axis=1).T
    inner = dot_full(turned[:, :depth], x_ref[...]) + turned[:, depth : depth + 1]
    feats = math.sqrt(2.0 / turned.shape[0]) * cosine(inner)
    th_ref[...], tl_ref[...] = split(feats)
    fh_ref[...], fl_ref[...] = split(feats.T)


def features(quarter, slot, scalars, frames_turned, blocks, before=()):
    depth, rows = frames_turned.shape
    feats = blocks.shape[0] * blocks.shape[2]
    tile = 256
    flat = pl.BlockSpec((tile, feats), lambda i, s: (i, 0))
    turned = pl.BlockSpec((feats, tile), lambda i, s: (slot, i))
    return pl.pallas_call(
        functools.partial(features_kernel, quarter),
        out_shape=[jax.ShapeDtypeStruct((rows, feats), BF16)] * 2 + [jax.ShapeDtypeStruct((2 * feats, rows), BF16)] * 2,
        grid_spec=pltpu.PrefetchScalarGridSpec(
            num_scalar_prefetch=1,
            grid=(rows // tile,),
            in_specs=[
                pl.BlockSpec((depth, tile), lambda i, s: (0, i)),
                pl.BlockSpec(blocks.shape, lambda i, s: (0, 0, 0)),
            ]
            + [pl.BlockSpec(memory_space=pl.ANY)] * len(before),
            out_specs=[flat, flat, turned, turned],
        ),
        input_output_aliases={3: 2, 4: 3} if before else {},
        compiler_params=params(),
        cost_estimate=cost(12 * rows * depth * feats, 4 * rows * depth + 8 * rows * feats),
        name="features",
    )(scalars, frames_turned, blocks, *before)


def gram_kernel(kept, s_ref, ah, al, bh, bl, th, tl, out_ref):
    order = s_ref[ORDER_OWN if kept else ORDER_OTH]
    half_row = s_ref[CORE] if kept else 1 - s_ref[CORE]
    m_is_second = half_row
    feats = th.shape[0] // 2
    mh, ml, oh, ol = (ah, al, bh, bl) if kept else (bh, bl, ah, al)
    m_at, o_at = (0, feats) if kept else (feats, 0)
    half = feats // 2
    pieces, _, height, _ = out_ref.shape

    def put(tile, value):
        for g in range(pieces):
            out_ref[g ^ order, tile] = value[g * height : (g + 1) * height]

    top = tuple(r[m_at : m_at + half] for r in (th, tl))
    low = tuple(r[m_at + half : m_at + feats] for r in (th, tl))
    left = (mh[:, :half], ml[:, :half])
    right = (mh[:, half:], ml[:, half:])
    put(0, dot3(top, left))
    put(1, dot3(low, left))
    put(2, dot3(low, right))

    def cross(at, h, l):
        start = pl.multiple_of(at + half_row * half, half)
        side = (th[pl.ds(start, half)], tl[pl.ds(start, half)])
        put(3, dot3(side, (h[:, :half], l[:, :half])))
        put(4, dot3(side, (h[:, half:], l[:, half:])))

    @pl.when(m_is_second == 1)
    def _():
        cross(m_at, oh, ol)

    @pl.when(m_is_second == 0)
    def _():
        cross(o_at, mh, ml)


def gram(kept, scalars, flat, turned):
    rows, feats = flat[0].shape
    return pl.pallas_call(
        functools.partial(gram_kernel, kept),
        out_shape=jax.ShapeDtypeStruct((16, 5, feats // 32, feats // 2), F32),
        in_specs=[pl.BlockSpec(memory_space=pltpu.SMEM)] + [pl.BlockSpec(memory_space=pltpu.VMEM)] * 6,
        out_specs=pl.BlockSpec(memory_space=pltpu.VMEM),
        compiler_params=params(),
        cost_estimate=cost(6 * rows * feats * feats * 1.25, 16 * rows * feats),
        name="gram",
    )(scalars, *flat, *turned)


def cross_kernel(base, s_ref, t_ref, th, tl, *rest):
    out_ref = rest[-1]
    core, turn, swap = s_ref[CORE], s_ref[TURN], s_ref[base] & 1
    feats = th.shape[0] // 2
    half = feats // 2
    width = out_ref.shape[2]
    first = 2 * pl.program_id(0)
    right = split(t_ref[...])

    def body(slot, carry):
        at = pl.ds(pl.multiple_of(slot * feats, feats), feats)
        value = dot3((th[at, :], tl[at, :]), right)
        for i in range(2):
            to = pl.ds(pl.multiple_of(((2 * (core ^ slot) + i) ^ turn) * half, half), half)
            for k in range(2):
                part = value[i * half : (i + 1) * half, k * width : (k + 1) * width]
                if len(rest) == 2:
                    part = part + rest[0][first + (k ^ swap), to, :]
                out_ref[first + (k ^ swap), to, :] = part
        return carry

    lax.fori_loop(0, 2, body, 0)


def cross(base, group, scalars, targets, turned, before=()):
    rows, columns = targets.shape
    feats = turned[0].shape[0] // 2
    width = columns // 16
    whole = pl.BlockSpec(memory_space=pltpu.VMEM)
    return pl.pallas_call(
        functools.partial(cross_kernel, base),
        out_shape=jax.ShapeDtypeStruct((4, 2 * feats, width), F32),
        grid_spec=pltpu.PrefetchScalarGridSpec(
            num_scalar_prefetch=1,
            grid=(2,),
            in_specs=[pl.BlockSpec((rows, 2 * width), lambda k, s: (0, 4 * group + ((s[base] >> 1) ^ k)))]
            + [whole] * (2 + len(before)),
            out_specs=whole,
        ),
        compiler_params=params(),
        cost_estimate=cost(3 * rows * feats * columns, 2 * rows * columns),
        name="cross",
    )(scalars, targets, *turned, *before)


def unit_inverse(block):
    size, lanes = block.shape
    groups = size // 8
    lane = lax.broadcasted_iota(jnp.int32, (8, lanes), 1)
    sub = lax.broadcasted_iota(jnp.int32, (8, lanes), 0)

    def wide(row):
        return jnp.broadcast_to(row, (8, lanes))

    def make(active):
        def turn(i, carry):
            rows, pivots = list(carry[0]), list(carry[1])
            spots = [jnp.full((8, lanes), 8 * i + k, jnp.int32) for k in range(8)]
            here = (lane >= 8 * i) & (lane < 8 * i + 8)
            top = rows[0]
            cols = [jnp.take_along_axis(top, spot, axis=1) for spot in spots]
            x = jnp.where(here, jnp.where(lane - 8 * i == sub, 1.0, 0.0), top)
            diagonal, inverse = top, []
            for j in range(0, 8, 2):
                a, b, c = wide(cols[j][j : j + 1]), wide(cols[j][j + 1 : j + 2]), wide(cols[j + 1][j + 1 : j + 2])
                inv_a = 1.0 / a
                inv_c = a * (1.0 / (a * c - b * b))
                link = b * inv_a
                inverse += [inv_a, inv_c]
                diagonal = jnp.where(sub == j, a, jnp.where(sub == j + 1, c - link * b, diagonal))
                m_a = jnp.where(sub > j, cols[j] * inv_a, 0.0)
                m_b = jnp.where(sub > j + 1, (cols[j + 1] - m_a * b) * inv_c, 0.0)

                def swept(value):
                    one = wide(value[j : j + 1])
                    two = wide(value[j + 1 : j + 2]) - link * one
                    return value - m_a * one - m_b * two

                for k in range(j + 1, 8):
                    cols[k] = swept(cols[k])
                x = swept(x)
            rest, z = x, [None] * 8
            for j in range(7, -1, -1):
                z[j] = wide(rest[j : j + 1]) * inverse[j]
                if j:
                    rest = rest - jnp.where(sub < j, cols[j], 0.0) * z[j]
            for g in range(1, active):
                parts = [jnp.take_along_axis(rows[g], spots[k], axis=1) * z[k] for k in range(8)]
                total = ((parts[0] + parts[1]) + (parts[2] + parts[3])) + ((parts[4] + parts[5]) + (parts[6] + parts[7]))
                rows[g] = jnp.where(g < groups - i, jnp.where(here, 0.0, rows[g]) - total, rows[g])
            return tuple(rows[1:] + [x]), tuple(pivots[1:] + [diagonal])

        return turn

    start = tuple(block[8 * g : 8 * g + 8] for g in range(groups))
    state = (start, start)
    state = lax.fori_loop(0, groups // 2, make(groups), state)
    rows, pivots = lax.fori_loop(groups // 2, groups, make(groups // 2), state)
    scaled = [
        jnp.where(lane <= sub + 8 * g, rows[g] * lax.rsqrt(pivots[g]), 0.0) for g in range(groups)
    ]
    return jnp.concatenate(scaled, axis=0)


def eliminate(m_ref, start, size):
    total = m_ref.shape[0]
    here = slice(start, start + size)
    inverse = unit_inverse(m_ref[here, here])
    if start:
        m_ref[here, :start] = dot_full(inverse, m_ref[here, :start])
    if start + size < total:
        below = slice(start + size, total)
        panel = lax.dot_general(
            m_ref[below, here], inverse, (((1,), (1,)), ((), ())), precision=HIGHEST, preferred_element_type=F32
        )
        m_ref[here, below] = dot_full(inverse, m_ref[here, below])
        m_ref[below, here] = jnp.zeros((total - start - size, size), F32)
        m_ref[here, here] = inverse
        m_ref[below, :] = m_ref[below, :] - dot_full(panel, m_ref[here, :])
    else:
        m_ref[here, here] = inverse


def assemble_kernel(s_ref, g_ref, a_ref, side_ref):
    order = s_ref[ORDER_OWN]
    pieces, _, height, half = g_ref.shape
    for g in range(pieces):
        piece = g_ref[g ^ order]
        here = slice(g * height, (g + 1) * height)
        there = slice(half + g * height, half + (g + 1) * height)
        a_ref[here, :half] = piece[0]
        a_ref[there, :half] = piece[1]
        a_ref[there, half:] = piece[2]
        side_ref[here, :half] = piece[3]
        side_ref[here, half:] = piece[4]
    a_ref[:half, half:] = a_ref[half:, :half].T
    whole = a_ref[...]
    eye = lax.broadcasted_iota(jnp.int32, whole.shape, 0) == lax.broadcasted_iota(jnp.int32, whole.shape, 1)
    diagonal = jnp.where(eye, whole, 0.0)
    damping = 0.1 * jnp.sum(diagonal) / whole.shape[0]
    a_ref[...] = whole + jnp.where(eye, damping, 0.0)
    eliminate(a_ref, 0, whole.shape[0] // 4)


def assemble(order, pieces):
    half = pieces.shape[3]
    return pl.pallas_call(
        assemble_kernel,
        out_shape=[jax.ShapeDtypeStruct((2 * half, 2 * half), F32), jax.ShapeDtypeStruct((half, 2 * half), F32)],
        in_specs=[pl.BlockSpec(memory_space=pltpu.SMEM), pl.BlockSpec(memory_space=pltpu.VMEM)],
        out_specs=[pl.BlockSpec(memory_space=pltpu.VMEM)] * 2,
        compiler_params=params(),
        cost_estimate=cost(1e10, 4e6),
        name="assemble",
    )(order, pieces)


def factor_kernel(step, m_ref, out_ref):
    out_ref[...] = m_ref[...]
    eliminate(out_ref, step * (m_ref.shape[0] // 4), m_ref.shape[0] // 4)
    if step == 3:
        whole = out_ref[...]
        low = lax.broadcasted_iota(jnp.int32, whole.shape, 0) >= lax.broadcasted_iota(jnp.int32, whole.shape, 1)
        whole = jnp.where(low, whole, 0.0)
        out_ref[...] = dot_full(whole.T, whole)


def factor(step, matrix):
    return pl.pallas_call(
        functools.partial(factor_kernel, step),
        out_shape=jax.ShapeDtypeStruct(matrix.shape, F32),
        in_specs=[pl.BlockSpec(memory_space=pltpu.VMEM)],
        out_specs=pl.BlockSpec(memory_space=pltpu.VMEM),
        compiler_params=params(),
        cost_estimate=cost(1e10, 4e6),
        name="factor",
    )(matrix)


def couple_kernel(s_ref, own_ref, oth_ref, gown_ref, goth_ref, out_ref):
    core = s_ref[CORE]
    half = gown_ref.shape[0]
    second = jnp.where(core == 1, own_ref[...], oth_ref[...])
    top = jnp.where(core == 0, gown_ref[...], goth_ref[...])
    low = jnp.where(core == 0, goth_ref[...], gown_ref[...])
    out_ref[...] = dot_full(second[:, :half], top) + dot_full(second[:, half:], low)


def couple(core, own, oth, side_own, side_oth):
    return pl.pallas_call(
        couple_kernel,
        out_shape=jax.ShapeDtypeStruct(own.shape, F32),
        in_specs=[pl.BlockSpec(memory_space=pltpu.SMEM)] + [pl.BlockSpec(memory_space=pltpu.VMEM)] * 4,
        compiler_params=params(),
        name="couple",
    )(core, own, oth, side_own, side_oth)


def solve_kernel(s_ref, own_ref, oth_ref, b_ref, c_ref, out_ref, one_ref):
    core, turn = s_ref[CORE], s_ref[TURN]
    feats = own_ref.shape[0]
    half = feats // 2
    width = c_ref.shape[2]

    def columns_of(step):
        starts = [pl.multiple_of(((2 * step + i) ^ turn) * half, half) for i in range(2)]
        return jnp.concatenate(
            [jnp.concatenate([c_ref[k, pl.ds(at, half), :] for k in range(2)], axis=1) for at in starts], axis=0
        )

    right = columns_of(0)

    def first(i, carry):
        here = pl.ds(pl.multiple_of(i * half, half), half)
        one = dot_full(jnp.where(core == 0, own_ref[here, :], oth_ref[here, :]), right)
        one_ref[here, :] = one
        for k in range(2):
            out_ref[k, here, :] = one[:, k * width : (k + 1) * width]
        return carry

    lax.fori_loop(0, 2, first, 0)
    right_two = jnp.concatenate([columns_of(1), one_ref[...]], axis=0)

    def second(i, carry):
        here = pl.ds(pl.multiple_of(i * half, half), half)
        there = pl.ds(pl.multiple_of(feats + i * half, half), half)
        left = jnp.where(core == 0, oth_ref[here, :], own_ref[here, :])
        two = dot_full(jnp.concatenate([left, -b_ref[here, :]], axis=1), right_two)
        for k in range(2):
            out_ref[k, there, :] = two[:, k * width : (k + 1) * width]
        return carry

    lax.fori_loop(0, 2, second, 0)


def solve(scalars, own, oth, coupling, crossed):
    count, height, width = crossed.shape
    feats = own.shape[0]
    whole = pl.BlockSpec((feats, feats), lambda k, s: (0, 0))
    pair = pl.BlockSpec((2, height, width), lambda k, s: (k, 0, 0))
    return pl.pallas_call(
        solve_kernel,
        out_shape=jax.ShapeDtypeStruct(crossed.shape, F32),
        grid_spec=pltpu.PrefetchScalarGridSpec(
            num_scalar_prefetch=1,
            grid=(count // 2,),
            in_specs=[whole] * 3 + [pair],
            out_specs=pair,
            scratch_shapes=[pltpu.VMEM((feats, 2 * width), F32)],
        ),
        compiler_params=params(),
        cost_estimate=cost(36 * feats * feats * count * width, 8 * count * height * width),
        name="solve",
    )(scalars, own, oth, coupling, crossed)


def residual_kernel(s_ref, t_ref, ah, al, bh, bl, wa_ref, wb_ref, *rest):
    r_ref, w_ref = rest[-2:]
    own = pl.program_id(0) == 0
    half = t_ref.shape[0]
    swap, core = jnp.where(own, s_ref[BASE_OWN], s_ref[BASE_OTH]) & 1, s_ref[CORE]
    feats = ah.shape[1]

    def take(step):
        here = pl.ds(pl.multiple_of(step * feats, feats), feats)
        return jnp.concatenate(
            [jnp.where(own, wa_ref[i ^ swap, here, :], wb_ref[i ^ swap, here, :]) for i in range(2)], axis=1
        )

    mine, other = take(core), take(1 - core)
    w_ref[core], w_ref[1 - core] = mine, other
    here = pl.ds(pl.multiple_of(pl.program_id(1) * half, half), half)
    fitted = dot3((ah[here, :], al[here, :]), split(mine)) + dot3((bh[here, :], bl[here, :]), split(other))
    r_ref[...] = t_ref[...] - fitted


def residual_part(group, pair, scalars, targets, mine, other, weights, weights_oth, before):
    rows, columns = targets.shape
    feats = mine[0].shape[1]
    _, _, width = weights.shape
    whole = pl.BlockSpec(memory_space=pltpu.VMEM)

    def place(k, s):
        return 4 * group + ((jnp.where(k == 0, s[BASE_OWN], s[BASE_OTH]) >> 1) ^ pair)

    block = pl.BlockSpec((rows // 2, 2 * width), lambda k, i, s: (i, place(k, s)))
    anywhere = pl.BlockSpec(memory_space=pl.ANY)
    return pl.pallas_call(
        residual_kernel,
        out_shape=[
            jax.ShapeDtypeStruct((rows, columns), F32),
            jax.ShapeDtypeStruct((2, feats, columns), F32),
        ],
        grid_spec=pltpu.PrefetchScalarGridSpec(
            num_scalar_prefetch=1,
            grid=(2, 2),
            in_specs=[block] + [whole] * 6 + [anywhere] * len(before),
            out_specs=[block, pl.BlockSpec((2, feats, 2 * width), lambda k, i, s: (0, 0, place(k, s)))],
        ),
        input_output_aliases={8: 0, 9: 1} if before else {},
        compiler_params=params(),
        cost_estimate=cost(3 * rows * feats * columns, 3 * rows * columns),
        name="residual",
    )(scalars, targets, mine[0], mine[1], other[0], other[1], weights, weights_oth, *before)


def ints(*values):
    return jnp.stack([jnp.asarray(v, jnp.int32) for v in values])


def per_device(count, frames, targets, projection, phases, block_order):
    n_bits = count.bit_length() - 1
    device = lax.axis_index(ALL)
    bit = [(device >> k) & 1 for k in range(n_bits)]
    core = bit[0]
    one = jnp.where(core == 0, bit[1], bit[2])
    two = jnp.where(core == 0, bit[2], bit[1])
    near, far = bit[3], bit[4]
    more = [1 << k for k in range(5, n_bits)]

    def exchange(value, even, odd=None):
        odd = even if odd is None else odd
        pairs = [(i, i ^ (odd if i & 1 else even)) for i in range(count)]
        return lax.ppermute(value, ALL, pairs)

    def flood(value, masks):
        for mask in masks:
            value = value + exchange(value, mask)
        return value

    scalars = ints(
        core * 4 + one * 2 + two,
        (1 - core) * 4 + two * 2 + one,
        core,
        near * 2 + far,
        one * 8 + two * 4 + near * 2 + far,
        two * 8 + one * 4 + near * 2 + far,
        one * 2 + two,
        two * 2 + one,
        device,
    )

    projection_oth, phases_oth = exchange(projection, 1), exchange(phases, 1)
    padded = (projection.shape[1] // 8 + 1) * 8
    blocks = pack(scalars, block_order, projection, projection_oth, phases, phases_oth, padded)
    part = blocks[:2] + exchange(blocks[2:], 2, 4)
    part = part[:1] + exchange(part[1:], 4, 2)
    part = flood(part, [8, 16] + more)
    part = jnp.concatenate([part, exchange(part, 4, 2)])
    blocks = jnp.concatenate([part, exchange(part, 2, 4)])
    blocks_oth = exchange(blocks, 1)
    *mine, high, low = features(QUARTER_OWN, 0, scalars, frames.T, blocks)
    *other, high, low = features(QUARTER_OTH, 1, scalars, frames.T, blocks_oth, (high, low))

    flat = mine + other

    def after(done, turned):
        return lax.optimization_barrier([done, *turned])[1:]

    sides = [high, low]
    gram_sent = gram(False, scalars, flat, sides)
    gram_came = exchange(gram_sent, 1)
    sides = after(gram_sent, sides)
    sent = cross(BASE_OTH, 0, scalars, targets, sides)
    came = exchange(sent, 1)
    sides = after(sent, sides)
    pieces = gram(True, scalars, flat, sides) + gram_came
    sides = after(pieces, sides)
    moved = exchange(pieces[8:], 2, 4)
    pieces = pieces[:8] + moved
    kept = [cross(BASE_OWN, 0, scalars, targets, sides, (came,))]
    sides = after(kept[0], sides)
    sent = cross(BASE_OTH, 1, scalars, targets, sides)
    came = exchange(sent, 1)
    sides = after(sent, sides)
    kept.append(cross(BASE_OWN, 1, scalars, targets, sides, (came,)))

    pieces = pieces[:4] + exchange(pieces[4:], 4, 2)
    pieces, kept[1] = lax.optimization_barrier([pieces, kept[1]])
    pieces = pieces[:2] + exchange(pieces[2:], 8)
    pieces = pieces[:1] + exchange(pieces[1:], 16)
    pieces = flood(pieces, more)
    for masks in ((16,), (8,), (4, 2), (2, 4)):
        pieces = jnp.concatenate([pieces, exchange(pieces, *masks)])

    crossed = []
    for value in kept:
        value = value[:2] + exchange(value[2:], 2, 4)
        value = value[:1] + exchange(value[1:], 4, 2)
        for mask in (8, 16):
            middle = value.shape[1] // 2
            value = value[:, :middle] + exchange(value[:, middle:], mask)
        value = flood(value, more)
        for mask in (16, 8):
            value = jnp.concatenate([value, exchange(value, mask)], axis=1)
        crossed.append(jnp.concatenate([value, exchange(value, 4, 2)]))

    matrix, side = assemble(scalars, pieces)
    side_oth = exchange(side, 1)
    for step in (1, 2, 3):
        matrix = factor(step, matrix)
    inverse = matrix
    inverse_oth = exchange(inverse, 1)
    coupling = couple(scalars, inverse, inverse_oth, side, side_oth)
    parts = []
    for value in crossed:
        near_part = solve(scalars, inverse, inverse_oth, coupling, value)
        parts.append((near_part, exchange(near_part, 2, 4)))
    outs = ()
    for pair in range(2):
        for group in range(2):
            value = parts[group][pair]
            value_oth = exchange(value, 1)
            outs = residual_part(group, pair, scalars, targets, mine, other, value, value_oth, tuple(outs))
    return tuple(outs)


def solution(mesh):
    count = math.prod(mesh.shape.values())

    def body(*arrays):
        return per_device(count, *arrays)

    return jax.shard_map(
        body,
        mesh=mesh,
        in_specs=(
            P(ALL, None),
            P(ALL, None),
            P(ALL, None, None),
            P(ALL, None),
            P(),
        ),
        out_specs=(P(ALL, None), P()),
        check_vma=False,
    )
```

```python
import functools
import math

import jax
import jax.numpy as jnp
from jax import lax
from jax.experimental import pallas as pl
from jax.experimental.pallas import tpu as pltpu
from jax.sharding import PartitionSpec as P

ALL = ("wide", "narrow")
F32 = jnp.float32
BF16 = jnp.bfloat16
HIGHEST = lax.Precision.HIGHEST


BASE_OWN, BASE_OTH, CORE, TURN, ORDER_OWN, ORDER_OTH, QUARTER_OWN, QUARTER_OTH, DEVICE = range(9)


def params(mib=24):
    return pltpu.CompilerParams(vmem_limit_bytes=mib * 1024 * 1024)


def cost(flops, nbytes):
    return pl.CostEstimate(flops=int(flops), bytes_accessed=int(nbytes), transcendentals=0)


def split(value):
    high = value.astype(BF16)
    return high, (value - high.astype(F32)).astype(BF16)


def dot_bf16(left, right):
    return jnp.dot(left, right, preferred_element_type=F32)


def dot3(left, right):
    (lh, ll), (rh, rl) = left, right
    return dot_bf16(lh, rh) + (dot_bf16(lh, rl) + dot_bf16(ll, rh))


def dot_full(left, right):
    return jnp.dot(left, right, precision=HIGHEST, preferred_element_type=F32)


TWO_PI = 2.0 * math.pi
PART_A = 6.28125
PART_B = 2.0 ** -24 * round((TWO_PI - PART_A) * 2.0 ** 24 / 2 ** 5) * 2 ** 5
PART_C = TWO_PI - PART_A - PART_B
SIN_POLY = [(-1.0) ** k / math.factorial(2 * k + 1) for k in range(7)]


def cosine(value):
    turns = jnp.floor(value * (1.0 / TWO_PI) + 0.5)
    rest = value - turns * PART_A
    rest = rest - turns * PART_B
    rest = rest - turns * PART_C
    half = rest * 0.5
    square = half * half
    poly = SIN_POLY[-1]
    for coefficient in SIN_POLY[-2::-1]:
        poly = poly * square + coefficient
    sine = half * poly
    return 1.0 - 2.0 * sine * sine


def pack_kernel(s_ref, order_ref, own_ref, oth_ref, pown_ref, poth_ref, out_ref):
    depth = own_ref.shape[1]
    wanted = order_ref[s_ref[CORE]]
    take_own = wanted == s_ref[DEVICE]
    take_oth = wanted == (s_ref[DEVICE] ^ 1)
    value = jnp.where(take_own, own_ref[0], jnp.where(take_oth, oth_ref[0], 0.0))
    phase = jnp.where(take_own, pown_ref[0], jnp.where(take_oth, poth_ref[0], 0.0))
    out_ref[0, :depth, :] = value
    tail = out_ref.shape[1] - depth
    rows = lax.broadcasted_iota(jnp.int32, (tail, out_ref.shape[2]), 0)
    out_ref[0, depth:, :] = jnp.where(rows == 0, jnp.broadcast_to(phase, rows.shape), 0.0)


def pack(scalars, block_order, own, oth, phase_own, phase_oth, padded):
    _, depth, feats = own.shape
    width = feats // 4
    block = pl.BlockSpec((1, depth, width), lambda q, s, o: (0, 0, q ^ s[QUARTER_OWN]))
    phase = pl.BlockSpec((1, 1, width), lambda q, s, o: (0, 0, q ^ s[QUARTER_OWN]))
    return pl.pallas_call(
        pack_kernel,
        out_shape=jax.ShapeDtypeStruct((4, padded, width), F32),
        grid_spec=pltpu.PrefetchScalarGridSpec(
            num_scalar_prefetch=2,
            grid=(4,),
            in_specs=[block, block, phase, phase],
            out_specs=pl.BlockSpec((1, padded, width), lambda q, s, o: (q, 0, 0)),
        ),
        compiler_params=params(),
        name="pack",
    )(scalars, block_order, own, oth, phase_own[:, None, :], phase_oth[:, None, :])


def features_kernel(quarter, s_ref, x_ref, p_ref, *rest):
    fh_ref, fl_ref, th_ref, tl_ref = rest[-4:]
    depth = x_ref.shape[0]
    swap = s_ref[quarter] & 1
    turned = jnp.concatenate([p_ref[i ^ swap] for i in range(2)], axis=1).T
    inner = dot_full(turned[:, :depth], x_ref[...]) + turned[:, depth : depth + 1]
    feats = math.sqrt(1.0 / turned.shape[0]) * cosine(inner)
    th_ref[...], tl_ref[...] = split(feats)
    fh_ref[...], fl_ref[...] = split(feats.T)


def features(quarter, slot, part, scalars, frames_turned, blocks, flat=(), stacked=()):
    depth, rows = frames_turned.shape
    half = blocks.shape[0] * blocks.shape[2]
    tile = 256
    before = tuple(flat) + tuple(stacked)
    n_flat = len(flat)
    aliases = {3 + k: k for k in range(n_flat)}
    aliases.update({3 + n_flat + k: 2 + k for k in range(len(stacked))})

    def pair(s):
        return part ^ (s[quarter] >> 1)

    return pl.pallas_call(
        functools.partial(features_kernel, quarter),
        out_shape=[jax.ShapeDtypeStruct((rows, 2 * half), BF16)] * 2
        + [jax.ShapeDtypeStruct((4 * half, rows), BF16)] * 2,
        grid_spec=pltpu.PrefetchScalarGridSpec(
            num_scalar_prefetch=1,
            grid=(rows // tile,),
            in_specs=[
                pl.BlockSpec((depth, tile), lambda i, s: (0, i)),
                pl.BlockSpec(blocks.shape, lambda i, s: (0, 0, 0)),
            ]
            + [pl.BlockSpec(memory_space=pl.ANY)] * len(before),
            out_specs=[pl.BlockSpec((tile, half), lambda i, s: (i, pair(s)))] * 2
            + [pl.BlockSpec((half, tile), lambda i, s: (2 * slot + pair(s), i))] * 2,
        ),
        input_output_aliases=aliases,
        compiler_params=params(),
        cost_estimate=cost(12 * rows * depth * half, 4 * rows * depth + 8 * rows * half),
        name="features",
    )(scalars, frames_turned, blocks, *before)


def gram_kernel(kept, s_ref, ah, al, bh, bl, th, tl, out_ref):
    order = s_ref[ORDER_OWN if kept else ORDER_OTH]
    half_row = s_ref[CORE] if kept else 1 - s_ref[CORE]
    m_is_second = half_row
    feats = th.shape[0] // 2
    mh, ml, oh, ol = (ah, al, bh, bl) if kept else (bh, bl, ah, al)
    m_at, o_at = (0, feats) if kept else (feats, 0)
    half = feats // 2
    pieces, _, height, _ = out_ref.shape

    def put(tile, value):
        for g in range(pieces):
            out_ref[g ^ order, tile] = value[g * height : (g + 1) * height]

    top = tuple(r[m_at : m_at + half] for r in (th, tl))
    low = tuple(r[m_at + half : m_at + feats] for r in (th, tl))
    left = (mh[:, :half], ml[:, :half])
    right = (mh[:, half:], ml[:, half:])
    put(0, dot3(top, left))
    put(1, dot3(low, left))
    put(2, dot3(low, right))

    def cross(at, h, l):
        start = pl.multiple_of(at + half_row * half, half)
        side = (th[pl.ds(start, half)], tl[pl.ds(start, half)])
        put(3, dot3(side, (h[:, :half], l[:, :half])))
        put(4, dot3(side, (h[:, half:], l[:, half:])))

    @pl.when(m_is_second == 1)
    def _():
        cross(m_at, oh, ol)

    @pl.when(m_is_second == 0)
    def _():
        cross(o_at, mh, ml)


def gram(kept, scalars, flat, turned):
    rows, feats = flat[0].shape
    return pl.pallas_call(
        functools.partial(gram_kernel, kept),
        out_shape=jax.ShapeDtypeStruct((16, 5, feats // 32, feats // 2), F32),
        in_specs=[pl.BlockSpec(memory_space=pltpu.SMEM)] + [pl.BlockSpec(memory_space=pltpu.VMEM)] * 6,
        out_specs=pl.BlockSpec(memory_space=pltpu.VMEM),
        compiler_params=params(),
        cost_estimate=cost(6 * rows * feats * feats * 1.25, 16 * rows * feats),
        name="gram",
    )(scalars, *flat, *turned)


def cross_kernel(base, s_ref, t_ref, th, tl, *rest):
    out_ref = rest[-1]
    core, turn, swap = s_ref[CORE], s_ref[TURN], s_ref[base] & 1
    feats = th.shape[0] // 2
    half = feats // 2
    width = out_ref.shape[2]
    first = 2 * pl.program_id(0)
    right = split(t_ref[...])

    def body(slot, carry):
        at = pl.ds(pl.multiple_of(slot * feats, feats), feats)
        value = dot3((th[at, :], tl[at, :]), right)
        for i in range(2):
            to = pl.ds(pl.multiple_of(((2 * (core ^ slot) + i) ^ turn) * half, half), half)
            for k in range(2):
                part = value[i * half : (i + 1) * half, k * width : (k + 1) * width]
                if len(rest) == 2:
                    part = part + rest[0][first + (k ^ swap), to, :]
                out_ref[first + (k ^ swap), to, :] = part
        return carry

    lax.fori_loop(0, 2, body, 0)


def cross(base, group, scalars, targets, turned, before=()):
    rows, columns = targets.shape
    feats = turned[0].shape[0] // 2
    width = columns // 16
    whole = pl.BlockSpec(memory_space=pltpu.VMEM)
    return pl.pallas_call(
        functools.partial(cross_kernel, base),
        out_shape=jax.ShapeDtypeStruct((4, 2 * feats, width), F32),
        grid_spec=pltpu.PrefetchScalarGridSpec(
            num_scalar_prefetch=1,
            grid=(2,),
            in_specs=[pl.BlockSpec((rows, 2 * width), lambda k, s: (0, 4 * group + ((s[base] >> 1) ^ k)))]
            + [whole] * (2 + len(before)),
            out_specs=whole,
        ),
        compiler_params=params(),
        cost_estimate=cost(3 * rows * feats * columns, 2 * rows * columns),
        name="cross",
    )(scalars, targets, *turned, *before)


def unit_inverse(block):
    size, lanes = block.shape
    groups = size // 8
    lane = lax.broadcasted_iota(jnp.int32, (8, lanes), 1)
    sub = lax.broadcasted_iota(jnp.int32, (8, lanes), 0)

    def wide(row):
        return jnp.broadcast_to(row, (8, lanes))

    def make(active):
        def turn(i, carry):
            rows, pivots = list(carry[0]), list(carry[1])
            spots = [jnp.full((8, lanes), 8 * i + k, jnp.int32) for k in range(8)]
            here = (lane >= 8 * i) & (lane < 8 * i + 8)
            top = rows[0]
            cols = [jnp.take_along_axis(top, spot, axis=1) for spot in spots]
            x = jnp.where(here, jnp.where(lane - 8 * i == sub, 1.0, 0.0), top)
            diagonal, inverse = top, []
            for j in range(0, 8, 2):
                a, b, c = wide(cols[j][j : j + 1]), wide(cols[j][j + 1 : j + 2]), wide(cols[j + 1][j + 1 : j + 2])
                inv_a = 1.0 / a
                inv_c = a * (1.0 / (a * c - b * b))
                link = b * inv_a
                inverse += [inv_a, inv_c]
                diagonal = jnp.where(sub == j, a, jnp.where(sub == j + 1, c - link * b, diagonal))
                m_a = jnp.where(sub > j, cols[j] * inv_a, 0.0)
                m_b = jnp.where(sub > j + 1, (cols[j + 1] - m_a * b) * inv_c, 0.0)

                def swept(value):
                    one = wide(value[j : j + 1])
                    two = wide(value[j + 1 : j + 2]) - link * one
                    return value - m_a * one - m_b * two

                for k in range(j + 1, 8):
                    cols[k] = swept(cols[k])
                x = swept(x)
            rest, z = x, [None] * 8
            for j in range(7, -1, -1):
                z[j] = wide(rest[j : j + 1]) * inverse[j]
                if j:
                    rest = rest - jnp.where(sub < j, cols[j], 0.0) * z[j]
            for g in range(1, active):
                parts = [jnp.take_along_axis(rows[g], spots[k], axis=1) * z[k] for k in range(8)]
                total = ((parts[0] + parts[1]) + (parts[2] + parts[3])) + ((parts[4] + parts[5]) + (parts[6] + parts[7]))
                rows[g] = jnp.where(g < groups - i, jnp.where(here, 0.0, rows[g]) - total, rows[g])
            return tuple(rows[1:] + [x]), tuple(pivots[1:] + [diagonal])

        return turn

    start = tuple(block[8 * g : 8 * g + 8] for g in range(groups))
    state = (start, start)
    state = lax.fori_loop(0, groups // 2, make(groups), state)
    rows, pivots = lax.fori_loop(groups // 2, groups, make(groups // 2), state)
    scaled = [
        jnp.where(lane <= sub + 8 * g, rows[g] * lax.rsqrt(pivots[g]), 0.0) for g in range(groups)
    ]
    return jnp.concatenate(scaled, axis=0)


def eliminate(m_ref, start, size):
    total = m_ref.shape[0]
    here = slice(start, start + size)
    inverse = unit_inverse(m_ref[here, here])
    if start:
        m_ref[here, :start] = dot_full(inverse, m_ref[here, :start])
    if start + size < total:
        below = slice(start + size, total)
        panel = lax.dot_general(
            m_ref[below, here], inverse, (((1,), (1,)), ((), ())), precision=HIGHEST, preferred_element_type=F32
        )
        m_ref[here, below] = dot_full(inverse, m_ref[here, below])
        m_ref[below, here] = jnp.zeros((total - start - size, size), F32)
        m_ref[here, here] = inverse
        m_ref[below, :] = m_ref[below, :] - dot_full(panel, m_ref[here, :])
    else:
        m_ref[here, here] = inverse


def assemble_kernel(s_ref, g_ref, a_ref, side_ref):
    order = s_ref[ORDER_OWN]
    pieces, _, height, half = g_ref.shape
    for g in range(pieces):
        piece = g_ref[g ^ order]
        here = slice(g * height, (g + 1) * height)
        there = slice(half + g * height, half + (g + 1) * height)
        a_ref[here, :half] = piece[0]
        a_ref[there, :half] = piece[1]
        a_ref[there, half:] = piece[2]
        side_ref[here, :half] = piece[3]
        side_ref[here, half:] = piece[4]
    a_ref[:half, half:] = a_ref[half:, :half].T
    whole = a_ref[...]
    eye = lax.broadcasted_iota(jnp.int32, whole.shape, 0) == lax.broadcasted_iota(jnp.int32, whole.shape, 1)
    diagonal = jnp.where(eye, whole, 0.0)
    damping = 0.1 * jnp.sum(diagonal) / whole.shape[0]
    a_ref[...] = whole + jnp.where(eye, damping, 0.0)
    eliminate(a_ref, 0, whole.shape[0] // 4)


def assemble(order, pieces):
    half = pieces.shape[3]
    return pl.pallas_call(
        assemble_kernel,
        out_shape=[jax.ShapeDtypeStruct((2 * half, 2 * half), F32), jax.ShapeDtypeStruct((half, 2 * half), F32)],
        in_specs=[pl.BlockSpec(memory_space=pltpu.SMEM), pl.BlockSpec(memory_space=pltpu.VMEM)],
        out_specs=[pl.BlockSpec(memory_space=pltpu.VMEM)] * 2,
        compiler_params=params(),
        cost_estimate=cost(1e10, 4e6),
        name="assemble",
    )(order, pieces)


def factor_kernel(step, m_ref, out_ref):
    out_ref[...] = m_ref[...]
    eliminate(out_ref, step * (m_ref.shape[0] // 4), m_ref.shape[0] // 4)
    if step == 3:
        whole = out_ref[...]
        low = lax.broadcasted_iota(jnp.int32, whole.shape, 0) >= lax.broadcasted_iota(jnp.int32, whole.shape, 1)
        whole = jnp.where(low, whole, 0.0)
        out_ref[...] = dot_full(whole.T, whole)


def factor(step, matrix):
    return pl.pallas_call(
        functools.partial(factor_kernel, step),
        out_shape=jax.ShapeDtypeStruct(matrix.shape, F32),
        in_specs=[pl.BlockSpec(memory_space=pltpu.VMEM)],
        out_specs=pl.BlockSpec(memory_space=pltpu.VMEM),
        compiler_params=params(),
        cost_estimate=cost(1e10, 4e6),
        name="factor",
    )(matrix)


def couple_kernel(s_ref, own_ref, oth_ref, gown_ref, goth_ref, out_ref):
    core = s_ref[CORE]
    half = gown_ref.shape[0]
    second = jnp.where(core == 1, own_ref[...], oth_ref[...])
    top = jnp.where(core == 0, gown_ref[...], goth_ref[...])
    low = jnp.where(core == 0, goth_ref[...], gown_ref[...])
    out_ref[...] = dot_full(second[:, :half], top) + dot_full(second[:, half:], low)


def couple(core, own, oth, side_own, side_oth):
    return pl.pallas_call(
        couple_kernel,
        out_shape=jax.ShapeDtypeStruct(own.shape, F32),
        in_specs=[pl.BlockSpec(memory_space=pltpu.SMEM)] + [pl.BlockSpec(memory_space=pltpu.VMEM)] * 4,
        compiler_params=params(),
        name="couple",
    )(core, own, oth, side_own, side_oth)


def solve_kernel(s_ref, own_ref, oth_ref, b_ref, c_ref, out_ref, one_ref):
    core, turn = s_ref[CORE], s_ref[TURN]
    feats = own_ref.shape[0]
    half = feats // 2
    width = c_ref.shape[2]

    def columns_of(step):
        starts = [pl.multiple_of(((2 * step + i) ^ turn) * half, half) for i in range(2)]
        return jnp.concatenate(
            [jnp.concatenate([c_ref[k, pl.ds(at, half), :] for k in range(2)], axis=1) for at in starts], axis=0
        )

    right = columns_of(0)

    def first(i, carry):
        here = pl.ds(pl.multiple_of(i * half, half), half)
        one = dot_full(jnp.where(core == 0, own_ref[here, :], oth_ref[here, :]), right)
        one_ref[here, :] = one
        for k in range(2):
            out_ref[k, here, :] = one[:, k * width : (k + 1) * width]
        return carry

    lax.fori_loop(0, 2, first, 0)
    right_two = jnp.concatenate([columns_of(1), one_ref[...]], axis=0)

    def second(i, carry):
        here = pl.ds(pl.multiple_of(i * half, half), half)
        there = pl.ds(pl.multiple_of(feats + i * half, half), half)
        left = jnp.where(core == 0, oth_ref[here, :], own_ref[here, :])
        two = dot_full(jnp.concatenate([left, -b_ref[here, :]], axis=1), right_two)
        for k in range(2):
            out_ref[k, there, :] = two[:, k * width : (k + 1) * width]
        return carry

    lax.fori_loop(0, 2, second, 0)


def solve(scalars, own, oth, coupling, crossed):
    count, height, width = crossed.shape
    feats = own.shape[0]
    whole = pl.BlockSpec((feats, feats), lambda k, s: (0, 0))
    pair = pl.BlockSpec((2, height, width), lambda k, s: (k, 0, 0))
    return pl.pallas_call(
        solve_kernel,
        out_shape=jax.ShapeDtypeStruct(crossed.shape, F32),
        grid_spec=pltpu.PrefetchScalarGridSpec(
            num_scalar_prefetch=1,
            grid=(count // 2,),
            in_specs=[whole] * 3 + [pair],
            out_specs=pair,
            scratch_shapes=[pltpu.VMEM((feats, 2 * width), F32)],
        ),
        compiler_params=params(),
        cost_estimate=cost(36 * feats * feats * count * width, 8 * count * height * width),
        name="solve",
    )(scalars, own, oth, coupling, crossed)


def residual_kernel(s_ref, t_ref, ah, al, bh, bl, wa_ref, wb_ref, *rest):
    r_ref, w_ref = rest[-2:]
    own = pl.program_id(0) == 0
    half = t_ref.shape[0]
    swap, core = jnp.where(own, s_ref[BASE_OWN], s_ref[BASE_OTH]) & 1, s_ref[CORE]
    feats = ah.shape[1]

    def take(step):
        here = pl.ds(pl.multiple_of(step * feats, feats), feats)
        return jnp.concatenate(
            [jnp.where(own, wa_ref[i ^ swap, here, :], wb_ref[i ^ swap, here, :]) for i in range(2)], axis=1
        )

    mine, other = take(core), take(1 - core)
    w_ref[core], w_ref[1 - core] = mine, other
    here = pl.ds(pl.multiple_of(pl.program_id(1) * half, half), half)
    fitted = dot3((ah[here, :], al[here, :]), split(mine)) + dot3((bh[here, :], bl[here, :]), split(other))
    r_ref[...] = t_ref[...] - fitted


def residual_part(group, pair, scalars, targets, mine, other, weights, weights_oth, before):
    rows, columns = targets.shape
    feats = mine[0].shape[1]
    _, _, width = weights.shape
    whole = pl.BlockSpec(memory_space=pltpu.VMEM)

    def place(k, s):
        return 4 * group + ((jnp.where(k == 0, s[BASE_OWN], s[BASE_OTH]) >> 1) ^ pair)

    block = pl.BlockSpec((rows // 2, 2 * width), lambda k, i, s: (i, place(k, s)))
    anywhere = pl.BlockSpec(memory_space=pl.ANY)
    return pl.pallas_call(
        residual_kernel,
        out_shape=[
            jax.ShapeDtypeStruct((rows, columns), F32),
            jax.ShapeDtypeStruct((2, feats, columns), F32),
        ],
        grid_spec=pltpu.PrefetchScalarGridSpec(
            num_scalar_prefetch=1,
            grid=(2, 2),
            in_specs=[block] + [whole] * 6 + [anywhere] * len(before),
            out_specs=[block, pl.BlockSpec((2, feats, 2 * width), lambda k, i, s: (0, 0, place(k, s)))],
        ),
        input_output_aliases={8: 0, 9: 1} if before else {},
        compiler_params=params(),
        cost_estimate=cost(3 * rows * feats * columns, 3 * rows * columns),
        name="residual",
    )(scalars, targets, mine[0], mine[1], other[0], other[1], weights, weights_oth, *before)


def ints(*values):
    return jnp.stack([jnp.asarray(v, jnp.int32) for v in values])


def per_device(count, frames, targets, projection, phases, block_order):
    n_bits = count.bit_length() - 1
    device = lax.axis_index(ALL)
    bit = [(device >> k) & 1 for k in range(n_bits)]
    core = bit[0]
    one = jnp.where(core == 0, bit[1], bit[2])
    two = jnp.where(core == 0, bit[2], bit[1])
    near, far = bit[3], bit[4]
    more = [1 << k for k in range(5, n_bits)]

    def exchange(value, even, odd=None):
        odd = even if odd is None else odd
        pairs = [(i, i ^ (odd if i & 1 else even)) for i in range(count)]
        return lax.ppermute(value, ALL, pairs)

    def flood(value, masks):
        for mask in masks:
            value = value + exchange(value, mask)
        return value

    scalars = ints(
        core * 4 + one * 2 + two,
        (1 - core) * 4 + two * 2 + one,
        core,
        near * 2 + far,
        one * 8 + two * 4 + near * 2 + far,
        two * 8 + one * 4 + near * 2 + far,
        one * 2 + two,
        two * 2 + one,
        device,
    )

    projection_oth, phases_oth = exchange(projection, 1), exchange(phases, 1)
    padded = (projection.shape[1] // 8 + 1) * 8
    blocks = pack(scalars, block_order, projection, projection_oth, phases, phases_oth, padded)
    part = blocks[:2] + exchange(blocks[2:], 2, 4)
    part = part[:1] + exchange(part[1:], 4, 2)
    part = flood(part, [8, 16] + more)
    part = jnp.concatenate([part, exchange(part, 4, 2)])
    part_b = exchange(part, 2, 4)
    mine, other, stacked = (), (), ()
    for half, value in enumerate((part, part_b)):
        value_oth = exchange(value, 1)
        *mine, high, low = features(QUARTER_OWN, 0, half, scalars, frames.T, value, mine, stacked)
        *other, high, low = features(QUARTER_OTH, 1, half, scalars, frames.T, value_oth, other, (high, low))
        stacked = (high, low)
    flat = mine + other

    def after(done, turned):
        return lax.optimization_barrier([done, *turned])[1:]

    sides = [high, low]
    gram_sent = gram(False, scalars, flat, sides)
    gram_came = exchange(gram_sent, 1)
    sides = after(gram_sent, sides)
    sent = cross(BASE_OTH, 0, scalars, targets, sides)
    came = exchange(sent, 1)
    sides = after(sent, sides)
    pieces = gram(True, scalars, flat, sides) + gram_came
    sides = after(pieces, sides)
    moved = exchange(pieces[8:], 2, 4)
    pieces = pieces[:8] + moved
    kept = [cross(BASE_OWN, 0, scalars, targets, sides, (came,))]
    sides = after(kept[0], sides)
    sent = cross(BASE_OTH, 1, scalars, targets, sides)
    came = exchange(sent, 1)
    sides = after(sent, sides)
    kept.append(cross(BASE_OWN, 1, scalars, targets, sides, (came,)))

    pieces = pieces[:4] + exchange(pieces[4:], 4, 2)
    pieces, kept[1] = lax.optimization_barrier([pieces, kept[1]])
    pieces = pieces[:2] + exchange(pieces[2:], 8)
    pieces = pieces[:1] + exchange(pieces[1:], 16)
    pieces = flood(pieces, more)
    for masks in ((16,), (8,), (4, 2), (2, 4)):
        pieces = jnp.concatenate([pieces, exchange(pieces, *masks)])

    crossed = []
    for value in kept:
        value = value[:2] + exchange(value[2:], 2, 4)
        value = value[:1] + exchange(value[1:], 4, 2)
        for mask in (8, 16):
            middle = value.shape[1] // 2
            value = value[:, :middle] + exchange(value[:, middle:], mask)
        value = flood(value, more)
        for mask in (16, 8):
            value = jnp.concatenate([value, exchange(value, mask)], axis=1)
        crossed.append(jnp.concatenate([value, exchange(value, 4, 2)]))

    matrix, side = assemble(scalars, pieces)
    side_oth = exchange(side, 1)
    for step in (1, 2, 3):
        matrix = factor(step, matrix)
    inverse = matrix
    inverse_oth = exchange(inverse, 1)
    coupling = couple(scalars, inverse, inverse_oth, side, side_oth)
    parts = []
    for value in crossed:
        near_part = solve(scalars, inverse, inverse_oth, coupling, value)
        parts.append((near_part, exchange(near_part, 2, 4)))
    outs = ()
    for pair in range(2):
        for group in range(2):
            value = parts[group][pair]
            value_oth = exchange(value, 1)
            outs = residual_part(group, pair, scalars, targets, mine, other, value, value_oth, tuple(outs))
    return tuple(outs)


def solution(mesh):
    count = math.prod(mesh.shape.values())

    def body(*arrays):
        return per_device(count, *arrays)

    return jax.shard_map(
        body,
        mesh=mesh,
        in_specs=(
            P(ALL, None),
            P(ALL, None),
            P(ALL, None, None),
            P(ALL, None),
            P(),
        ),
        out_specs=(P(ALL, None), P()),
        check_vma=False,
    )
```

```python
import functools
import math

import jax
import jax.numpy as jnp
from jax import lax
from jax.experimental import pallas as pl
from jax.experimental.pallas import tpu as pltpu
from jax.sharding import PartitionSpec as P

ALL = ("wide", "narrow")
F32 = jnp.float32
BF16 = jnp.bfloat16
HIGHEST = lax.Precision.HIGHEST


BASE_OWN, BASE_OTH, CORE, TURN, ORDER_OWN, ORDER_OTH, QUARTER_OWN, QUARTER_OTH, DEVICE = range(9)


def params(mib=24):
    return pltpu.CompilerParams(vmem_limit_bytes=mib * 1024 * 1024)


def cost(flops, nbytes):
    return pl.CostEstimate(flops=int(flops), bytes_accessed=int(nbytes), transcendentals=0)


def split(value):
    high = value.astype(BF16)
    return high, (value - high.astype(F32)).astype(BF16)


def dot_bf16(left, right):
    return jnp.dot(left, right, preferred_element_type=F32)


def dot3(left, right):
    (lh, ll), (rh, rl) = left, right
    return dot_bf16(lh, rh) + (dot_bf16(lh, rl) + dot_bf16(ll, rh))


def dot_full(left, right):
    return jnp.dot(left, right, precision=HIGHEST, preferred_element_type=F32)


TWO_PI = 2.0 * math.pi
PART_A = 6.28125
PART_B = 2.0 ** -24 * round((TWO_PI - PART_A) * 2.0 ** 24 / 2 ** 5) * 2 ** 5
PART_C = TWO_PI - PART_A - PART_B
SIN_POLY = [(-1.0) ** k / math.factorial(2 * k + 1) for k in range(7)]


def cosine(value):
    turns = jnp.floor(value * (1.0 / TWO_PI) + 0.5)
    rest = value - turns * PART_A
    rest = rest - turns * PART_B
    rest = rest - turns * PART_C
    half = rest * 0.5
    square = half * half
    poly = SIN_POLY[-1]
    for coefficient in SIN_POLY[-2::-1]:
        poly = poly * square + coefficient
    sine = half * poly
    return 1.0 - 2.0 * sine * sine


def pack_kernel(s_ref, order_ref, own_ref, oth_ref, pown_ref, poth_ref, out_ref):
    depth = own_ref.shape[1]
    wanted = order_ref[s_ref[CORE]]
    take_own = wanted == s_ref[DEVICE]
    take_oth = wanted == (s_ref[DEVICE] ^ 1)
    value = jnp.where(take_own, own_ref[0], jnp.where(take_oth, oth_ref[0], 0.0))
    phase = jnp.where(take_own, pown_ref[0], jnp.where(take_oth, poth_ref[0], 0.0))
    out_ref[0, :depth, :] = value
    tail = out_ref.shape[1] - depth
    rows = lax.broadcasted_iota(jnp.int32, (tail, out_ref.shape[2]), 0)
    out_ref[0, depth:, :] = jnp.where(rows == 0, jnp.broadcast_to(phase, rows.shape), 0.0)


def pack(scalars, block_order, own, oth, phase_own, phase_oth, padded):
    _, depth, feats = own.shape
    width = feats // 4
    block = pl.BlockSpec((1, depth, width), lambda q, s, o: (0, 0, q ^ s[QUARTER_OWN]))
    phase = pl.BlockSpec((1, 1, width), lambda q, s, o: (0, 0, q ^ s[QUARTER_OWN]))
    return pl.pallas_call(
        pack_kernel,
        out_shape=jax.ShapeDtypeStruct((4, padded, width), F32),
        grid_spec=pltpu.PrefetchScalarGridSpec(
            num_scalar_prefetch=2,
            grid=(4,),
            in_specs=[block, block, phase, phase],
            out_specs=pl.BlockSpec((1, padded, width), lambda q, s, o: (q, 0, 0)),
        ),
        compiler_params=params(),
        name="pack",
    )(scalars, block_order, own, oth, phase_own[:, None, :], phase_oth[:, None, :])


def features_kernel(quarter, slot, part, s_ref, x_ref, p_ref, *rest):
    fh_ref, fl_ref, th_ref, tl_ref = rest[-4:]
    depth, rows = x_ref.shape
    swap, pair = s_ref[quarter] & 1, part ^ (s_ref[quarter] >> 1)
    turned = jnp.concatenate([p_ref[i ^ swap] for i in range(2)], axis=1).T
    half = turned.shape[0]
    weights, phase = turned[:, :depth], turned[:, depth : depth + 1]
    across = pl.ds(pl.multiple_of(pair * half, half), half)
    down = pl.ds(pl.multiple_of((2 * slot + pair) * half, half), half)
    tile = 256

    def body(i, carry):
        at = pl.ds(pl.multiple_of(i * tile, tile), tile)
        feats = math.sqrt(1.0 / half) * cosine(dot_full(weights, x_ref[:, at]) + phase)
        th_ref[down, at], tl_ref[down, at] = split(feats)
        fh_ref[at, across], fl_ref[at, across] = split(feats.T)
        return carry

    lax.fori_loop(0, rows // tile, body, 0)


def features(quarter, slot, part, scalars, frames_turned, blocks, flat=(), stacked=()):
    depth, rows = frames_turned.shape
    half = blocks.shape[0] * blocks.shape[2]
    before = tuple(flat) + tuple(stacked)
    n_flat = len(flat)
    aliases = {3 + k: k for k in range(n_flat)}
    aliases.update({3 + n_flat + k: 2 + k for k in range(len(stacked))})
    whole = pl.BlockSpec(memory_space=pltpu.VMEM)
    return pl.pallas_call(
        functools.partial(features_kernel, quarter, slot, part),
        out_shape=[jax.ShapeDtypeStruct((rows, 2 * half), BF16)] * 2
        + [jax.ShapeDtypeStruct((4 * half, rows), BF16)] * 2,
        in_specs=[pl.BlockSpec(memory_space=pltpu.SMEM)] + [whole] * (2 + len(before)),
        out_specs=[whole] * 4,
        input_output_aliases=aliases,
        compiler_params=params(),
        cost_estimate=cost(12 * rows * depth * half, 4 * rows * depth + 8 * rows * half),
        name="features",
    )(scalars, frames_turned, blocks, *before)


def gram_kernel(kept, s_ref, ah, al, bh, bl, th, tl, out_ref):
    order = s_ref[ORDER_OWN if kept else ORDER_OTH]
    half_row = s_ref[CORE] if kept else 1 - s_ref[CORE]
    m_is_second = half_row
    feats = th.shape[0] // 2
    mh, ml, oh, ol = (ah, al, bh, bl) if kept else (bh, bl, ah, al)
    m_at, o_at = (0, feats) if kept else (feats, 0)
    half = feats // 2
    pieces, _, height, _ = out_ref.shape

    def put(tile, value):
        for g in range(pieces):
            out_ref[g ^ order, tile] = value[g * height : (g + 1) * height]

    top = tuple(r[m_at : m_at + half] for r in (th, tl))
    low = tuple(r[m_at + half : m_at + feats] for r in (th, tl))
    left = (mh[:, :half], ml[:, :half])
    right = (mh[:, half:], ml[:, half:])
    put(0, dot3(top, left))
    put(1, dot3(low, left))
    put(2, dot3(low, right))

    def cross(at, h, l):
        start = pl.multiple_of(at + half_row * half, half)
        side = (th[pl.ds(start, half)], tl[pl.ds(start, half)])
        put(3, dot3(side, (h[:, :half], l[:, :half])))
        put(4, dot3(side, (h[:, half:], l[:, half:])))

    @pl.when(m_is_second == 1)
    def _():
        cross(m_at, oh, ol)

    @pl.when(m_is_second == 0)
    def _():
        cross(o_at, mh, ml)


def gram(kept, scalars, flat, turned):
    rows, feats = flat[0].shape
    return pl.pallas_call(
        functools.partial(gram_kernel, kept),
        out_shape=jax.ShapeDtypeStruct((16, 5, feats // 32, feats // 2), F32),
        in_specs=[pl.BlockSpec(memory_space=pltpu.SMEM)] + [pl.BlockSpec(memory_space=pltpu.VMEM)] * 6,
        out_specs=pl.BlockSpec(memory_space=pltpu.VMEM),
        compiler_params=params(),
        cost_estimate=cost(6 * rows * feats * feats * 1.25, 16 * rows * feats),
        name="gram",
    )(scalars, *flat, *turned)


def cross_kernel(base, s_ref, t_ref, th, tl, *rest):
    out_ref = rest[-1]
    core, turn, swap = s_ref[CORE], s_ref[TURN], s_ref[base] & 1
    feats = th.shape[0] // 2
    half = feats // 2
    width = out_ref.shape[2]
    first = 2 * pl.program_id(0)
    right = split(t_ref[...])

    def body(slot, carry):
        at = pl.ds(pl.multiple_of(slot * feats, feats), feats)
        value = dot3((th[at, :], tl[at, :]), right)
        for i in range(2):
            to = pl.ds(pl.multiple_of(((2 * (core ^ slot) + i) ^ turn) * half, half), half)
            for k in range(2):
                part = value[i * half : (i + 1) * half, k * width : (k + 1) * width]
                if len(rest) == 2:
                    part = part + rest[0][first + (k ^ swap), to, :]
                out_ref[first + (k ^ swap), to, :] = part
        return carry

    lax.fori_loop(0, 2, body, 0)


def cross(base, group, scalars, targets, turned, before=()):
    rows, columns = targets.shape
    feats = turned[0].shape[0] // 2
    width = columns // 16
    whole = pl.BlockSpec(memory_space=pltpu.VMEM)
    return pl.pallas_call(
        functools.partial(cross_kernel, base),
        out_shape=jax.ShapeDtypeStruct((4, 2 * feats, width), F32),
        grid_spec=pltpu.PrefetchScalarGridSpec(
            num_scalar_prefetch=1,
            grid=(2,),
            in_specs=[pl.BlockSpec((rows, 2 * width), lambda k, s: (0, 4 * group + ((s[base] >> 1) ^ k)))]
            + [whole] * (2 + len(before)),
            out_specs=whole,
        ),
        compiler_params=params(),
        cost_estimate=cost(3 * rows * feats * columns, 2 * rows * columns),
        name="cross",
    )(scalars, targets, *turned, *before)


def unit_inverse(block):
    size, lanes = block.shape
    groups = size // 8
    lane = lax.broadcasted_iota(jnp.int32, (8, lanes), 1)
    sub = lax.broadcasted_iota(jnp.int32, (8, lanes), 0)

    def wide(row):
        return jnp.broadcast_to(row, (8, lanes))

    def make(active):
        def turn(i, carry):
            rows, pivots = list(carry[0]), list(carry[1])
            spots = [jnp.full((8, lanes), 8 * i + k, jnp.int32) for k in range(8)]
            here = (lane >= 8 * i) & (lane < 8 * i + 8)
            top = rows[0]
            cols = [jnp.take_along_axis(top, spot, axis=1) for spot in spots]
            x = jnp.where(here, jnp.where(lane - 8 * i == sub, 1.0, 0.0), top)
            diagonal, inverse = top, []
            for j in range(0, 8, 2):
                a, b, c = wide(cols[j][j : j + 1]), wide(cols[j][j + 1 : j + 2]), wide(cols[j + 1][j + 1 : j + 2])
                inv_a = 1.0 / a
                inv_c = a * (1.0 / (a * c - b * b))
                link = b * inv_a
                inverse += [inv_a, inv_c]
                diagonal = jnp.where(sub == j, a, jnp.where(sub == j + 1, c - link * b, diagonal))
                m_a = jnp.where(sub > j, cols[j] * inv_a, 0.0)
                m_b = jnp.where(sub > j + 1, (cols[j + 1] - m_a * b) * inv_c, 0.0)

                def swept(value):
                    one = wide(value[j : j + 1])
                    two = wide(value[j + 1 : j + 2]) - link * one
                    return value - m_a * one - m_b * two

                for k in range(j + 1, 8):
                    cols[k] = swept(cols[k])
                x = swept(x)
            rest, z = x, [None] * 8
            for j in range(7, -1, -1):
                z[j] = wide(rest[j : j + 1]) * inverse[j]
                if j:
                    rest = rest - jnp.where(sub < j, cols[j], 0.0) * z[j]
            for g in range(1, active):
                parts = [jnp.take_along_axis(rows[g], spots[k], axis=1) * z[k] for k in range(8)]
                total = ((parts[0] + parts[1]) + (parts[2] + parts[3])) + ((parts[4] + parts[5]) + (parts[6] + parts[7]))
                rows[g] = jnp.where(g < groups - i, jnp.where(here, 0.0, rows[g]) - total, rows[g])
            return tuple(rows[1:] + [x]), tuple(pivots[1:] + [diagonal])

        return turn

    start = tuple(block[8 * g : 8 * g + 8] for g in range(groups))
    state = (start, start)
    state = lax.fori_loop(0, groups // 2, make(groups), state)
    rows, pivots = lax.fori_loop(groups // 2, groups, make(groups // 2), state)
    scaled = [
        jnp.where(lane <= sub + 8 * g, rows[g] * lax.rsqrt(pivots[g]), 0.0) for g in range(groups)
    ]
    return jnp.concatenate(scaled, axis=0)


def eliminate(m_ref, start, size):
    total = m_ref.shape[0]
    here = slice(start, start + size)
    inverse = unit_inverse(m_ref[here, here])
    if start:
        m_ref[here, :start] = dot_full(inverse, m_ref[here, :start])
    if start + size < total:
        below = slice(start + size, total)
        panel = lax.dot_general(
            m_ref[below, here], inverse, (((1,), (1,)), ((), ())), precision=HIGHEST, preferred_element_type=F32
        )
        m_ref[here, below] = dot_full(inverse, m_ref[here, below])
        m_ref[below, here] = jnp.zeros((total - start - size, size), F32)
        m_ref[here, here] = inverse
        m_ref[below, :] = m_ref[below, :] - dot_full(panel, m_ref[here, :])
    else:
        m_ref[here, here] = inverse


def assemble_kernel(s_ref, g_ref, a_ref, side_ref):
    order = s_ref[ORDER_OWN]
    pieces, _, height, half = g_ref.shape
    for g in range(pieces):
        piece = g_ref[g ^ order]
        here = slice(g * height, (g + 1) * height)
        there = slice(half + g * height, half + (g + 1) * height)
        a_ref[here, :half] = piece[0]
        a_ref[there, :half] = piece[1]
        a_ref[there, half:] = piece[2]
        side_ref[here, :half] = piece[3]
        side_ref[here, half:] = piece[4]
    a_ref[:half, half:] = a_ref[half:, :half].T
    whole = a_ref[...]
    eye = lax.broadcasted_iota(jnp.int32, whole.shape, 0) == lax.broadcasted_iota(jnp.int32, whole.shape, 1)
    diagonal = jnp.where(eye, whole, 0.0)
    damping = 0.1 * jnp.sum(diagonal) / whole.shape[0]
    a_ref[...] = whole + jnp.where(eye, damping, 0.0)
    eliminate(a_ref, 0, whole.shape[0] // 4)


def assemble(order, pieces):
    half = pieces.shape[3]
    return pl.pallas_call(
        assemble_kernel,
        out_shape=[jax.ShapeDtypeStruct((2 * half, 2 * half), F32), jax.ShapeDtypeStruct((half, 2 * half), F32)],
        in_specs=[pl.BlockSpec(memory_space=pltpu.SMEM), pl.BlockSpec(memory_space=pltpu.VMEM)],
        out_specs=[pl.BlockSpec(memory_space=pltpu.VMEM)] * 2,
        compiler_params=params(),
        cost_estimate=cost(1e10, 4e6),
        name="assemble",
    )(order, pieces)


def factor_kernel(step, m_ref, out_ref):
    out_ref[...] = m_ref[...]
    eliminate(out_ref, step * (m_ref.shape[0] // 4), m_ref.shape[0] // 4)
    if step == 3:
        whole = out_ref[...]
        low = lax.broadcasted_iota(jnp.int32, whole.shape, 0) >= lax.broadcasted_iota(jnp.int32, whole.shape, 1)
        whole = jnp.where(low, whole, 0.0)
        out_ref[...] = dot_full(whole.T, whole)


def factor(step, matrix):
    return pl.pallas_call(
        functools.partial(factor_kernel, step),
        out_shape=jax.ShapeDtypeStruct(matrix.shape, F32),
        in_specs=[pl.BlockSpec(memory_space=pltpu.VMEM)],
        out_specs=pl.BlockSpec(memory_space=pltpu.VMEM),
        compiler_params=params(),
        cost_estimate=cost(1e10, 4e6),
        name="factor",
    )(matrix)


def couple_kernel(s_ref, own_ref, oth_ref, gown_ref, goth_ref, out_ref):
    core = s_ref[CORE]
    half = gown_ref.shape[0]
    second = jnp.where(core == 1, own_ref[...], oth_ref[...])
    top = jnp.where(core == 0, gown_ref[...], goth_ref[...])
    low = jnp.where(core == 0, goth_ref[...], gown_ref[...])
    out_ref[...] = dot_full(second[:, :half], top) + dot_full(second[:, half:], low)


def couple(core, own, oth, side_own, side_oth):
    return pl.pallas_call(
        couple_kernel,
        out_shape=jax.ShapeDtypeStruct(own.shape, F32),
        in_specs=[pl.BlockSpec(memory_space=pltpu.SMEM)] + [pl.BlockSpec(memory_space=pltpu.VMEM)] * 4,
        compiler_params=params(),
        name="couple",
    )(core, own, oth, side_own, side_oth)


def solve_kernel(s_ref, own_ref, oth_ref, b_ref, c_ref, out_ref, one_ref):
    core, turn = s_ref[CORE], s_ref[TURN]
    feats = own_ref.shape[0]
    half = feats // 2
    width = c_ref.shape[2]

    def columns_of(step):
        starts = [pl.multiple_of(((2 * step + i) ^ turn) * half, half) for i in range(2)]
        return jnp.concatenate(
            [jnp.concatenate([c_ref[k, pl.ds(at, half), :] for k in range(2)], axis=1) for at in starts], axis=0
        )

    right = columns_of(0)

    def first(i, carry):
        here = pl.ds(pl.multiple_of(i * half, half), half)
        one = dot_full(jnp.where(core == 0, own_ref[here, :], oth_ref[here, :]), right)
        one_ref[here, :] = one
        for k in range(2):
            out_ref[k, here, :] = one[:, k * width : (k + 1) * width]
        return carry

    lax.fori_loop(0, 2, first, 0)
    right_two = jnp.concatenate([columns_of(1), one_ref[...]], axis=0)

    def second(i, carry):
        here = pl.ds(pl.multiple_of(i * half, half), half)
        there = pl.ds(pl.multiple_of(feats + i * half, half), half)
        left = jnp.where(core == 0, oth_ref[here, :], own_ref[here, :])
        two = dot_full(jnp.concatenate([left, -b_ref[here, :]], axis=1), right_two)
        for k in range(2):
            out_ref[k, there, :] = two[:, k * width : (k + 1) * width]
        return carry

    lax.fori_loop(0, 2, second, 0)


def solve(scalars, own, oth, coupling, crossed):
    count, height, width = crossed.shape
    feats = own.shape[0]
    whole = pl.BlockSpec((feats, feats), lambda k, s: (0, 0))
    pair = pl.BlockSpec((2, height, width), lambda k, s: (k, 0, 0))
    return pl.pallas_call(
        solve_kernel,
        out_shape=jax.ShapeDtypeStruct(crossed.shape, F32),
        grid_spec=pltpu.PrefetchScalarGridSpec(
            num_scalar_prefetch=1,
            grid=(count // 2,),
            in_specs=[whole] * 3 + [pair],
            out_specs=pair,
            scratch_shapes=[pltpu.VMEM((feats, 2 * width), F32)],
        ),
        compiler_params=params(),
        cost_estimate=cost(36 * feats * feats * count * width, 8 * count * height * width),
        name="solve",
    )(scalars, own, oth, coupling, crossed)


def residual_kernel(s_ref, t_ref, ah, al, bh, bl, wa_ref, wb_ref, *rest):
    r_ref, w_ref = rest[-2:]
    own = pl.program_id(0) == 0
    half = t_ref.shape[0]
    swap, core = jnp.where(own, s_ref[BASE_OWN], s_ref[BASE_OTH]) & 1, s_ref[CORE]
    feats = ah.shape[1]

    def take(step):
        here = pl.ds(pl.multiple_of(step * feats, feats), feats)
        return jnp.concatenate(
            [jnp.where(own, wa_ref[i ^ swap, here, :], wb_ref[i ^ swap, here, :]) for i in range(2)], axis=1
        )

    mine, other = take(core), take(1 - core)
    w_ref[core], w_ref[1 - core] = mine, other
    here = pl.ds(pl.multiple_of(pl.program_id(1) * half, half), half)
    fitted = dot3((ah[here, :], al[here, :]), split(mine)) + dot3((bh[here, :], bl[here, :]), split(other))
    r_ref[...] = t_ref[...] - fitted


def residual_part(group, pair, scalars, targets, mine, other, weights, weights_oth, before):
    rows, columns = targets.shape
    feats = mine[0].shape[1]
    _, _, width = weights.shape
    whole = pl.BlockSpec(memory_space=pltpu.VMEM)

    def place(k, s):
        return 4 * group + ((jnp.where(k == 0, s[BASE_OWN], s[BASE_OTH]) >> 1) ^ pair)

    block = pl.BlockSpec((rows // 2, 2 * width), lambda k, i, s: (i, place(k, s)))
    anywhere = pl.BlockSpec(memory_space=pl.ANY)
    return pl.pallas_call(
        residual_kernel,
        out_shape=[
            jax.ShapeDtypeStruct((rows, columns), F32),
            jax.ShapeDtypeStruct((2, feats, columns), F32),
        ],
        grid_spec=pltpu.PrefetchScalarGridSpec(
            num_scalar_prefetch=1,
            grid=(2, 2),
            in_specs=[block] + [whole] * 6 + [anywhere] * len(before),
            out_specs=[block, pl.BlockSpec((2, feats, 2 * width), lambda k, i, s: (0, 0, place(k, s)))],
        ),
        input_output_aliases={8: 0, 9: 1} if before else {},
        compiler_params=params(),
        cost_estimate=cost(3 * rows * feats * columns, 3 * rows * columns),
        name="residual",
    )(scalars, targets, mine[0], mine[1], other[0], other[1], weights, weights_oth, *before)


def ints(*values):
    return jnp.stack([jnp.asarray(v, jnp.int32) for v in values])


def per_device(count, frames, targets, projection, phases, block_order):
    n_bits = count.bit_length() - 1
    device = lax.axis_index(ALL)
    bit = [(device >> k) & 1 for k in range(n_bits)]
    core = bit[0]
    one = jnp.where(core == 0, bit[1], bit[2])
    two = jnp.where(core == 0, bit[2], bit[1])
    near, far = bit[3], bit[4]
    more = [1 << k for k in range(5, n_bits)]

    def exchange(value, even, odd=None):
        odd = even if odd is None else odd
        pairs = [(i, i ^ (odd if i & 1 else even)) for i in range(count)]
        return lax.ppermute(value, ALL, pairs)

    def flood(value, masks):
        for mask in masks:
            value = value + exchange(value, mask)
        return value

    scalars = ints(
        core * 4 + one * 2 + two,
        (1 - core) * 4 + two * 2 + one,
        core,
        near * 2 + far,
        one * 8 + two * 4 + near * 2 + far,
        two * 8 + one * 4 + near * 2 + far,
        one * 2 + two,
        two * 2 + one,
        device,
    )

    projection_oth, phases_oth = exchange(projection, 1), exchange(phases, 1)
    padded = (projection.shape[1] // 8 + 1) * 8
    blocks = pack(scalars, block_order, projection, projection_oth, phases, phases_oth, padded)
    part = blocks[:2] + exchange(blocks[2:], 2, 4)
    part = part[:1] + exchange(part[1:], 4, 2)
    part = flood(part, [8, 16] + more)
    part = jnp.concatenate([part, exchange(part, 4, 2)])
    part_b = exchange(part, 2, 4)
    mine, other, stacked = (), (), ()
    for half, value in enumerate((part, part_b)):
        value_oth = exchange(value, 1)
        *mine, high, low = features(QUARTER_OWN, 0, half, scalars, frames.T, value, mine, stacked)
        *other, high, low = features(QUARTER_OTH, 1, half, scalars, frames.T, value_oth, other, (high, low))
        stacked = (high, low)
    flat = mine + other

    def after(done, turned):
        return lax.optimization_barrier([done, *turned])[1:]

    sides = [high, low]
    gram_sent = gram(False, scalars, flat, sides)
    gram_came = exchange(gram_sent, 1)
    sides = after(gram_sent, sides)
    sent = cross(BASE_OTH, 0, scalars, targets, sides)
    came = exchange(sent, 1)
    sides = after(sent, sides)
    pieces = gram(True, scalars, flat, sides) + gram_came
    sides = after(pieces, sides)
    moved = exchange(pieces[8:], 2, 4)
    pieces = pieces[:8] + moved
    kept = [cross(BASE_OWN, 0, scalars, targets, sides, (came,))]
    sides = after(kept[0], sides)
    sent = cross(BASE_OTH, 1, scalars, targets, sides)
    came = exchange(sent, 1)
    sides = after(sent, sides)
    kept.append(cross(BASE_OWN, 1, scalars, targets, sides, (came,)))

    pieces = pieces[:4] + exchange(pieces[4:], 4, 2)
    pieces, kept[1] = lax.optimization_barrier([pieces, kept[1]])
    pieces = pieces[:2] + exchange(pieces[2:], 8)
    pieces = pieces[:1] + exchange(pieces[1:], 16)
    pieces = flood(pieces, more)
    for masks in ((16,), (8,), (4, 2), (2, 4)):
        pieces = jnp.concatenate([pieces, exchange(pieces, *masks)])

    crossed = []
    for value in kept:
        value = value[:2] + exchange(value[2:], 2, 4)
        value = value[:1] + exchange(value[1:], 4, 2)
        for mask in (8, 16):
            middle = value.shape[1] // 2
            value = value[:, :middle] + exchange(value[:, middle:], mask)
        value = flood(value, more)
        for mask in (16, 8):
            value = jnp.concatenate([value, exchange(value, mask)], axis=1)
        crossed.append(jnp.concatenate([value, exchange(value, 4, 2)]))

    matrix, side = assemble(scalars, pieces)
    side_oth = exchange(side, 1)
    for step in (1, 2, 3):
        matrix = factor(step, matrix)
    inverse = matrix
    inverse_oth = exchange(inverse, 1)
    coupling = couple(scalars, inverse, inverse_oth, side, side_oth)
    parts = []
    for value in crossed:
        near_part = solve(scalars, inverse, inverse_oth, coupling, value)
        parts.append((near_part, exchange(near_part, 2, 4)))
    outs = ()
    for pair in range(2):
        for group in range(2):
            value = parts[group][pair]
            value_oth = exchange(value, 1)
            outs = residual_part(group, pair, scalars, targets, mine, other, value, value_oth, tuple(outs))
    return tuple(outs)


def solution(mesh):
    count = math.prod(mesh.shape.values())

    def body(*arrays):
        return per_device(count, *arrays)

    return jax.shard_map(
        body,
        mesh=mesh,
        in_specs=(
            P(ALL, None),
            P(ALL, None),
            P(ALL, None, None),
            P(ALL, None),
            P(),
        ),
        out_specs=(P(ALL, None), P()),
        check_vma=False,
    )
```

```python
import functools
import math

import jax
import jax.numpy as jnp
from jax import lax
from jax.experimental import pallas as pl
from jax.experimental.pallas import tpu as pltpu
from jax.sharding import PartitionSpec as P

ALL = ("wide", "narrow")
F32 = jnp.float32
BF16 = jnp.bfloat16
HIGHEST = lax.Precision.HIGHEST


BASE_OWN, BASE_OTH, CORE, TURN, ORDER_OWN, ORDER_OTH, QUARTER_OWN, QUARTER_OTH, DEVICE = range(9)


def params(mib=24):
    return pltpu.CompilerParams(vmem_limit_bytes=mib * 1024 * 1024)


def cost(flops, nbytes):
    return pl.CostEstimate(flops=int(flops), bytes_accessed=int(nbytes), transcendentals=0)


def split(value):
    high = value.astype(BF16)
    return high, (value - high.astype(F32)).astype(BF16)


def dot_bf16(left, right):
    return jnp.dot(left, right, preferred_element_type=F32)


def dot3(left, right):
    (lh, ll), (rh, rl) = left, right
    return dot_bf16(lh, rh) + (dot_bf16(lh, rl) + dot_bf16(ll, rh))


def dot_full(left, right):
    return jnp.dot(left, right, precision=HIGHEST, preferred_element_type=F32)


TWO_PI = 2.0 * math.pi
PART_A = 6.28125
PART_B = 2.0 ** -24 * round((TWO_PI - PART_A) * 2.0 ** 24 / 2 ** 5) * 2 ** 5
PART_C = TWO_PI - PART_A - PART_B
SIN_POLY = [(-1.0) ** k / math.factorial(2 * k + 1) for k in range(7)]


def cosine(value):
    turns = jnp.floor(value * (1.0 / TWO_PI) + 0.5)
    rest = value - turns * PART_A
    rest = rest - turns * PART_B
    rest = rest - turns * PART_C
    half = rest * 0.5
    square = half * half
    poly = SIN_POLY[-1]
    for coefficient in SIN_POLY[-2::-1]:
        poly = poly * square + coefficient
    sine = half * poly
    return 1.0 - 2.0 * sine * sine


def pack_kernel(s_ref, order_ref, own_ref, oth_ref, pown_ref, poth_ref, out_ref):
    depth = own_ref.shape[1]
    wanted = order_ref[s_ref[CORE]]
    take_own = wanted == s_ref[DEVICE]
    take_oth = wanted == (s_ref[DEVICE] ^ 1)
    value = jnp.where(take_own, own_ref[0], jnp.where(take_oth, oth_ref[0], 0.0))
    phase = jnp.where(take_own, pown_ref[0], jnp.where(take_oth, poth_ref[0], 0.0))
    out_ref[0, :depth, :] = value
    tail = out_ref.shape[1] - depth
    rows = lax.broadcasted_iota(jnp.int32, (tail, out_ref.shape[2]), 0)
    out_ref[0, depth:, :] = jnp.where(rows == 0, jnp.broadcast_to(phase, rows.shape), 0.0)


def pack(scalars, block_order, own, oth, phase_own, phase_oth, padded):
    _, depth, feats = own.shape
    width = feats // 4
    block = pl.BlockSpec((1, depth, width), lambda q, s, o: (0, 0, q ^ s[QUARTER_OWN]))
    phase = pl.BlockSpec((1, 1, width), lambda q, s, o: (0, 0, q ^ s[QUARTER_OWN]))
    return pl.pallas_call(
        pack_kernel,
        out_shape=jax.ShapeDtypeStruct((4, padded, width), F32),
        grid_spec=pltpu.PrefetchScalarGridSpec(
            num_scalar_prefetch=2,
            grid=(4,),
            in_specs=[block, block, phase, phase],
            out_specs=pl.BlockSpec((1, padded, width), lambda q, s, o: (q, 0, 0)),
        ),
        compiler_params=params(),
        name="pack",
    )(scalars, block_order, own, oth, phase_own[:, None, :], phase_oth[:, None, :])


def features_kernel(quarter, slot, part, s_ref, x_ref, p_ref, *rest):
    fh_ref, fl_ref, th_ref, tl_ref = rest[-4:]
    depth, rows = x_ref.shape
    swap, pair = s_ref[quarter] & 1, part ^ (s_ref[quarter] >> 1)
    turned = jnp.concatenate([p_ref[i ^ swap] for i in range(2)], axis=1).T
    half = turned.shape[0]
    weights, phase = turned[:, :depth], turned[:, depth : depth + 1]
    across = pl.ds(pl.multiple_of(pair * half, half), half)
    down = pl.ds(pl.multiple_of((2 * slot + pair) * half, half), half)
    tile = 256

    def body(i, carry):
        at = pl.ds(pl.multiple_of(i * tile, tile), tile)
        feats = math.sqrt(1.0 / half) * cosine(dot_full(weights, x_ref[:, at]) + phase)
        th_ref[down, at], tl_ref[down, at] = split(feats)
        fh_ref[at, across], fl_ref[at, across] = split(feats.T)
        return carry

    lax.fori_loop(0, rows // tile, body, 0)


def features(quarter, slot, part, scalars, frames_turned, blocks, flat=(), stacked=()):
    depth, rows = frames_turned.shape
    half = blocks.shape[0] * blocks.shape[2]
    before = tuple(flat) + tuple(stacked)
    n_flat = len(flat)
    aliases = {3 + k: k for k in range(n_flat)}
    aliases.update({3 + n_flat + k: 2 + k for k in range(len(stacked))})
    whole = pl.BlockSpec(memory_space=pltpu.VMEM)
    return pl.pallas_call(
        functools.partial(features_kernel, quarter, slot, part),
        out_shape=[jax.ShapeDtypeStruct((rows, 2 * half), BF16)] * 2
        + [jax.ShapeDtypeStruct((4 * half, rows), BF16)] * 2,
        in_specs=[pl.BlockSpec(memory_space=pltpu.SMEM)] + [whole] * (2 + len(before)),
        out_specs=[whole] * 4,
        input_output_aliases=aliases,
        compiler_params=params(),
        cost_estimate=cost(12 * rows * depth * half, 4 * rows * depth + 8 * rows * half),
        name="features",
    )(scalars, frames_turned, blocks, *before)


def gram_kernel(kept, s_ref, ah, al, bh, bl, th, tl, out_ref):
    order = s_ref[ORDER_OWN if kept else ORDER_OTH]
    half_row = s_ref[CORE] if kept else 1 - s_ref[CORE]
    m_is_second = half_row
    feats = th.shape[0] // 2
    mh, ml, oh, ol = (ah, al, bh, bl) if kept else (bh, bl, ah, al)
    m_at, o_at = (0, feats) if kept else (feats, 0)
    half = feats // 2
    pieces, _, height, _ = out_ref.shape

    def put(tile, value):
        for g in range(pieces):
            out_ref[g ^ order, tile] = value[g * height : (g + 1) * height]

    top = tuple(r[m_at : m_at + half] for r in (th, tl))
    low = tuple(r[m_at + half : m_at + feats] for r in (th, tl))
    left = (mh[:, :half], ml[:, :half])
    right = (mh[:, half:], ml[:, half:])
    put(0, dot3(top, left))
    put(1, dot3(low, left))
    put(2, dot3(low, right))

    def cross(at, h, l):
        start = pl.multiple_of(at + half_row * half, half)
        side = (th[pl.ds(start, half)], tl[pl.ds(start, half)])
        put(3, dot3(side, (h[:, :half], l[:, :half])))
        put(4, dot3(side, (h[:, half:], l[:, half:])))

    @pl.when(m_is_second == 1)
    def _():
        cross(m_at, oh, ol)

    @pl.when(m_is_second == 0)
    def _():
        cross(o_at, mh, ml)


def gram(kept, scalars, flat, turned):
    rows, feats = flat[0].shape
    return pl.pallas_call(
        functools.partial(gram_kernel, kept),
        out_shape=jax.ShapeDtypeStruct((16, 5, feats // 32, feats // 2), F32),
        in_specs=[pl.BlockSpec(memory_space=pltpu.SMEM)] + [pl.BlockSpec(memory_space=pltpu.VMEM)] * 6,
        out_specs=pl.BlockSpec(memory_space=pltpu.VMEM),
        compiler_params=params(),
        cost_estimate=cost(6 * rows * feats * feats * 1.25, 16 * rows * feats),
        name="gram",
    )(scalars, *flat, *turned)


def cross_kernel(base, s_ref, t_ref, th, tl, *rest):
    out_ref = rest[-1]
    core, turn, swap = s_ref[CORE], s_ref[TURN], s_ref[base] & 1
    feats = th.shape[0] // 2
    half = feats // 2
    width = out_ref.shape[2]
    first = 2 * pl.program_id(0)
    right = split(t_ref[...])

    def body(slot, carry):
        at = pl.ds(pl.multiple_of(slot * feats, feats), feats)
        value = dot3((th[at, :], tl[at, :]), right)
        for i in range(2):
            to = pl.ds(pl.multiple_of(((2 * (core ^ slot) + i) ^ turn) * half, half), half)
            for k in range(2):
                part = value[i * half : (i + 1) * half, k * width : (k + 1) * width]
                if len(rest) == 2:
                    part = part + rest[0][first + (k ^ swap), to, :]
                out_ref[first + (k ^ swap), to, :] = part
        return carry

    lax.fori_loop(0, 2, body, 0)


def cross(base, group, scalars, targets, turned, before=()):
    rows, columns = targets.shape
    feats = turned[0].shape[0] // 2
    width = columns // 16
    whole = pl.BlockSpec(memory_space=pltpu.VMEM)
    return pl.pallas_call(
        functools.partial(cross_kernel, base),
        out_shape=jax.ShapeDtypeStruct((4, 2 * feats, width), F32),
        grid_spec=pltpu.PrefetchScalarGridSpec(
            num_scalar_prefetch=1,
            grid=(2,),
            in_specs=[pl.BlockSpec((rows, 2 * width), lambda k, s: (0, 4 * group + ((s[base] >> 1) ^ k)))]
            + [whole] * (2 + len(before)),
            out_specs=whole,
        ),
        compiler_params=params(),
        cost_estimate=cost(3 * rows * feats * columns, 2 * rows * columns),
        name="cross",
    )(scalars, targets, *turned, *before)


def unit_inverse(block):
    size, lanes = block.shape
    groups = size // 8
    lane = lax.broadcasted_iota(jnp.int32, (8, lanes), 1)
    sub = lax.broadcasted_iota(jnp.int32, (8, lanes), 0)

    def wide(row):
        return jnp.broadcast_to(row, (8, lanes))

    def make(active):
        def turn(i, carry):
            rows, pivots = list(carry[0]), list(carry[1])
            spots = [jnp.full((8, lanes), 8 * i + k, jnp.int32) for k in range(8)]
            here = (lane >= 8 * i) & (lane < 8 * i + 8)
            top = rows[0]
            cols = [jnp.take_along_axis(top, spot, axis=1) for spot in spots]
            x = jnp.where(here, jnp.where(lane - 8 * i == sub, 1.0, 0.0), top)
            diagonal, inverse = top, []
            for j in range(0, 8, 2):
                a, b, c = wide(cols[j][j : j + 1]), wide(cols[j][j + 1 : j + 2]), wide(cols[j + 1][j + 1 : j + 2])
                inv_a = 1.0 / a
                inv_c = a * (1.0 / (a * c - b * b))
                link = b * inv_a
                inverse += [inv_a, inv_c]
                diagonal = jnp.where(sub == j, a, jnp.where(sub == j + 1, c - link * b, diagonal))
                m_a = jnp.where(sub > j, cols[j] * inv_a, 0.0)
                m_b = jnp.where(sub > j + 1, (cols[j + 1] - m_a * b) * inv_c, 0.0)

                def swept(value):
                    one = wide(value[j : j + 1])
                    two = wide(value[j + 1 : j + 2]) - link * one
                    return value - m_a * one - m_b * two

                for k in range(j + 1, 8):
                    cols[k] = swept(cols[k])
                x = swept(x)
            rest, z = x, [None] * 8
            for j in range(7, -1, -1):
                z[j] = wide(rest[j : j + 1]) * inverse[j]
                if j:
                    rest = rest - jnp.where(sub < j, cols[j], 0.0) * z[j]
            for g in range(1, active):
                parts = [jnp.take_along_axis(rows[g], spots[k], axis=1) * z[k] for k in range(8)]
                total = ((parts[0] + parts[1]) + (parts[2] + parts[3])) + ((parts[4] + parts[5]) + (parts[6] + parts[7]))
                rows[g] = jnp.where(g < groups - i, jnp.where(here, 0.0, rows[g]) - total, rows[g])
            return tuple(rows[1:] + [x]), tuple(pivots[1:] + [diagonal])

        return turn

    start = tuple(block[8 * g : 8 * g + 8] for g in range(groups))
    state = (start, start)
    state = lax.fori_loop(0, groups // 2, make(groups), state)
    rows, pivots = lax.fori_loop(groups // 2, groups, make(groups // 2), state)
    scaled = [
        jnp.where(lane <= sub + 8 * g, rows[g] * lax.rsqrt(pivots[g]), 0.0) for g in range(groups)
    ]
    return jnp.concatenate(scaled, axis=0)


def eliminate(m_ref, start, size):
    total = m_ref.shape[0]
    here = slice(start, start + size)
    inverse = unit_inverse(m_ref[here, here])
    if start:
        m_ref[here, :start] = dot_full(inverse, m_ref[here, :start])
    if start + size < total:
        below = slice(start + size, total)
        panel = lax.dot_general(
            m_ref[below, here], inverse, (((1,), (1,)), ((), ())), precision=HIGHEST, preferred_element_type=F32
        )
        m_ref[here, below] = dot_full(inverse, m_ref[here, below])
        m_ref[below, here] = jnp.zeros((total - start - size, size), F32)
        m_ref[here, here] = inverse
        m_ref[below, :] = m_ref[below, :] - dot_full(panel, m_ref[here, :])
    else:
        m_ref[here, here] = inverse


def assemble_kernel(s_ref, g_ref, a_ref, side_ref):
    order = s_ref[ORDER_OWN]
    pieces, _, height, half = g_ref.shape
    for g in range(pieces):
        piece = g_ref[g ^ order]
        here = slice(g * height, (g + 1) * height)
        there = slice(half + g * height, half + (g + 1) * height)
        a_ref[here, :half] = piece[0]
        a_ref[there, :half] = piece[1]
        a_ref[there, half:] = piece[2]
        side_ref[here, :half] = piece[3]
        side_ref[here, half:] = piece[4]
    a_ref[:half, half:] = a_ref[half:, :half].T
    whole = a_ref[...]
    eye = lax.broadcasted_iota(jnp.int32, whole.shape, 0) == lax.broadcasted_iota(jnp.int32, whole.shape, 1)
    diagonal = jnp.where(eye, whole, 0.0)
    damping = 0.1 * jnp.sum(diagonal) / whole.shape[0]
    a_ref[...] = whole + jnp.where(eye, damping, 0.0)
    eliminate(a_ref, 0, whole.shape[0] // 4)


def assemble(order, pieces):
    half = pieces.shape[3]
    return pl.pallas_call(
        assemble_kernel,
        out_shape=[jax.ShapeDtypeStruct((2 * half, 2 * half), F32), jax.ShapeDtypeStruct((half, 2 * half), F32)],
        in_specs=[pl.BlockSpec(memory_space=pltpu.SMEM), pl.BlockSpec(memory_space=pltpu.VMEM)],
        out_specs=[pl.BlockSpec(memory_space=pltpu.VMEM)] * 2,
        compiler_params=params(),
        cost_estimate=cost(1e10, 4e6),
        name="assemble",
    )(order, pieces)


def factor_kernel(step, m_ref, out_ref):
    out_ref[...] = m_ref[...]
    eliminate(out_ref, step * (m_ref.shape[0] // 4), m_ref.shape[0] // 4)
    if step == 3:
        whole = out_ref[...]
        low = lax.broadcasted_iota(jnp.int32, whole.shape, 0) >= lax.broadcasted_iota(jnp.int32, whole.shape, 1)
        whole = jnp.where(low, whole, 0.0)
        out_ref[...] = dot_full(whole.T, whole)


def factor(step, matrix):
    return pl.pallas_call(
        functools.partial(factor_kernel, step),
        out_shape=jax.ShapeDtypeStruct(matrix.shape, F32),
        in_specs=[pl.BlockSpec(memory_space=pltpu.VMEM)],
        out_specs=pl.BlockSpec(memory_space=pltpu.VMEM),
        compiler_params=params(),
        cost_estimate=cost(1e10, 4e6),
        name="factor",
    )(matrix)


def solve_kernel(s_ref, own_ref, oth_ref, gown_ref, goth_ref, c_ref, out_ref, one_ref, two_ref):
    core, turn = s_ref[CORE], s_ref[TURN]
    feats = own_ref.shape[0]
    half = feats // 2
    width = c_ref.shape[2]

    def columns_of(step):
        starts = [pl.multiple_of(((2 * step + i) ^ turn) * half, half) for i in range(2)]
        return jnp.concatenate(
            [jnp.concatenate([c_ref[k, pl.ds(at, half), :] for k in range(2)], axis=1) for at in starts], axis=0
        )

    right = columns_of(0)

    def first(i, carry):
        here = pl.ds(pl.multiple_of(i * half, half), half)
        one = dot_full(jnp.where(core == 0, own_ref[here, :], oth_ref[here, :]), right)
        one_ref[here, :] = one
        for k in range(2):
            out_ref[k, here, :] = one[:, k * width : (k + 1) * width]
        return carry

    lax.fori_loop(0, 2, first, 0)
    two_ref[...] = columns_of(1)

    def couple(i, carry):
        here = pl.ds(pl.multiple_of(i * half, half), half)
        side = jnp.where((core ^ i) == 0, gown_ref[...], goth_ref[...])
        two_ref[here, :] = two_ref[here, :] - dot_full(side, one_ref[...])
        return carry

    lax.fori_loop(0, 2, couple, 0)

    def second(i, carry):
        here = pl.ds(pl.multiple_of(i * half, half), half)
        there = pl.ds(pl.multiple_of(feats + i * half, half), half)
        two = dot_full(jnp.where(core == 0, oth_ref[here, :], own_ref[here, :]), two_ref[...])
        for k in range(2):
            out_ref[k, there, :] = two[:, k * width : (k + 1) * width]
        return carry

    lax.fori_loop(0, 2, second, 0)


def solve(scalars, own, oth, side, side_oth, crossed):
    count, height, width = crossed.shape
    feats = own.shape[0]
    whole = pl.BlockSpec(memory_space=pltpu.VMEM)
    pair = pl.BlockSpec((2, height, width), lambda k, s: (k, 0, 0))
    return pl.pallas_call(
        solve_kernel,
        out_shape=jax.ShapeDtypeStruct(crossed.shape, F32),
        grid_spec=pltpu.PrefetchScalarGridSpec(
            num_scalar_prefetch=1,
            grid=(count // 2,),
            in_specs=[whole] * 4 + [pair],
            out_specs=pair,
            scratch_shapes=[pltpu.VMEM((feats, 2 * width), F32)] * 2,
        ),
        compiler_params=params(),
        cost_estimate=cost(36 * feats * feats * count * width, 8 * count * height * width),
        name="solve",
    )(scalars, own, oth, side, side_oth, crossed)


def residual_kernel(only, s_ref, t_ref, ah, al, bh, bl, wa_ref, wb_ref, *rest):
    r_ref, w_ref = rest[-2:]
    own = pl.program_id(0) + only == 0
    half = t_ref.shape[0]
    swap, core = jnp.where(own, s_ref[BASE_OWN], s_ref[BASE_OTH]) & 1, s_ref[CORE]
    feats = ah.shape[1]

    def take(step):
        here = pl.ds(pl.multiple_of(step * feats, feats), feats)
        return jnp.concatenate(
            [jnp.where(own, wa_ref[i ^ swap, here, :], wb_ref[i ^ swap, here, :]) for i in range(2)], axis=1
        )

    mine, other = take(core), take(1 - core)
    w_ref[core], w_ref[1 - core] = mine, other
    here = pl.ds(pl.multiple_of(pl.program_id(1) * half, half), half)
    fitted = dot3((ah[here, :], al[here, :]), split(mine)) + dot3((bh[here, :], bl[here, :]), split(other))
    r_ref[...] = t_ref[...] - fitted


def residual_part(group, pair, sides, scalars, targets, mine, other, weights, weights_oth, before):
    rows, columns = targets.shape
    feats = mine[0].shape[1]
    _, _, width = weights.shape
    whole = pl.BlockSpec(memory_space=pltpu.VMEM)

    def place(k, s):
        return 4 * group + ((jnp.where(k + sides[0] == 0, s[BASE_OWN], s[BASE_OTH]) >> 1) ^ pair)

    block = pl.BlockSpec((rows // 2, 2 * width), lambda k, i, s: (i, place(k, s)))
    anywhere = pl.BlockSpec(memory_space=pl.ANY)
    return pl.pallas_call(
        functools.partial(residual_kernel, sides[0]),
        out_shape=[
            jax.ShapeDtypeStruct((rows, columns), F32),
            jax.ShapeDtypeStruct((2, feats, columns), F32),
        ],
        grid_spec=pltpu.PrefetchScalarGridSpec(
            num_scalar_prefetch=1,
            grid=(len(sides), 2),
            in_specs=[block] + [whole] * 6 + [anywhere] * len(before),
            out_specs=[block, pl.BlockSpec((2, feats, 2 * width), lambda k, i, s: (0, 0, place(k, s)))],
        ),
        input_output_aliases={8: 0, 9: 1} if before else {},
        compiler_params=params(),
        cost_estimate=cost(3 * rows * feats * columns, 3 * rows * columns),
        name="residual",
    )(scalars, targets, mine[0], mine[1], other[0], other[1], weights, weights_oth, *before)


def ints(*values):
    return jnp.stack([jnp.asarray(v, jnp.int32) for v in values])


def per_device(count, frames, targets, projection, phases, block_order):
    n_bits = count.bit_length() - 1
    device = lax.axis_index(ALL)
    bit = [(device >> k) & 1 for k in range(n_bits)]
    core = bit[0]
    one = jnp.where(core == 0, bit[1], bit[2])
    two = jnp.where(core == 0, bit[2], bit[1])
    near, far = bit[3], bit[4]
    more = [1 << k for k in range(5, n_bits)]

    def exchange(value, even, odd=None):
        odd = even if odd is None else odd
        pairs = [(i, i ^ (odd if i & 1 else even)) for i in range(count)]
        return lax.ppermute(value, ALL, pairs)

    def flood(value, masks):
        for mask in masks:
            value = value + exchange(value, mask)
        return value

    scalars = ints(
        core * 4 + one * 2 + two,
        (1 - core) * 4 + two * 2 + one,
        core,
        near * 2 + far,
        one * 8 + two * 4 + near * 2 + far,
        two * 8 + one * 4 + near * 2 + far,
        one * 2 + two,
        two * 2 + one,
        device,
    )

    projection_oth, phases_oth = exchange(projection, 1), exchange(phases, 1)
    padded = (projection.shape[1] // 8 + 1) * 8
    blocks = pack(scalars, block_order, projection, projection_oth, phases, phases_oth, padded)
    part = blocks[:2] + exchange(blocks[2:], 2, 4)
    part = part[:1] + exchange(part[1:], 4, 2)
    part = flood(part, [8, 16] + more)
    part = jnp.concatenate([part, exchange(part, 4, 2)])
    part_b = exchange(part, 2, 4)
    mine, other, stacked = (), (), ()
    for half, value in enumerate((part, part_b)):
        value_oth = exchange(value, 1)
        *mine, high, low = features(QUARTER_OWN, 0, half, scalars, frames.T, value, mine, stacked)
        *other, high, low = features(QUARTER_OTH, 1, half, scalars, frames.T, value_oth, other, (high, low))
        stacked = (high, low)
    flat = mine + other

    def after(done, turned):
        return lax.optimization_barrier([done, *turned])[1:]

    sides = [high, low]
    gram_sent = gram(False, scalars, flat, sides)
    gram_came = exchange(gram_sent, 1)
    sides = after(gram_sent, sides)
    sent = cross(BASE_OTH, 0, scalars, targets, sides)
    came = exchange(sent, 1)
    sides = after(sent, sides)
    pieces = gram(True, scalars, flat, sides) + gram_came
    sides = after(pieces, sides)
    moved = exchange(pieces[8:], 2, 4)
    pieces = pieces[:8] + moved
    kept = [cross(BASE_OWN, 0, scalars, targets, sides, (came,))]
    sides = after(kept[0], sides)
    sent = cross(BASE_OTH, 1, scalars, targets, sides)
    came = exchange(sent, 1)
    sides = after(sent, sides)
    kept.append(cross(BASE_OWN, 1, scalars, targets, sides, (came,)))

    pieces = pieces[:4] + exchange(pieces[4:], 4, 2)
    pieces, kept[1] = lax.optimization_barrier([pieces, kept[1]])
    pieces = pieces[:2] + exchange(pieces[2:], 8)
    pieces = pieces[:1] + exchange(pieces[1:], 16)
    pieces = flood(pieces, more)
    for masks in ((16,), (8,), (4, 2), (2, 4)):
        pieces = jnp.concatenate([pieces, exchange(pieces, *masks)])

    crossed = []
    for value in kept:
        value = value[:2] + exchange(value[2:], 2, 4)
        value = value[:1] + exchange(value[1:], 4, 2)
        for mask in (8, 16):
            middle = value.shape[1] // 2
            value = value[:, :middle] + exchange(value[:, middle:], mask)
        value = flood(value, more)
        for mask in (16, 8):
            value = jnp.concatenate([value, exchange(value, mask)], axis=1)
        crossed.append(jnp.concatenate([value, exchange(value, 4, 2)]))

    matrix, side = assemble(scalars, pieces)
    side_oth = exchange(side, 1)
    for step in (1, 2, 3):
        matrix = factor(step, matrix)
    inverse = matrix
    inverse_oth = exchange(inverse, 1)
    parts = []
    for value in crossed:
        near_part = solve(scalars, inverse, inverse_oth, side, side_oth, value)
        parts.append((near_part, exchange(near_part, 2, 4)))
    outs = ()
    for pair in range(2):
        for group in range(2):
            value = parts[group][pair]
            value_oth = exchange(value, 1)
            last = group + pair == 2
            for sides in ((0,), (1,)) if last else ((0, 1),):
                held = value if sides == (0,) else value_oth
                outs = residual_part(group, pair, sides, scalars, targets, mine, other, value, held, tuple(outs))
    return tuple(outs)


def solution(mesh):
    count = math.prod(mesh.shape.values())

    def body(*arrays):
        return per_device(count, *arrays)

    return jax.shard_map(
        body,
        mesh=mesh,
        in_specs=(
            P(ALL, None),
            P(ALL, None),
            P(ALL, None, None),
            P(ALL, None),
            P(),
        ),
        out_specs=(P(ALL, None), P()),
        check_vma=False,
    )
```
